32 devices in a mesh: group: 2 (over x), tok: 16 (over z, y, core).
Axes of the slice: x: 2, y: 2, z: 4, core: 2. Of those that a mesh axis runs over, the one named last changes fastest.
Arguments:
- initial_guess: float32 [512, 16, 128], P(('group', 'tok')), parts along dimension 0, may hold values from -6 to 6
- noise_draws: float32 [512, 16, 128], P(('group', 'tok')), parts along dimension 0, may hold values from -6 to 6
- drift_state: float32 [16], replicated, may hold values from 0 to 0.15
- drift_denoise: float32 [16], replicated, may hold values from -0.4 to -0.15
- noise_scale: float32 [16], replicated, may hold values from 0.05 to 0.3
- modulation: float32 [16, 8, 1152], replicated, may hold values from -3 to 3
- embed_weight: bfloat16 [16, 1152], replicated, may hold values from -1.5 to 1.5
- space_input: bfloat16 [1152, 1728], replicated, may hold values from -0.1875 to 0.1875
- space_output: bfloat16 [576, 1152], replicated, may hold values from -0.25 to 0.25
- time_input: bfloat16 [1152, 1728], replicated, may hold values from -0.1875 to 0.1875
- time_output: bfloat16 [576, 1152], replicated, may hold values from -0.25 to 0.25
- final_weight: bfloat16 [1152, 16], replicated, may hold values from -0.1875 to 0.1875
Outputs:
- next_states: float32 [512, 16, 128], P(('group', 'tok')), parts along dimension 0
The draws below stay inside these ranges and needn't reach their ends.
There are 2 independent parts, one for each index of `group`. The reference program is written for one: setup_inputs(seed, part) draws one part's arguments, and reference() takes and returns one part's arrays. A program takes and returns all parts, laid end to end along the dimension named above; an argument that names none is the same for every part. Nothing has to cross between parts.
All inputs are finite; a program needn't handle non-finite values.
Results may differ from the reference program's by a relative error of at most 0.006.
Values may be sent and summed in bfloat16 or wider, within the bound.
A program may use at most 128 MiB of HBM per device.

```python
import jax
import jax.numpy as jnp
from jax import lax

D = 1152
HEADS = 8
HD = 72
LCH = 16
F = 16
P_SIZE = 16
ITERS = 2
HW = 128
INNER = 576
ROWS = 256


def steps_of(stream_key, shape, cuts, least, largest):
    gain, own = 1.0, jax.random.fold_in(stream_key, 6)
    for position, shards_of in cuts:
        steps = jnp.exp(jax.random.uniform(jax.random.fold_in(own, position), (shards_of,), jnp.float32, least / len(cuts), largest / len(cuts)))
        gain = gain * jnp.repeat(steps, shape[position] // shards_of).reshape([-1 if axis == position else 1 for axis in range(len(shape))])
    return gain


def centred(key, shape, spread, bound, shards=(), kind=jnp.bfloat16):
    values = spread * jax.random.normal(key, shape, jnp.float32)
    if shards:
        values = values * steps_of(key, shape, shards, -0.22, 0.18)
    return jnp.clip(values, -bound, bound).astype(kind)


def setup_inputs(seed: int = 0, part: int = 0) -> dict:
    arg_keys = jax.random.split(jax.random.key(seed), 13)
    part_splits = jax.random.split(jax.random.fold_in(arg_keys[12], part), 13)
    return {
        "initial_guess": centred(part_splits[0], (ROWS, LCH, HW), 1.0, 6.0, ((0, 16),), jnp.float32),
        "noise_draws": centred(part_splits[1], (ROWS, LCH, HW), 1.0, 6.0, ((0, 16),), jnp.float32),
        "drift_state": jnp.clip(jax.random.uniform(arg_keys[2], (P_SIZE,), jnp.float32, 0.0, 0.15), 0.0, 0.15),
        "drift_denoise": jnp.clip(jax.random.uniform(arg_keys[3], (P_SIZE,), jnp.float32, -0.4, -0.15), -0.4, -0.15),
        "noise_scale": jnp.clip(jax.random.uniform(arg_keys[4], (P_SIZE,), jnp.float32, 0.05, 0.3), 0.05, 0.3),
        "modulation": centred(arg_keys[5], (P_SIZE, 8, D), 0.4, 3.0, (), jnp.float32),
        "embed_weight": centred(arg_keys[6], (LCH, D), LCH ** -0.5, 1.5),
        "space_input": centred(arg_keys[7], (D, 3 * INNER), D ** -0.5, 0.1875),
        "space_output": centred(arg_keys[8], (INNER, D), INNER ** -0.5, 0.25),
        "time_input": centred(arg_keys[9], (D, 3 * INNER), D ** -0.5, 0.1875),
        "time_output": centred(arg_keys[10], (INNER, D), INNER ** -0.5, 0.25),
        "final_weight": centred(arg_keys[11], (D, LCH), D ** -0.5, 0.1875),
    }


def layer_norm(values):
    center = values - lax.optimization_barrier(jnp.mean(values, -1, keepdims=True))
    return center * lax.rsqrt(lax.optimization_barrier(jnp.mean(center * center, -1, keepdims=True)) + 1e-06)

def head_norm(values):
    return values * lax.rsqrt(lax.optimization_barrier(jnp.mean(values * values, -1, keepdims=True)) + 1e-06)

def attention_mix(normed, input_weight, output_weight):
    batches, length, feature_width = normed.shape
    packed = jnp.dot(normed.reshape(-1, feature_width), input_weight, preferred_element_type=jnp.float32)
    packed = packed.reshape(batches, length, 3, HEADS, HD)
    queries = head_norm(packed[:, :, 0]).astype(jnp.bfloat16)
    key_rows = head_norm(packed[:, :, 1]).astype(jnp.bfloat16)
    value_rows = packed[:, :, 2].astype(jnp.bfloat16)
    scores = jnp.einsum('blhe,bmhe->bhlm', queries.astype(jnp.float32), key_rows.astype(jnp.float32)) * HD ** (-0.5)
    weights = jnp.exp(scores)
    weights = (weights / lax.optimization_barrier(jnp.sum(weights, -1, keepdims=True))).astype(jnp.bfloat16)
    attended = jnp.einsum('bhlm,bmhe->blhe', weights.astype(jnp.float32), value_rows.astype(jnp.float32)).astype(jnp.bfloat16)
    result = jnp.dot(attended.reshape(-1, HEADS * HD), output_weight, preferred_element_type=jnp.float32)
    return result.reshape(batches, length, feature_width)

def denoiser(latent, modulation_row, embed_weight, space_input, space_output, time_input, time_output, final_weight):
    embedded = jnp.einsum('fch,cd->fhd', latent.astype(jnp.bfloat16).astype(jnp.float32), embed_weight.astype(jnp.float32))
    normed = (layer_norm(embedded) * (1.0 + modulation_row[1]) + modulation_row[0]).astype(jnp.bfloat16)
    after_space = (embedded + modulation_row[2] * attention_mix(normed, space_input, space_output)).astype(jnp.bfloat16)
    after_space = lax.optimization_barrier(after_space)
    hidden = jnp.swapaxes(after_space, 0, 1).astype(jnp.float32)
    normed = (layer_norm(hidden) * (1.0 + modulation_row[4]) + modulation_row[3]).astype(jnp.bfloat16)
    after_time = (hidden + modulation_row[5] * attention_mix(normed, time_input, time_output)).astype(jnp.bfloat16)
    after_time = lax.optimization_barrier(after_time).astype(jnp.float32)
    normed = (layer_norm(after_time) * (1.0 + modulation_row[7]) + modulation_row[6]).astype(jnp.bfloat16)
    return jnp.einsum('hfd,dc->fch', normed.astype(jnp.float32), final_weight.astype(jnp.float32))

def reference(initial_guess, noise_draws, drift_state, drift_denoise, noise_scale, modulation, embed_weight, space_input, space_output, time_input, time_output, final_weight):
    latent = initial_guess.reshape(P_SIZE, F, LCH, HW)
    fresh_noise = noise_draws.reshape(P_SIZE, F, LCH, HW)
    leading = (jnp.arange(P_SIZE) == 0)[:, None, None, None]
    rate_state = drift_state[:, None, None, None]
    rate_denoise = drift_denoise[:, None, None, None]
    rate_noise = noise_scale[:, None, None, None]
    running = latent
    for iteration in range(ITERS):
        predicted = lax.map(lambda paired: denoiser(paired[0], paired[1], embed_weight, space_input, space_output, time_input, time_output, final_weight), (latent, modulation))
        increment = rate_state * latent + rate_denoise * predicted + rate_noise * fresh_noise
        increment = jnp.where(leading, increment + latent, increment)
        running = jnp.cumsum(increment, axis=0)
        latent = jnp.concatenate([latent[:1], running[:-1]], axis=0)
    return running.reshape(ROWS, LCH, HW)
```

```python
import functools
import math

import jax
import jax.numpy as jnp
from jax import lax
from jax.experimental import pallas as pl
from jax.experimental.pallas import tpu as pltpu
from jax.sharding import PartitionSpec as P

HEADS = 8
HD = 72
P_SIZE = 16
ITERS = 2
LANES = 128
INNER = HEADS * HD
SIDE = math.isqrt(P_SIZE)
EPS = 1e-06
CHANNELS = 16
WIDE = 2 * LANES
ROWS_T = HEADS * CHANNELS
ROWS_AA = 3 * ROWS_T + 32
BASE = 512
TAIL = INNER - BASE
V_COLS = BASE + LANES
PACKED = 2 * HEADS * LANES + V_COLS
LAT, DUP, ZERO, ONE, ATT = 128, 144, 160, 184, 192
SCALE = HD**-0.5 * math.log2(math.e)
UNIT = HD**0.5 * math.log2(math.e)


def dot_rows(values, weight_rows, precision=None):
    return lax.dot_general(
        values,
        weight_rows,
        (((1,), (1,)), ((), ())),
        preferred_element_type=jnp.float32,
        precision=precision,
    )


def dot(values, weights):
    return jnp.dot(values, weights, preferred_element_type=jnp.float32)


def halves(values):
    high = values.astype(jnp.bfloat16)
    return high, (values - high.astype(jnp.float32)).astype(jnp.bfloat16)


def lane_of(shape):
    return lax.broadcasted_iota(jnp.int32, shape, len(shape) - 1)


def row_of(shape):
    return lax.broadcasted_iota(jnp.int32, shape, 0)


def centred(rows):
    return rows - jnp.mean(rows, -1, keepdims=True)


def by_head(rows, order):
    count, width = rows.shape
    if order == "hc":
        spread = jnp.concatenate([rows] * HEADS, axis=0)
        head = row_of(spread.shape) // count
    else:
        spread = jnp.broadcast_to(rows[:, None, :], (count, HEADS, width)).reshape(-1, width)
        head = row_of(spread.shape) % HEADS
    return jnp.where(lane_of(spread.shape) // HD == head, spread, 0.0)


def fold_kernel(
    step_ref, table_ref, embed_ref, space_in_ref, space_out_ref, time_in_ref, time_out_ref, final_ref,
    first_ref, offset_ref, packed_ref, square_ref, shift_ref, lines_ref,
):
    def table(row):
        return table_ref[row : row + 1, :]

    def zeros(rows, width=None):
        return jnp.zeros((rows, width or table_ref.shape[1]), jnp.float32)

    highest = lax.Precision.HIGHEST
    features = table_ref.shape[1]
    embed = centred(embed_ref[...].astype(jnp.float32))
    lines = embed * (1.0 + table(1))
    shift = jnp.concatenate([table(0), zeros(7)], axis=0)
    high, low = halves(lines)
    shift_high, shift_low = halves(shift)
    tail = jnp.concatenate([shift_high.astype(jnp.float32), shift_low.astype(jnp.float32)], axis=0)
    folded = dot_rows(
        jnp.concatenate([high, low, tail.astype(jnp.bfloat16)], axis=0), space_in_ref[...]
    )
    lat = folded[:CHANNELS] + folded[CHANNELS : 2 * CHANNELS]
    const = folded[2 * CHANNELS : 2 * CHANNELS + 8] + folded[2 * CHANNELS + 8 :]

    def part(values, which):
        return values[:, which * INNER : (which + 1) * INNER]

    query, key, value = (part(lat, which) for which in range(3))
    query_c, key_c, value_c = (part(const, which)[:1] for which in range(3))
    key_side = jnp.concatenate([key, key, key_c, zeros(7, INNER)], axis=0)
    query_side = jnp.concatenate([query, query, query_c, zeros(7, INNER)], axis=0)
    scores = dot_rows(
        jnp.concatenate([by_head(query, "hc"), by_head(query_c, "ch")], axis=0) * SCALE,
        key_side, highest,
    )
    key_square = dot_rows(
        jnp.concatenate([by_head(key, "ch"), by_head(key_c, "ch")], axis=0) * (1.0 / HD),
        key_side, highest,
    )
    query_square = dot_rows(
        jnp.concatenate([by_head(query, "ch"), by_head(query_c, "ch")], axis=0) * (1.0 / HD),
        query_side, highest,
    )
    gram = dot_rows(embed, jnp.concatenate([embed, embed, zeros(8)], axis=0), highest) * (
        1.0 / features
    )
    first = jnp.concatenate(
        [scores, key_square[:ROWS_T], query_square[:ROWS_T], gram, zeros(8, 2 * CHANNELS + 8)],
        axis=0,
    )
    high, low = halves(first)
    upper = lane_of(first.shape) < CHANNELS
    chosen = jnp.where(upper, high.astype(jnp.float32), low.astype(jnp.float32))
    first_ref[...] = chosen[:, : 2 * CHANNELS].astype(jnp.bfloat16)
    point = 2 * CHANNELS
    offset_ref[: ROWS_T + 8] = jnp.broadcast_to(scores[:, point : point + 1], (ROWS_T + 8, LANES))
    for index, square in enumerate((key_square, query_square)):
        start = ROWS_T + 8 + index * (ROWS_T + 8)
        offset_ref[start : start + ROWS_T] = jnp.broadcast_to(
            2.0 * square[:ROWS_T, point : point + 1], (ROWS_T, LANES)
        )
        offset_ref[start + ROWS_T : start + ROWS_T + 8] = jnp.broadcast_to(
            square[ROWS_T:, point : point + 1], (8, LANES)
        )

    value_high, value_low = halves(by_head(value, "hc"))
    const_high, const_low = halves(jnp.concatenate([value_c, zeros(7, INNER)], axis=0))
    tail = jnp.concatenate([const_high.astype(jnp.float32), const_low.astype(jnp.float32)], axis=0)
    mixed = dot(
        jnp.concatenate([value_high, value_low, tail.astype(jnp.bfloat16)], axis=0),
        space_out_ref[...],
    )
    gate = table(2)
    attended = centred(gate * (mixed[:ROWS_T] + mixed[ROWS_T : 2 * ROWS_T]))
    point = centred(gate * (mixed[2 * ROWS_T : 2 * ROWS_T + 8] + mixed[2 * ROWS_T + 8 :]))

    scaled = 1.0 + table(4)
    lat_high, lat_low = halves(embed * scaled)
    ends = jnp.concatenate([table(3), point[:1] * scaled, zeros(6)], axis=0)
    ends_high, ends_low = halves(ends)
    tail = jnp.concatenate([ends_high.astype(jnp.float32), ends_low.astype(jnp.float32)], axis=0)
    rows = jnp.concatenate(
        [(attended * scaled).astype(jnp.bfloat16), lat_high, lat_low, tail.astype(jnp.bfloat16)],
        axis=0,
    )

    def settle(columns):
        lat = columns[LAT:DUP] + columns[DUP : DUP + CHANNELS]
        lat_high = lat.astype(jnp.bfloat16).astype(jnp.float32)
        ends = columns[DUP + CHANNELS : DUP + CHANNELS + 8] + columns[DUP + CHANNELS + 8 :]
        ends_high = ends.astype(jnp.bfloat16).astype(jnp.float32)
        ends_low = ends - ends_high
        width = columns.shape[1]
        return jnp.concatenate(
            [
                columns[:LAT], lat_high, lat - lat_high,
                ends_high[:1], ends_high[:1], ends_low[:1], zeros(ONE - ZERO - 3, width),
                ends_high[1:2], ends_low[1:2], zeros(WIDE - ONE - 2, width),
            ],
            axis=0,
        ).astype(jnp.bfloat16)

    packed_ref[...] = jnp.zeros_like(packed_ref)
    for which in range(3):
        columns = settle(dot_rows(rows, time_in_ref[which * INNER : (which + 1) * INNER, :]))
        if which == 2:
            start = 2 * HEADS * LANES
            packed_ref[:, start : start + BASE] = columns[:, :BASE]
            packed_ref[:, start + BASE + LANES - TAIL : start + V_COLS] = columns[:, BASE:]
        else:
            for head in range(HEADS):
                start = (which * HEADS + head) * LANES
                packed_ref[:, start : start + HD] = columns[:, head * HD : (head + 1) * HD]

    gate = table(5)
    lat_high, lat_low = halves(embed)
    point_high, point_low = halves(point[:1])
    lines_ref[:LAT] = attended.astype(jnp.bfloat16)
    lines_ref[LAT:DUP] = lat_high
    lines_ref[DUP:ZERO] = lat_low
    lines_ref[ZERO:ATT] = jnp.concatenate(
        [
            zeros(ONE - ZERO), point_high.astype(jnp.float32), point_low.astype(jnp.float32),
            zeros(ATT - ONE - 2),
        ],
        axis=0,
    ).astype(jnp.bfloat16)
    lines_ref[ATT:WIDE] = centred(gate * time_out_ref[BASE:].astype(jnp.float32)).astype(jnp.bfloat16)
    for start in range(0, BASE, LANES):
        lines_ref[WIDE + start : WIDE + start + LANES] = centred(
            gate * time_out_ref[start : start + LANES].astype(jnp.float32)
        ).astype(jnp.bfloat16)
    final = final_ref[...].astype(jnp.float32)
    shift_ref[...] = jnp.broadcast_to(
        jnp.sum(final * table(6), -1, keepdims=True), (CHANNELS, LANES)
    )
    base = jnp.concatenate(
        [
            lines_ref[:ZERO],
            (final * (1.0 + table(7))).astype(jnp.bfloat16),
            lines_ref[ZERO + CHANNELS : WIDE],
        ],
        axis=0,
    )
    lane = lane_of((1, WIDE))
    plain = (lane >= ZERO) & (lane < ZERO + CHANNELS)
    tiles = lines_ref.shape[0] // WIDE
    for column in range(tiles):
        other = lines_ref[column * WIDE : (column + 1) * WIDE] if column else base
        for row in range(column, tiles):
            block = dot_rows(lines_ref[row * WIDE : (row + 1) * WIDE], other)
            block = block * ((1.0 if row == column else 2.0) / features) if column else (
                block * jnp.where(plain, 1.0, (1.0 if row == column else 2.0) / features)
            )
            square_ref[row * WIDE : (row + 1) * WIDE, column * WIDE : (column + 1) * WIDE] = (
                block.astype(jnp.bfloat16)
            )


def space_kernel(latent_ref, first_ref, offset_ref, token_ref):
    frames, channels, spatial = latent_ref.shape
    bf16 = jnp.bfloat16
    f32 = jnp.float32
    head_lane = lane_of((spatial, LANES)) // CHANNELS
    head_row = row_of((HEADS, spatial))
    kept = lane_of((spatial, 64))
    kept = (kept < 32) | (kept >= 56)

    def offset(start, rows):
        return offset_ref[start : start + rows]

    stacked = []
    for frame in range(frames):
        latent = latent_ref[frame].astype(bf16)
        stacked.append(jnp.concatenate([latent, latent], axis=0))
    product = dot(first_ref[...], jnp.concatenate(stacked, axis=1))
    for frame in range(frames):
        result = product[:, frame * spatial : (frame + 1) * spatial]
        latent = stacked[frame][:channels].astype(f32)
        gram = result[3 * ROWS_T + 8 : 3 * ROWS_T + 8 + channels]
        variance = jnp.maximum(jnp.sum(latent * gram, 0, keepdims=True), 0.0) + EPS
        rate = lax.rsqrt(variance)
        spread = variance * rate
        scaled = latent * rate

        def norm(index):
            start = ROWS_T + 8 + index * ROWS_T
            place = ROWS_T + 8 + index * (ROWS_T + 8)
            terms = rate * result[start : start + ROWS_T] + offset(place, ROWS_T)
            terms = terms.reshape(channels, HEADS, spatial) * scaled[:, None, :]
            total = jnp.sum(terms, 0) + offset(place + ROWS_T, 8)
            return lax.rsqrt(jnp.maximum(total, 0.0) + EPS)

        key_rate, query_rate = norm(0), norm(1)
        query_rate = (query_rate * rate).T
        terms = rate * result[:ROWS_T] + offset(0, ROWS_T)
        point = (rate * result[ROWS_T : ROWS_T + 8] + offset(ROWS_T, 8)) * key_rate
        point_high = point.astype(bf16).astype(f32)
        point_low = point - point_high
        spread = jnp.broadcast_to(spread, (8, spatial))
        spread_high = spread.astype(bf16).astype(f32)
        ends = jnp.concatenate(
            [spread_high, spread - spread_high, spread_high, jnp.ones_like(spread)], axis=0
        ).astype(bf16)
        tokens = jnp.concatenate([stacked[frame], ends], axis=0).T

        def columns(head):
            own = terms[head * channels : (head + 1) * channels] * key_rate[head : head + 1]
            high, low = halves(own)
            mine = head_row == head
            point_mine = jnp.where(mine, point_high, 0.0)
            ends = jnp.concatenate(
                [point_mine, point_mine, jnp.where(mine, point_low, 0.0), jnp.zeros_like(point_mine)],
                axis=0,
            ).astype(bf16)
            return jnp.concatenate([high, low, ends], axis=0)

        spot = jnp.concatenate([scaled] * HEADS, axis=0).astype(bf16).T
        mixed = None
        weights, sources = [], []
        for pair in range(HEADS // 2):
            heads = (2 * pair, 2 * pair + 1)
            score = dot(tokens, jnp.concatenate([columns(head) for head in heads], axis=1))
            for place, head in enumerate(heads):
                own = score[:, place * spatial : (place + 1) * spatial]
                weights.append(jnp.exp2(own * query_rate[:, head : head + 1]).astype(bf16))
                mine = head_lane == head
                sources.append(
                    jnp.concatenate(
                        [
                            jnp.where(mine, spot, jnp.zeros_like(spot)),
                            jnp.where(mine, 1.0, 0.0).astype(bf16),
                        ],
                        axis=1,
                    )
                )
        mixed = dot(jnp.concatenate(weights, axis=1), jnp.concatenate(sources, axis=0))
        average = mixed[:, :LANES] / mixed[:, LANES:]
        token_ref[frame, :, :LANES] = average.astype(bf16)
        token_ref[frame, :, LANES:] = jnp.concatenate(
            [jnp.where(kept, tokens, jnp.zeros_like(tokens)), jnp.zeros_like(tokens)], axis=1
        )


def time_kernel(fused, *refs):
    step_ref, token_ref, packed_ref, square_ref, shift_ref, *refs = refs
    if fused:
        latent_ref, noise_ref, *rate_refs, increment_ref, sent_ref = refs[:7]
    else:
        result_ref = refs[0]
    predicted_ref = refs[-1]
    bf16 = jnp.bfloat16
    f32 = jnp.float32
    frames, positions, width = token_ref.shape
    count = frames * positions
    chunk = 8
    rows = frames * chunk
    tokens = token_ref[...].reshape(count, width)
    variance = jnp.sum(tokens.astype(f32) * dot(tokens, square_ref[:WIDE, :WIDE]), -1, keepdims=True)
    variance = jnp.maximum(variance, 0.0) + EPS
    pace = lax.rsqrt(variance)
    spread = variance * pace
    spread_high = spread.astype(bf16).astype(f32)
    lane = lane_of((count, LANES))
    upper = tokens[:, LANES:].astype(f32)
    upper = jnp.where((lane == ZERO - LANES) | (lane == ZERO - LANES + 2), spread_high, upper)
    upper = jnp.where(lane == ZERO - LANES + 1, spread - spread_high, upper)
    entry = jnp.concatenate([tokens[:, :LANES], upper.astype(bf16)], axis=1)
    packed = dot(entry, packed_ref[...])
    floor = (HD * EPS) * variance
    keep = (row_of((rows, rows)) % chunk) == (lane_of((rows, rows)) % chunk)
    value_lane = lane_of((rows, V_COLS))
    value_lane = jnp.where(value_lane < BASE, value_lane, jnp.where(value_lane < BASE + LANES - TAIL, -1, value_lane - (LANES - TAIL)))
    value_head = jnp.where(value_lane < 0, -1, value_lane // HD)
    parts = positions // chunk

    def of_part(values, part):
        lanes = values.shape[1]
        return values.reshape(frames, parts, chunk, lanes)[:, part].reshape(rows, lanes)

    for part in range(parts):
        own_floor = of_part(floor, part)
        own_tokens = of_part(tokens.astype(f32), part)
        values = of_part(packed[:, 2 * HEADS * LANES :], part) * of_part(pace, part)
        values = values.astype(bf16)

        def slab(which, head, gain):
            start = (which * HEADS + head) * LANES
            own = of_part(packed[:, start : start + LANES], part)
            size = lax.rsqrt(jnp.sum(own * own, -1, keepdims=True) + own_floor)
            return (own * (size * gain if gain else size)).astype(bf16)

        weights = []
        for pair in range(HEADS // 2):
            heads = (2 * pair, 2 * pair + 1)
            query = jnp.concatenate([slab(0, head, UNIT) for head in heads], axis=1)
            key = [slab(1, head, None) for head in heads]
            blank = jnp.zeros_like(key[0])
            keys = jnp.concatenate(
                [jnp.concatenate([key[0], blank], axis=1), jnp.concatenate([blank, key[1]], axis=1)],
                axis=0,
            )
            score = dot_rows(query, keys)
            for place in range(2):
                weight = jnp.where(keep, jnp.exp2(score[:, place * rows : (place + 1) * rows]), 0.0)
                total = jnp.sum(weight, -1, keepdims=True)
                weights.append((weight * (1.0 / total)).astype(bf16))

        def mixed(heads, start, stop):
            source = [
                jnp.where(value_head[:, start:stop] == head, values[:, start:stop], jnp.zeros((), bf16))
                for head in heads
            ]
            return dot(
                jnp.concatenate([weights[head] for head in heads], axis=1),
                jnp.concatenate(source, axis=0),
            )

        def heads_in(start, stop):
            return range(start // HD, (stop - 1) // HD + 1)

        low = mixed(heads_in(0, WIDE), 0, WIDE)
        high = mixed(heads_in(WIDE, BASE), WIDE, BASE)
        tail = mixed(heads_in(BASE, INNER), BASE, V_COLS)
        state = jnp.concatenate(
            [own_tokens[:, :LANES], own_tokens[:, LANES:] + tail, low, high], axis=1
        ).astype(bf16)
        total = jnp.zeros((rows, LANES), f32)
        for column in range(state.shape[1] // WIDE):
            own = slice(column * WIDE, (column + 1) * WIDE)
            block = dot(state[:, column * WIDE :], square_ref[column * WIDE :, own])
            if column == 0:
                predicted = block[:, LANES:]
            for half in range(2):
                lanes = slice(half * LANES, (half + 1) * LANES)
                total = total + block[:, lanes] * state[:, own][:, lanes].astype(f32)
        rate = lax.rsqrt(jnp.maximum(jnp.sum(total, -1, keepdims=True), 0.0) + EPS)
        start = pl.multiple_of(pl.program_id(0) * positions + part * chunk, chunk)
        predicted_ref[:, pl.ds(start, chunk), :] = (predicted * rate).reshape(frames, chunk, LANES)

    @pl.when(pl.program_id(0) == pl.num_programs(0) - 1)
    def _():
        if fused:
            timestep = step_ref[0]
            rate_state, rate_denoise, rate_noise = (ref[timestep] for ref in rate_refs)
            rate_state = rate_state + jnp.where(timestep == 0, 1.0, 0.0)
        for frame in range(frames):
            turned = predicted_ref[frame].T[ZERO - LANES : ZERO - LANES + CHANNELS]
            turned = turned + shift_ref[:, : turned.shape[1]]
            if fused:
                turned = (
                    rate_state * latent_ref[frame]
                    + rate_denoise * turned
                    + rate_noise * noise_ref[frame]
                )
                increment_ref[frame] = turned
                sent_ref[frame] = turned.astype(jnp.bfloat16)
            else:
                result_ref[frame] = turned


def whole(array):
    zeros = (0,) * array.ndim
    return pl.BlockSpec(array.shape, lambda *_: zeros, pipeline_mode=pl.Buffered(1))


def fold(own, modulation, embed_weight, space_input, space_output, time_input, time_output, final_weight):
    features = modulation.shape[2]
    shapes = [
        ((ROWS_AA, 2 * CHANNELS), jnp.bfloat16),
        ((3 * (ROWS_T + 8), LANES), jnp.float32),
        ((WIDE, PACKED), jnp.bfloat16),
        ((BASE + WIDE, BASE + WIDE), jnp.bfloat16),
        ((CHANNELS, LANES), jnp.float32),
    ]
    weights = (embed_weight, space_input, space_output, time_input, time_output, final_weight)
    return pl.pallas_call(
        fold_kernel,
        out_shape=[jax.ShapeDtypeStruct(*shape) for shape in shapes],
        grid_spec=pltpu.PrefetchScalarGridSpec(
            num_scalar_prefetch=1,
            grid=(1,),
            in_specs=[
                pl.BlockSpec(
                    (None,) + modulation.shape[1:],
                    lambda step, own: (own[0], 0, 0),
                    pipeline_mode=pl.Buffered(1),
                )
            ]
            + [whole(weight) for weight in weights],
            out_specs=[
                pl.BlockSpec(shape, lambda *_: (0, 0), pipeline_mode=pl.Buffered(1))
                for shape, kind in shapes
            ],
            scratch_shapes=[pltpu.VMEM((BASE + WIDE, features), jnp.bfloat16)],
        ),
        compiler_params=pltpu.CompilerParams(vmem_limit_bytes=60 * 1024 * 1024),
        name="fold",
    )(own, modulation, *weights)


def space_block(latent, first, offset):
    frames, channels, spatial = latent.shape
    step_frames = math.gcd(frames, 2)
    return pl.pallas_call(
        space_kernel,
        out_shape=jax.ShapeDtypeStruct((frames, spatial, WIDE), jnp.bfloat16),
        grid=(frames // step_frames,),
        in_specs=[
            pl.BlockSpec((step_frames, channels, spatial), lambda step: (step, 0, 0)),
            whole(first),
            whole(offset),
        ],
        out_specs=pl.BlockSpec((step_frames, spatial, WIDE), lambda step: (step, 0, 0)),
        compiler_params=pltpu.CompilerParams(vmem_limit_bytes=60 * 1024 * 1024),
        name="space_block",
    )(latent, first, offset)


def time_block(own, tokens, packed, square, shift, fused=()):
    frames, positions, width = tokens.shape
    step_positions = math.gcd(positions, 16)
    shape = (frames, CHANNELS, positions)
    kinds = [jnp.float32] + [jnp.bfloat16] * bool(fused)
    return pl.pallas_call(
        functools.partial(time_kernel, bool(fused)),
        out_shape=[jax.ShapeDtypeStruct(shape, kind) for kind in kinds],
        grid_spec=pltpu.PrefetchScalarGridSpec(
            num_scalar_prefetch=1,
            grid=(positions // step_positions,),
            in_specs=[
                pl.BlockSpec((frames, step_positions, width), lambda step, own: (0, step, 0)),
                whole(packed),
                whole(square),
                whole(shift),
            ]
            + [
                whole(array) if array.ndim > 1 else pl.BlockSpec(memory_space=pltpu.SMEM)
                for array in fused
            ],
            out_specs=[
                pl.BlockSpec(shape, lambda step, own: (0, 0, 0), pipeline_mode=pl.Buffered(1))
                for kind in kinds
            ],
            scratch_shapes=[pltpu.VMEM((frames, positions, LANES), jnp.float32)],
        ),
        compiler_params=pltpu.CompilerParams(vmem_limit_bytes=60 * 1024 * 1024),
        name="time_block",
    )(own, tokens, packed, square, shift, *fused)


def carry_kernel(
    last, groups, sent_ref, increment_ref, latent_ref, out_ref,
    part_ref, total_ref, plane_ref, early_ref, stage_ref, before_ref,
    part_send, part_recv, plane_send, plane_recv, stage_send, stage_recv,
):
    quarter = part_ref.shape[1]
    own = lax.axis_index("tok")
    timestep = own // groups
    plane, seat = timestep // SIDE, timestep % SIDE

    def device(plane, seat):
        return {"tok": (plane * SIDE + seat) * groups + own % groups}

    def seat_after(hop):
        return (seat + hop) % SIDE

    barrier = pltpu.get_barrier_semaphore()
    for hop in range(1, SIDE):
        for target in (device(plane, seat_after(hop)), device((plane + hop) % SIDE, seat)):
            pl.semaphore_signal(
                barrier, inc=1, device_id=target, device_id_type=pl.DeviceIdType.MESH
            )
    pl.semaphore_wait(barrier, 2 * (SIDE - 1))

    def copy(source, target, send, receive, to):
        return pltpu.make_async_remote_copy(
            src_ref=source,
            dst_ref=target,
            send_sem=send,
            recv_sem=receive,
            device_id=to,
            device_id_type=pl.DeviceIdType.MESH,
        )

    def rows_of(index):
        return pl.ds(pl.multiple_of(index * quarter, quarter), quarter)

    parts = []
    for hop in range(1, SIDE):
        seat_to = seat_after(hop)
        parts.append(
            copy(
                sent_ref.at[rows_of(seat_to)], part_ref.at[hop - 1],
                part_send.at[hop - 1], part_recv.at[hop - 1], device(plane, seat_to),
            )
        )
        parts[-1].start()
    held = [sent_ref[rows_of(seat)].astype(jnp.float32)]
    for hop in range(1, SIDE):
        parts[hop - 1].wait_recv()
        held.append(part_ref[hop - 1].astype(jnp.float32))
    total_ref[...] = functools.reduce(jnp.add, held).astype(jnp.bfloat16)
    planes = [
        copy(
            total_ref, plane_ref.at[hop - 1], plane_send.at[hop - 1], plane_recv.at[hop - 1],
            device((plane + hop) % SIDE, seat),
        )
        for hop in range(1, SIDE)
    ]
    for hop in range(1, SIDE):
        pl.when(plane + hop < SIDE)(planes[hop - 1].start)

    def earlier_seats(limit):
        total = jnp.zeros_like(held[0])
        for hop in range(SIDE):
            total = total + jnp.where((seat + SIDE - hop) % SIDE < limit, held[hop], 0.0)
        return total

    early_ref[...] = jnp.zeros_like(early_ref)
    for hop in range(1, SIDE):

        @pl.when(plane >= hop)
        def _(hop=hop):
            planes[hop - 1].wait_recv()
            early_ref[...] += plane_ref[hop - 1].astype(jnp.float32)

    early = early_ref[...]
    stages = []
    for hop in range(1, SIDE):
        seat_to = seat_after(hop)
        stage_ref[hop - 1] = early + earlier_seats(seat_to)
        stages.append(
            copy(
                stage_ref.at[hop - 1], before_ref.at[rows_of(seat)],
                stage_send.at[hop - 1], stage_recv.at[hop - 1], device(plane, seat_to),
            )
        )
        stages[-1].start()
    own_rows = rows_of(seat)

    def settle(rows, before):
        if last:
            out_ref[rows] = before + increment_ref[rows]
        else:
            out_ref[rows] = jnp.where(timestep == 0, latent_ref[rows], before)

    settle(own_rows, early + earlier_seats(seat))
    for hop in range(1, SIDE):
        stages[hop - 1].wait_recv()
        rows = rows_of((seat + SIDE - hop) % SIDE)
        settle(rows, before_ref[rows])
    for hop in range(1, SIDE):
        parts[hop - 1].wait_send()
        pl.when(plane + hop < SIDE)(planes[hop - 1].wait_send)
        stages[hop - 1].wait_send()


def carried_kernel(last, groups, sent, increment, latent):
    rows, lanes = sent.shape
    quarter = rows // SIDE
    hops = SIDE - 1
    vmem = pl.BlockSpec(memory_space=pltpu.VMEM)
    return pl.pallas_call(
        functools.partial(carry_kernel, last, groups),
        out_shape=jax.ShapeDtypeStruct((rows, lanes), jnp.float32),
        in_specs=[vmem] * 3,
        out_specs=vmem,
        scratch_shapes=[
            pltpu.VMEM((hops, quarter, lanes), jnp.bfloat16),
            pltpu.VMEM((quarter, lanes), jnp.bfloat16),
            pltpu.VMEM((hops, quarter, lanes), jnp.bfloat16),
            pltpu.VMEM((quarter, lanes), jnp.float32),
            pltpu.VMEM((hops, quarter, lanes), jnp.float32),
            pltpu.VMEM((rows, lanes), jnp.float32),
        ]
        + [pltpu.SemaphoreType.DMA((hops,))] * 6,
        compiler_params=pltpu.CompilerParams(collective_id=int(last), has_side_effects=True),
        name="carry_last" if last else "carry",
    )(sent, increment, latent)


def carried_in(last, groups, same_block, timestep, sent, increment, latent):
    rows = sent.size // LANES
    if sent.shape[-1] == LANES and rows % (SIDE * 16) == 0:
        flat = [array.reshape(rows, LANES) for array in (sent, increment, latent)]
        return carried_kernel(last, groups, *flat).reshape(latent.shape)
    gathered = lax.all_gather(
        sent, "tok", axis_index_groups=same_block if groups > 1 else None
    )
    earlier = (jnp.arange(P_SIZE) < timestep)[:, None, None, None]
    before = jnp.sum(jnp.where(earlier, gathered.astype(jnp.float32), 0.0), axis=0)
    return before + increment if last else jnp.where(timestep == 0, latent, before)


def body(
    initial_guess,
    noise_draws,
    drift_state,
    drift_denoise,
    noise_scale,
    modulation,
    embed_weight,
    space_input,
    space_output,
    time_input,
    time_output,
    final_weight,
):
    devices = lax.axis_size("tok")
    own_index = lax.axis_index("tok")
    groups = devices // P_SIZE
    timestep = own_index // groups
    own = jnp.reshape(timestep, (1,)).astype(jnp.int32)
    rates = (drift_state, drift_denoise, noise_scale)
    same_step = [[step * groups + block for block in range(groups)] for step in range(P_SIZE)]
    same_block = [[step * groups + block for step in range(P_SIZE)] for block in range(groups)]
    first, offset, packed, square, shift = fold(
        own, modulation, embed_weight, space_input.T, space_output, time_input.T, time_output,
        final_weight.T,
    )
    latent = initial_guess
    for iteration in range(ITERS):
        tokens = space_block(latent, first, offset)
        if groups == 1:
            increment, sent = time_block(
                own, tokens, packed, square, shift, (latent, noise_draws) + rates
            )
        else:
            tokens = lax.all_to_all(
                tokens, "tok", split_axis=1, concat_axis=0, axis_index_groups=same_step, tiled=True
            )
            (predicted,) = time_block(own, tokens, packed, square, shift)
            predicted = lax.all_to_all(
                predicted, "tok", split_axis=0, concat_axis=2, axis_index_groups=same_step, tiled=True
            )
            rate_state, rate_denoise, rate_noise = (
                lax.dynamic_index_in_dim(rate, timestep, 0, keepdims=False) for rate in rates
            )
            rate_state = rate_state + jnp.where(timestep == 0, 1.0, 0.0)
            increment = rate_state * latent + rate_denoise * predicted + rate_noise * noise_draws
            sent = increment.astype(jnp.bfloat16)
        latent = carried_in(
            iteration == ITERS - 1, groups, same_block, timestep, sent, increment, latent
        )
    return latent


def solution(mesh):
    placed = (
        P(("group", "tok"), None, None),
        P(("group", "tok"), None, None),
        P(),
        P(),
        P(),
        P(),
        P(),
        P(),
        P(),
        P(),
        P(),
        P(),
    )
    return jax.shard_map(
        body, mesh=mesh, in_specs=placed, out_specs=P(("group", "tok"), None, None), check_vma=False
    )
```

```python
import functools
import math

import jax
import jax.numpy as jnp
from jax import lax
from jax.experimental import pallas as pl
from jax.experimental.pallas import tpu as pltpu
from jax.sharding import PartitionSpec as P

HEADS = 8
HD = 72
P_SIZE = 16
ITERS = 2
LANES = 128
INNER = HEADS * HD
SIDE = math.isqrt(P_SIZE)
EPS = 1e-06
CHANNELS = 16
WIDE = 2 * LANES
ROWS_T = HEADS * CHANNELS
ROWS_AA = 3 * ROWS_T + 32
BASE = 512
TAIL = INNER - BASE
LAT, DUP, ZERO, ONE, ATT = 128, 144, 160, 184, 192
SCALE = HD**-0.5 * math.log2(math.e)
UNIT = HD**0.5 * math.log2(math.e)


def dot_rows(values, weight_rows, precision=None):
    return lax.dot_general(
        values,
        weight_rows,
        (((1,), (1,)), ((), ())),
        preferred_element_type=jnp.float32,
        precision=precision,
    )


def dot(values, weights):
    return jnp.dot(values, weights, preferred_element_type=jnp.float32)


def halves(values):
    high = values.astype(jnp.bfloat16)
    return high, (values - high.astype(jnp.float32)).astype(jnp.bfloat16)


def lane_of(shape):
    return lax.broadcasted_iota(jnp.int32, shape, len(shape) - 1)


def row_of(shape):
    return lax.broadcasted_iota(jnp.int32, shape, 0)


def centred(rows):
    return rows - jnp.mean(rows, -1, keepdims=True)


def by_head(rows, order):
    count, width = rows.shape
    if order == "hc":
        spread = jnp.concatenate([rows] * HEADS, axis=0)
        head = row_of(spread.shape) // count
    else:
        spread = jnp.broadcast_to(rows[:, None, :], (count, HEADS, width)).reshape(-1, width)
        head = row_of(spread.shape) % HEADS
    return jnp.where(lane_of(spread.shape) // HD == head, spread, 0.0)


def fold_kernel(
    step_ref, table_ref, embed_ref, space_in_ref, space_out_ref, time_in_ref, time_out_ref, final_ref,
    first_ref, offset_ref, packed_ref, square_ref, shift_ref, lines_ref,
):
    def table(row):
        return table_ref[row : row + 1, :]

    def zeros(rows, width=None):
        return jnp.zeros((rows, width or table_ref.shape[1]), jnp.float32)

    highest = lax.Precision.HIGHEST
    features = table_ref.shape[1]
    embed = centred(embed_ref[...].astype(jnp.float32))
    lines = embed * (1.0 + table(1))
    shift = jnp.concatenate([table(0), zeros(7)], axis=0)
    high, low = halves(lines)
    shift_high, shift_low = halves(shift)
    tail = jnp.concatenate([shift_high.astype(jnp.float32), shift_low.astype(jnp.float32)], axis=0)
    folded = dot_rows(
        jnp.concatenate([high, low, tail.astype(jnp.bfloat16)], axis=0), space_in_ref[...]
    )
    lat = folded[:CHANNELS] + folded[CHANNELS : 2 * CHANNELS]
    const = folded[2 * CHANNELS : 2 * CHANNELS + 8] + folded[2 * CHANNELS + 8 :]

    def part(values, which):
        return values[:, which * INNER : (which + 1) * INNER]

    query, key, value = (part(lat, which) for which in range(3))
    query_c, key_c, value_c = (part(const, which)[:1] for which in range(3))
    key_side = jnp.concatenate([key, key, key_c, zeros(7, INNER)], axis=0)
    query_side = jnp.concatenate([query, query, query_c, zeros(7, INNER)], axis=0)
    scores = dot_rows(
        jnp.concatenate([by_head(query, "hc"), by_head(query_c, "ch")], axis=0) * SCALE,
        key_side, highest,
    )
    key_square = dot_rows(
        jnp.concatenate([by_head(key, "ch"), by_head(key_c, "ch")], axis=0) * (1.0 / HD),
        key_side, highest,
    )
    query_square = dot_rows(
        jnp.concatenate([by_head(query, "ch"), by_head(query_c, "ch")], axis=0) * (1.0 / HD),
        query_side, highest,
    )
    gram = dot_rows(embed, jnp.concatenate([embed, embed, zeros(8)], axis=0), highest) * (
        1.0 / features
    )
    first = jnp.concatenate(
        [scores, key_square[:ROWS_T], query_square[:ROWS_T], gram, zeros(8, 2 * CHANNELS + 8)],
        axis=0,
    )
    high, low = halves(first)
    upper = lane_of(first.shape) < CHANNELS
    chosen = jnp.where(upper, high.astype(jnp.float32), low.astype(jnp.float32))
    first_ref[...] = chosen[:, : 2 * CHANNELS].astype(jnp.bfloat16)
    point = 2 * CHANNELS
    offset_ref[: ROWS_T + 8] = jnp.broadcast_to(scores[:, point : point + 1], (ROWS_T + 8, LANES))
    for index, square in enumerate((key_square, query_square)):
        start = ROWS_T + 8 + index * (ROWS_T + 8)
        offset_ref[start : start + ROWS_T] = jnp.broadcast_to(
            2.0 * square[:ROWS_T, point : point + 1], (ROWS_T, LANES)
        )
        offset_ref[start + ROWS_T : start + ROWS_T + 8] = jnp.broadcast_to(
            square[ROWS_T:, point : point + 1], (8, LANES)
        )

    value_high, value_low = halves(by_head(value, "hc"))
    const_high, const_low = halves(jnp.concatenate([value_c, zeros(7, INNER)], axis=0))
    tail = jnp.concatenate([const_high.astype(jnp.float32), const_low.astype(jnp.float32)], axis=0)
    mixed = dot(
        jnp.concatenate([value_high, value_low, tail.astype(jnp.bfloat16)], axis=0),
        space_out_ref[...],
    )
    gate = table(2)
    attended = centred(gate * (mixed[:ROWS_T] + mixed[ROWS_T : 2 * ROWS_T]))
    point = centred(gate * (mixed[2 * ROWS_T : 2 * ROWS_T + 8] + mixed[2 * ROWS_T + 8 :]))

    scaled = 1.0 + table(4)
    lat_high, lat_low = halves(embed * scaled)
    ends = jnp.concatenate([table(3), point[:1] * scaled, zeros(6)], axis=0)
    ends_high, ends_low = halves(ends)
    tail = jnp.concatenate([ends_high.astype(jnp.float32), ends_low.astype(jnp.float32)], axis=0)
    rows = jnp.concatenate(
        [(attended * scaled).astype(jnp.bfloat16), lat_high, lat_low, tail.astype(jnp.bfloat16)],
        axis=0,
    )

    def settle(columns):
        lat = columns[LAT:DUP] + columns[DUP : DUP + CHANNELS]
        lat_high = lat.astype(jnp.bfloat16).astype(jnp.float32)
        ends = columns[DUP + CHANNELS : DUP + CHANNELS + 8] + columns[DUP + CHANNELS + 8 :]
        ends_high = ends.astype(jnp.bfloat16).astype(jnp.float32)
        ends_low = ends - ends_high
        width = columns.shape[1]
        return jnp.concatenate(
            [
                columns[:LAT], lat_high, lat - lat_high,
                ends_high[:1], ends_high[:1], ends_low[:1], zeros(ONE - ZERO - 3, width),
                ends_high[1:2], ends_low[1:2], zeros(WIDE - ONE - 2, width),
            ],
            axis=0,
        ).astype(jnp.bfloat16)

    for which in range(3):
        own = slice(which * INNER, (which + 1) * INNER)
        packed_ref[own] = settle(dot_rows(rows, time_in_ref[own, :])).T

    gate = table(5)
    lat_high, lat_low = halves(embed)
    point_high, point_low = halves(point[:1])
    lines_ref[:LAT] = attended.astype(jnp.bfloat16)
    lines_ref[LAT:DUP] = lat_high
    lines_ref[DUP:ZERO] = lat_low
    lines_ref[ZERO:ATT] = jnp.concatenate(
        [
            zeros(ONE - ZERO), point_high.astype(jnp.float32), point_low.astype(jnp.float32),
            zeros(ATT - ONE - 2),
        ],
        axis=0,
    ).astype(jnp.bfloat16)
    lines_ref[ATT:WIDE] = centred(gate * time_out_ref[BASE:].astype(jnp.float32)).astype(jnp.bfloat16)
    for start in range(0, BASE, LANES):
        lines_ref[WIDE + start : WIDE + start + LANES] = centred(
            gate * time_out_ref[start : start + LANES].astype(jnp.float32)
        ).astype(jnp.bfloat16)
    final = final_ref[...].astype(jnp.float32)
    shift_ref[...] = jnp.broadcast_to(
        jnp.sum(final * table(6), -1, keepdims=True), (CHANNELS, LANES)
    )
    base = jnp.concatenate(
        [
            lines_ref[:ZERO],
            (final * (1.0 + table(7))).astype(jnp.bfloat16),
            lines_ref[ZERO + CHANNELS : WIDE],
        ],
        axis=0,
    )
    line = row_of((WIDE, 1))
    plain = (line >= ZERO) & (line < ZERO + CHANNELS)
    tiles = lines_ref.shape[0] // WIDE
    for column in range(tiles):
        other = lines_ref[column * WIDE : (column + 1) * WIDE] if column else base
        for row in range(column, tiles):
            block = dot_rows(other, lines_ref[row * WIDE : (row + 1) * WIDE])
            block = block * ((1.0 if row == column else 2.0) / features) if column else (
                block * jnp.where(plain, 1.0, (1.0 if row == column else 2.0) / features)
            )
            square_ref[column * WIDE : (column + 1) * WIDE, row * WIDE : (row + 1) * WIDE] = (
                block.astype(jnp.bfloat16)
            )


def stack(*parts):
    return jnp.concatenate(parts, axis=0)


def beside(*parts):
    return jnp.concatenate(parts, axis=1)


def on_diagonal(first, second):
    blank = jnp.zeros_like(first)
    return stack(beside(first, blank), beside(blank, second))


def interleave(tasks):
    tasks, running = list(tasks), []
    while tasks or running:
        running += [tasks.pop(0)] if tasks else []
        running = [task for task in running if next(task, tasks) is not tasks]


def pause(turns):
    for turn in range(turns):
        yield


def wait_for(state, key):
    while key not in state:
        yield


def space_kernel(lags, latent_ref, first_ref, offset_ref, token_ref):
    frames, channels, spatial = latent_ref.shape
    bf16 = jnp.bfloat16
    f32 = jnp.float32
    row = row_of((8, spatial))
    blank = jnp.zeros((8, spatial), f32)
    ones = jnp.ones((8, spatial), f32)
    states = [{} for frame in range(frames)]

    def offset(start, rows):
        return offset_ref[start : start + rows]

    def twice(frame):
        latent = latent_ref[frame].astype(bf16)
        return stack(latent, latent)

    def couple_task(frame):
        own = range(frame, min(frame + 2, frames))
        product = dot(first_ref[...], beside(*(twice(index) for index in own)))
        yield from pause(lags[0])
        for place, index in enumerate(own):
            states[index]["result"] = product[:, place * spatial : (place + 1) * spatial]

    def frame_task(frame):
        state = states[frame]
        yield from wait_for(state, "result")
        result = state["result"]
        latent = latent_ref[frame].astype(bf16).astype(f32)
        gram = result[3 * ROWS_T + 8 : 3 * ROWS_T + 8 + channels]
        variance = jnp.maximum(jnp.sum(latent * gram, 0, keepdims=True), 0.0) + EPS
        rate = lax.rsqrt(variance)
        yield
        spread = variance * rate
        scaled = latent * rate

        def norm(index):
            start = ROWS_T + 8 + index * ROWS_T
            place = ROWS_T + 8 + index * (ROWS_T + 8)
            terms = rate * result[start : start + ROWS_T] + offset(place, ROWS_T)
            terms = terms.reshape(channels, HEADS, spatial) * scaled[:, None, :]
            total = jnp.sum(terms, 0) + offset(place + ROWS_T, 8)
            return lax.rsqrt(jnp.maximum(total, 0.0) + EPS)

        key_rate = norm(0)
        yield
        query_rate = norm(1) * rate
        yield
        point = (rate * result[ROWS_T : ROWS_T + 8] + offset(ROWS_T, 8)) * key_rate
        point_high = point.astype(bf16).astype(f32)
        spread_high = spread.astype(bf16).astype(f32)
        ends = jnp.where(row == 1, spread - spread_high, jnp.where(row < 3, spread_high, 0.0))
        source = stack(twice(frame), stack(ends, blank).astype(bf16))
        state.update(
            terms=lambda start: rate * result[start : start + channels] + offset(start, channels),
            key_rate=key_rate,
            query_rate=query_rate,
            point=(point_high, point - point_high),
            right=on_diagonal(source, source),
            rows=stack(scaled, ones, blank).astype(bf16),
            averages=[],
        )

    def pair_task(frame, pair):
        state = states[frame]
        heads = (2 * pair, 2 * pair + 1)
        yield from wait_for(state, "rows")
        left = []
        for head in heads:
            own = state["terms"](head * channels) * state["key_rate"][head : head + 1]
            high, low = (part[head : head + 1] for part in state["point"])
            own_point = jnp.where(row < 2, high, jnp.where(row == 2, low, 0.0))
            left += [*halves(own), stack(own_point, blank).astype(bf16)]
        left = stack(*left).T
        yield
        score = dot(left, state["right"])
        yield from pause(lags[1])
        pace = beside(*(state["query_rate"][head : head + 1] for head in heads))
        weight = jnp.exp2(score * pace).astype(bf16)
        yield
        mixed = dot(state["rows"], weight)
        yield from pause(lags[2])
        share = 1.0 / mixed[channels : channels + 8]
        mixed = (mixed[:channels].reshape(-1, 8, 2 * spatial) * share[None]).reshape(channels, -1)
        state["averages"] += [mixed[:, :spatial], mixed[:, spatial:]]
        if pair == HEADS // 2 - 1:
            latent = latent_ref[frame].astype(bf16).astype(f32)
            token = stack(
                *state["averages"], latent, latent, blank, blank, blank, ones, *[blank] * 8
            )
            token_ref[frame] = token.astype(bf16).T

    def tasks():
        for frame in range(-2, frames):
            ahead = frame + 2
            if ahead < frames:
                if ahead % 2 == 0:
                    yield couple_task(ahead)
                yield frame_task(ahead)
            if frame >= 0:
                yield from (pair_task(frame, pair) for pair in range(HEADS // 2))

    interleave(tasks())


def time_kernel(lags, fused, *refs):
    step_ref, token_ref, packed_ref, square_ref, shift_ref, *refs = refs
    if fused:
        latent_ref, noise_ref, *rate_refs, increment_ref, sent_ref = refs[:7]
    else:
        result_ref = refs[0]
    predicted_ref = refs[-1]
    bf16 = jnp.bfloat16
    f32 = jnp.float32
    frames, positions, width = token_ref.shape
    chunk = 8
    rows = frames * chunk
    size = math.gcd(positions, 2 * chunk)
    parts = size // chunk
    groups = positions // size
    count = parts * rows
    keep = (row_of((rows, 2 * rows)) % chunk) == (lane_of((rows, 2 * rows)) % chunk)
    ones = jnp.ones((8, rows), f32)
    row = row_of((16, count))
    states = [{} for group in range(groups)]

    def group_task(group):
        state = states[group]
        tokens = token_ref[:, group * size : (group + 1) * size, :].astype(f32)
        tokens = tokens.reshape(frames, parts, chunk, width)
        tokens = beside(
            *(tokens[:, part].reshape(rows, width).astype(bf16).T for part in range(parts))
        )
        yield
        squares = dot(square_ref[:ATT, :WIDE], tokens)
        yield from pause(lags[0])
        variance = jnp.sum(tokens[:ATT].astype(f32) * squares, 0, keepdims=True)
        variance = jnp.maximum(variance, 0.0) + EPS
        pace = lax.rsqrt(variance)
        spread = variance * pace
        spread_high = spread.astype(bf16).astype(f32)
        yield
        ends = jnp.where(row == 1, spread - spread_high, jnp.where(row < 3, spread_high, 0.0))
        state.update(
            tokens=tokens, pace=pace, floor=(HD * EPS) * variance, outputs={},
            entry=stack(tokens[:ZERO], ends.astype(bf16), tokens[ZERO + 16 :]),
        )

    def project_task(group, pair):
        state = states[group]
        yield from wait_for(state, "entry")
        starts = [which * INNER + pair * 2 * HD for which in range(3)]
        packed = [dot(packed_ref[start : start + 2 * HD], state["entry"]) for start in starts]
        yield from pause(lags[1])
        state["packed", pair] = packed

    def pair_task(group, pair, part):
        state = states[group]
        own = slice(part * rows, (part + 1) * rows)
        yield from wait_for(state, ("packed", pair))
        packed = [values[:, own] for values in state["packed", pair]]

        def unit(which, head, gain):
            values = packed[which][head * HD : (head + 1) * HD]
            size = lax.rsqrt(jnp.sum(values * values, 0, keepdims=True) + state["floor"][:, own])
            return values * (size * gain if gain else size)

        left = stack(unit(1, 0, None), unit(1, 1, None), jnp.zeros((16, rows), f32)).astype(bf16).T
        yield
        right = on_diagonal(unit(0, 0, UNIT), unit(0, 1, UNIT))
        right = stack(right, jnp.zeros((16, 2 * rows), f32)).astype(bf16)
        score = dot(left, right)
        yield from pause(lags[2])
        weight = jnp.where(keep, jnp.exp2(score), 0.0).astype(bf16)
        yield
        value = packed[2] * state["pace"][:, own]
        value = beside(stack(value[:HD], ones), stack(value[HD:], ones)).astype(bf16)
        mixed = dot(value, on_diagonal(weight[:, :rows], weight[:, rows:]))
        yield from pause(lags[3])
        share = 1.0 / mixed[HD:]
        mixed = (mixed[:HD].reshape(-1, 8, 2 * rows) * share[None]).reshape(HD, 2 * rows)
        state["outputs"][part, pair] = stack(mixed[:, :rows], mixed[:, rows:])

    def last_task(group):
        state = states[group]
        while len(state.get("outputs", ())) < parts * HEADS // 2:
            yield
        attended = beside(
            *(
                stack(*(state["outputs"][part, pair] for pair in range(HEADS // 2)))
                for part in range(parts)
            )
        )
        exact = stack(state["tokens"][:ATT].astype(f32), attended[BASE:], attended[:BASE])
        inputs = exact.astype(bf16)
        yield
        blocks = []
        for start in range(0, exact.shape[0], WIDE):
            blocks.append(dot(square_ref[start : start + WIDE, start:], inputs[start:]))
            yield
        yield from pause(lags[4])
        total = 0.0
        for index, block in enumerate(blocks):
            terms = block * exact[index * WIDE : (index + 1) * WIDE]
            total = total + jnp.sum(terms.reshape(-1, 8, count), 0)
        rate = lax.rsqrt(jnp.maximum(jnp.sum(total, 0, keepdims=True), 0.0) + EPS)
        yield
        predicted = blocks[0][ZERO : ZERO + CHANNELS] * rate
        for part in range(parts):
            index = (pl.program_id(0) * groups + group) * parts + part
            predicted_ref[index] = predicted[:, part * rows : (part + 1) * rows]

    def tasks():
        yield group_task(0)
        for group in range(groups):
            for pair in range(HEADS // 2):
                yield project_task(group, pair)
                if pair == 1 and group + 1 < groups:
                    yield group_task(group + 1)
                yield from (pair_task(group, pair, part) for part in range(parts))
            yield last_task(group)

    interleave(tasks())

    @pl.when(pl.program_id(0) == pl.num_programs(0) - 1)
    def _():
        if fused:
            timestep = step_ref[0]
            rate_state, rate_denoise, rate_noise = (ref[timestep] for ref in rate_refs)
            rate_state = rate_state + jnp.where(timestep == 0, 1.0, 0.0)
        chunks = [predicted_ref[index] for index in range(predicted_ref.shape[0])]
        block = lane_of(chunks[0].shape) // chunk
        if len(chunks) == frames and frames & (frames - 1) == 0:
            step = 1
            while step < frames:
                moved = (block & step) != 0
                for low in range(frames):
                    if low & step == 0:
                        first, second = chunks[low], chunks[low + step]
                        chunks[low] = jnp.where(moved, pltpu.roll(second, step * chunk, 1), first)
                        chunks[low + step] = jnp.where(
                            moved, second, pltpu.roll(first, rows - step * chunk, 1)
                        )
                step *= 2
            turned_of = chunks.__getitem__
        else:
            def turned_of(frame):
                return beside(*(part[:, frame * chunk : (frame + 1) * chunk] for part in chunks))
        for frame in range(frames):
            turned = turned_of(frame)
            turned = turned + shift_ref[:, : turned.shape[1]]
            if fused:
                turned = (
                    rate_state * latent_ref[frame]
                    + rate_denoise * turned
                    + rate_noise * noise_ref[frame]
                )
                increment_ref[frame] = turned
                sent_ref[frame] = turned.astype(jnp.bfloat16)
            else:
                result_ref[frame] = turned


def whole(array):
    zeros = (0,) * array.ndim
    return pl.BlockSpec(array.shape, lambda *_: zeros, pipeline_mode=pl.Buffered(1))


def fold(own, modulation, embed_weight, space_input, space_output, time_input, time_output, final_weight):
    features = modulation.shape[2]
    shapes = [
        ((ROWS_AA, 2 * CHANNELS), jnp.bfloat16),
        ((3 * (ROWS_T + 8), LANES), jnp.float32),
        ((3 * INNER, WIDE), jnp.bfloat16),
        ((BASE + WIDE, BASE + WIDE), jnp.bfloat16),
        ((CHANNELS, LANES), jnp.float32),
    ]
    weights = (embed_weight, space_input, space_output, time_input, time_output, final_weight)
    return pl.pallas_call(
        fold_kernel,
        out_shape=[jax.ShapeDtypeStruct(*shape) for shape in shapes],
        grid_spec=pltpu.PrefetchScalarGridSpec(
            num_scalar_prefetch=1,
            grid=(1,),
            in_specs=[
                pl.BlockSpec(
                    (None,) + modulation.shape[1:],
                    lambda step, own: (own[0], 0, 0),
                    pipeline_mode=pl.Buffered(1),
                )
            ]
            + [whole(weight) for weight in weights],
            out_specs=[
                pl.BlockSpec(shape, lambda *_: (0, 0), pipeline_mode=pl.Buffered(1))
                for shape, kind in shapes
            ],
            scratch_shapes=[pltpu.VMEM((BASE + WIDE, features), jnp.bfloat16)],
        ),
        compiler_params=pltpu.CompilerParams(vmem_limit_bytes=60 * 1024 * 1024),
        name="fold",
    )(own, modulation, *weights)


def space_block(latent, first, offset):
    frames, channels, spatial = latent.shape
    step_frames = math.gcd(frames, 16)
    return pl.pallas_call(
        functools.partial(space_kernel, (2, 3, 2)),
        out_shape=jax.ShapeDtypeStruct((frames, spatial, WIDE), jnp.bfloat16),
        grid=(frames // step_frames,),
        in_specs=[
            pl.BlockSpec((step_frames, channels, spatial), lambda step: (step, 0, 0)),
            whole(first),
            whole(offset),
        ],
        out_specs=pl.BlockSpec((step_frames, spatial, WIDE), lambda step: (step, 0, 0)),
        compiler_params=pltpu.CompilerParams(vmem_limit_bytes=60 * 1024 * 1024),
        name="space_block",
    )(latent, first, offset)


def time_block(own, tokens, packed, square, shift, fused=()):
    frames, positions, width = tokens.shape
    step_positions = math.gcd(positions, 64)
    shape = (frames, CHANNELS, positions)
    kinds = [jnp.float32] + [jnp.bfloat16] * bool(fused)
    return pl.pallas_call(
        functools.partial(time_kernel, (2, 2, 3, 2, 1), bool(fused)),
        out_shape=[jax.ShapeDtypeStruct(shape, kind) for kind in kinds],
        grid_spec=pltpu.PrefetchScalarGridSpec(
            num_scalar_prefetch=1,
            grid=(positions // step_positions,),
            in_specs=[
                pl.BlockSpec((frames, step_positions, width), lambda step, own: (0, step, 0)),
                whole(packed),
                whole(square),
                whole(shift),
            ]
            + [
                whole(array) if array.ndim > 1 else pl.BlockSpec(memory_space=pltpu.SMEM)
                for array in fused
            ],
            out_specs=[
                pl.BlockSpec(shape, lambda step, own: (0, 0, 0), pipeline_mode=pl.Buffered(1))
                for kind in kinds
            ],
            scratch_shapes=[pltpu.VMEM((positions // 8, CHANNELS, frames * 8), jnp.float32)],
        ),
        compiler_params=pltpu.CompilerParams(vmem_limit_bytes=60 * 1024 * 1024),
        name="time_block",
    )(own, tokens, packed, square, shift, *fused)


def carry_kernel(
    last, groups, sent_ref, increment_ref, latent_ref, out_ref,
    part_ref, total_ref, plane_ref, early_ref, stage_ref, before_ref,
    part_send, part_recv, plane_send, plane_recv, stage_send, stage_recv,
):
    quarter = part_ref.shape[1]
    own = lax.axis_index("tok")
    timestep = own // groups
    plane, seat = timestep // SIDE, timestep % SIDE

    def device(plane, seat):
        return {"tok": (plane * SIDE + seat) * groups + own % groups}

    def seat_after(hop):
        return (seat + hop) % SIDE

    barrier = pltpu.get_barrier_semaphore()
    for hop in range(1, SIDE):
        for target in (device(plane, seat_after(hop)), device((plane + hop) % SIDE, seat)):
            pl.semaphore_signal(
                barrier, inc=1, device_id=target, device_id_type=pl.DeviceIdType.MESH
            )
    pl.semaphore_wait(barrier, 2 * (SIDE - 1))

    def copy(source, target, send, receive, to):
        return pltpu.make_async_remote_copy(
            src_ref=source,
            dst_ref=target,
            send_sem=send,
            recv_sem=receive,
            device_id=to,
            device_id_type=pl.DeviceIdType.MESH,
        )

    def rows_of(index):
        return pl.ds(pl.multiple_of(index * quarter, quarter), quarter)

    parts = []
    for hop in range(1, SIDE):
        seat_to = seat_after(hop)
        parts.append(
            copy(
                sent_ref.at[rows_of(seat_to)], part_ref.at[hop - 1],
                part_send.at[hop - 1], part_recv.at[hop - 1], device(plane, seat_to),
            )
        )
        parts[-1].start()
    held = [sent_ref[rows_of(seat)].astype(jnp.float32)]
    for hop in range(1, SIDE):
        parts[hop - 1].wait_recv()
        held.append(part_ref[hop - 1].astype(jnp.float32))
    total_ref[...] = functools.reduce(jnp.add, held).astype(jnp.bfloat16)
    planes = [
        copy(
            total_ref, plane_ref.at[hop - 1], plane_send.at[hop - 1], plane_recv.at[hop - 1],
            device((plane + hop) % SIDE, seat),
        )
        for hop in range(1, SIDE)
    ]
    for hop in range(1, SIDE):
        pl.when(plane + hop < SIDE)(planes[hop - 1].start)

    def earlier_seats(limit):
        total = jnp.zeros_like(held[0])
        for hop in range(SIDE):
            total = total + jnp.where((seat + SIDE - hop) % SIDE < limit, held[hop], 0.0)
        return total

    early_ref[...] = jnp.zeros_like(early_ref)
    for hop in range(1, SIDE):

        @pl.when(plane >= hop)
        def _(hop=hop):
            planes[hop - 1].wait_recv()
            early_ref[...] += plane_ref[hop - 1].astype(jnp.float32)

    early = early_ref[...]
    stages = []
    for hop in range(1, SIDE):
        seat_to = seat_after(hop)
        stage_ref[hop - 1] = early + earlier_seats(seat_to)
        stages.append(
            copy(
                stage_ref.at[hop - 1], before_ref.at[rows_of(seat)],
                stage_send.at[hop - 1], stage_recv.at[hop - 1], device(plane, seat_to),
            )
        )
        stages[-1].start()
    own_rows = rows_of(seat)

    def settle(rows, before):
        if last:
            out_ref[rows] = before + increment_ref[rows]
        else:
            out_ref[rows] = jnp.where(timestep == 0, latent_ref[rows], before)

    settle(own_rows, early + earlier_seats(seat))
    for hop in range(1, SIDE):
        stages[hop - 1].wait_recv()
        rows = rows_of((seat + SIDE - hop) % SIDE)
        settle(rows, before_ref[rows])
    for hop in range(1, SIDE):
        parts[hop - 1].wait_send()
        pl.when(plane + hop < SIDE)(planes[hop - 1].wait_send)
        stages[hop - 1].wait_send()


def carried_kernel(last, groups, sent, increment, latent):
    rows, lanes = sent.shape
    quarter = rows // SIDE
    hops = SIDE - 1
    vmem = pl.BlockSpec(memory_space=pltpu.VMEM)
    return pl.pallas_call(
        functools.partial(carry_kernel, last, groups),
        out_shape=jax.ShapeDtypeStruct((rows, lanes), jnp.float32),
        in_specs=[vmem] * 3,
        out_specs=vmem,
        scratch_shapes=[
            pltpu.VMEM((hops, quarter, lanes), jnp.bfloat16),
            pltpu.VMEM((quarter, lanes), jnp.bfloat16),
            pltpu.VMEM((hops, quarter, lanes), jnp.bfloat16),
            pltpu.VMEM((quarter, lanes), jnp.float32),
            pltpu.VMEM((hops, quarter, lanes), jnp.float32),
            pltpu.VMEM((rows, lanes), jnp.float32),
        ]
        + [pltpu.SemaphoreType.DMA((hops,))] * 6,
        compiler_params=pltpu.CompilerParams(collective_id=int(last), has_side_effects=True),
        name="carry_last" if last else "carry",
    )(sent, increment, latent)


def carried_in(last, groups, same_block, timestep, sent, increment, latent):
    rows = sent.size // LANES
    if sent.shape[-1] == LANES and rows % (SIDE * 16) == 0:
        flat = [array.reshape(rows, LANES) for array in (sent, increment, latent)]
        return carried_kernel(last, groups, *flat).reshape(latent.shape)
    gathered = lax.all_gather(
        sent, "tok", axis_index_groups=same_block if groups > 1 else None
    )
    earlier = (jnp.arange(P_SIZE) < timestep)[:, None, None, None]
    before = jnp.sum(jnp.where(earlier, gathered.astype(jnp.float32), 0.0), axis=0)
    return before + increment if last else jnp.where(timestep == 0, latent, before)


def body(
    initial_guess,
    noise_draws,
    drift_state,
    drift_denoise,
    noise_scale,
    modulation,
    embed_weight,
    space_input,
    space_output,
    time_input,
    time_output,
    final_weight,
):
    devices = lax.axis_size("tok")
    own_index = lax.axis_index("tok")
    groups = devices // P_SIZE
    timestep = own_index // groups
    own = jnp.reshape(timestep, (1,)).astype(jnp.int32)
    rates = (drift_state, drift_denoise, noise_scale)
    same_step = [[step * groups + block for block in range(groups)] for step in range(P_SIZE)]
    same_block = [[step * groups + block for step in range(P_SIZE)] for block in range(groups)]
    first, offset, packed, square, shift = fold(
        own, modulation, embed_weight, space_input.T, space_output, time_input.T, time_output,
        final_weight.T,
    )
    latent = initial_guess
    for iteration in range(ITERS):
        tokens = space_block(latent, first, offset)
        if groups == 1:
            increment, sent = time_block(
                own, tokens, packed, square, shift, (latent, noise_draws) + rates
            )
        else:
            tokens = lax.all_to_all(
                tokens, "tok", split_axis=1, concat_axis=0, axis_index_groups=same_step, tiled=True
            )
            (predicted,) = time_block(own, tokens, packed, square, shift)
            predicted = lax.all_to_all(
                predicted, "tok", split_axis=0, concat_axis=2, axis_index_groups=same_step, tiled=True
            )
            rate_state, rate_denoise, rate_noise = (
                lax.dynamic_index_in_dim(rate, timestep, 0, keepdims=False) for rate in rates
            )
            rate_state = rate_state + jnp.where(timestep == 0, 1.0, 0.0)
            increment = rate_state * latent + rate_denoise * predicted + rate_noise * noise_draws
            sent = increment.astype(jnp.bfloat16)
        latent = carried_in(
            iteration == ITERS - 1, groups, same_block, timestep, sent, increment, latent
        )
    return latent


def solution(mesh):
    placed = (
        P(("group", "tok"), None, None),
        P(("group", "tok"), None, None),
        P(),
        P(),
        P(),
        P(),
        P(),
        P(),
        P(),
        P(),
        P(),
        P(),
    )
    return jax.shard_map(
        body, mesh=mesh, in_specs=placed, out_specs=P(("group", "tok"), None, None), check_vma=False
    )
```

```python
import functools
import math

import jax
import jax.numpy as jnp
from jax import lax
from jax.experimental import pallas as pl
from jax.experimental.pallas import tpu as pltpu
from jax.sharding import PartitionSpec as P

HEADS = 8
HD = 72
P_SIZE = 16
ITERS = 2
LANES = 128
INNER = HEADS * HD
SIDE = math.isqrt(P_SIZE)
CHUNK = 8
CARRIED = 2
SPACE_LAGS = (2, 8, 6)
TIME_LAGS = (4, 8, 10, 8, 2, 48)
EPS = 1e-06
CHANNELS = 16
WIDE = 2 * LANES
ROWS_T = HEADS * CHANNELS
ROWS_AA = 3 * ROWS_T + 32
BASE = 512
TAIL = INNER - BASE
LAT, DUP, ZERO, ONE, ATT = 128, 144, 160, 184, 192
SCALE = HD**-0.5 * math.log2(math.e)
UNIT = HD**0.5 * math.log2(math.e)


def dot_rows(values, weight_rows, precision=None):
    return lax.dot_general(
        values,
        weight_rows,
        (((1,), (1,)), ((), ())),
        preferred_element_type=jnp.float32,
        precision=precision,
    )


def dot(values, weights):
    return jnp.dot(values, weights, preferred_element_type=jnp.float32)


def halves(values):
    high = values.astype(jnp.bfloat16)
    return high, (values - high.astype(jnp.float32)).astype(jnp.bfloat16)


def lane_of(shape):
    return lax.broadcasted_iota(jnp.int32, shape, len(shape) - 1)


def row_of(shape):
    return lax.broadcasted_iota(jnp.int32, shape, 0)


def centred(rows):
    return rows - jnp.mean(rows, -1, keepdims=True)


def by_head(rows, order):
    count, width = rows.shape
    if order == "hc":
        spread = jnp.concatenate([rows] * HEADS, axis=0)
        head = row_of(spread.shape) // count
    else:
        spread = jnp.broadcast_to(rows[:, None, :], (count, HEADS, width)).reshape(-1, width)
        head = row_of(spread.shape) % HEADS
    return jnp.where(lane_of(spread.shape) // HD == head, spread, 0.0)


def fold_kernel(
    step_ref, table_ref, embed_ref, space_in_ref, space_out_ref, time_in_ref, time_out_ref, final_ref,
    first_ref, offset_ref, packed_ref, square_ref, shift_ref, lines_ref,
):
    def table(row):
        return table_ref[row : row + 1, :]

    def zeros(rows, width=None):
        return jnp.zeros((rows, width or table_ref.shape[1]), jnp.float32)

    highest = lax.Precision.HIGHEST
    features = table_ref.shape[1]
    embed = centred(embed_ref[...].astype(jnp.float32))
    lines = embed * (1.0 + table(1))
    shift = jnp.concatenate([table(0), zeros(7)], axis=0)
    high, low = halves(lines)
    shift_high, shift_low = halves(shift)
    tail = jnp.concatenate([shift_high.astype(jnp.float32), shift_low.astype(jnp.float32)], axis=0)
    folded = dot_rows(
        jnp.concatenate([high, low, tail.astype(jnp.bfloat16)], axis=0), space_in_ref[...]
    )
    lat = folded[:CHANNELS] + folded[CHANNELS : 2 * CHANNELS]
    const = folded[2 * CHANNELS : 2 * CHANNELS + 8] + folded[2 * CHANNELS + 8 :]

    def part(values, which):
        return values[:, which * INNER : (which + 1) * INNER]

    query, key, value = (part(lat, which) for which in range(3))
    query_c, key_c, value_c = (part(const, which)[:1] for which in range(3))
    key_side = jnp.concatenate([key, key, key_c, zeros(7, INNER)], axis=0)
    query_side = jnp.concatenate([query, query, query_c, zeros(7, INNER)], axis=0)
    scores = dot_rows(
        jnp.concatenate([by_head(query, "hc"), by_head(query_c, "ch")], axis=0) * SCALE,
        key_side, highest,
    )
    key_square = dot_rows(
        jnp.concatenate([by_head(key, "ch"), by_head(key_c, "ch")], axis=0) * (1.0 / HD),
        key_side, highest,
    )
    query_square = dot_rows(
        jnp.concatenate([by_head(query, "ch"), by_head(query_c, "ch")], axis=0) * (1.0 / HD),
        query_side, highest,
    )
    gram = dot_rows(embed, jnp.concatenate([embed, embed, zeros(8)], axis=0), highest) * (
        1.0 / features
    )
    first = jnp.concatenate(
        [scores, key_square[:ROWS_T], query_square[:ROWS_T], gram, zeros(8, 2 * CHANNELS + 8)],
        axis=0,
    )
    high, low = halves(first)
    upper = lane_of(first.shape) < CHANNELS
    chosen = jnp.where(upper, high.astype(jnp.float32), low.astype(jnp.float32))
    first_ref[...] = chosen[:, : 2 * CHANNELS].astype(jnp.bfloat16)
    point = 2 * CHANNELS
    offset_ref[: ROWS_T + 8] = jnp.broadcast_to(scores[:, point : point + 1], (ROWS_T + 8, LANES))
    for index, square in enumerate((key_square, query_square)):
        start = ROWS_T + 8 + index * (ROWS_T + 8)
        offset_ref[start : start + ROWS_T] = jnp.broadcast_to(
            2.0 * square[:ROWS_T, point : point + 1], (ROWS_T, LANES)
        )
        offset_ref[start + ROWS_T : start + ROWS_T + 8] = jnp.broadcast_to(
            square[ROWS_T:, point : point + 1], (8, LANES)
        )

    value_high, value_low = halves(by_head(value, "hc"))
    const_high, const_low = halves(jnp.concatenate([value_c, zeros(7, INNER)], axis=0))
    tail = jnp.concatenate([const_high.astype(jnp.float32), const_low.astype(jnp.float32)], axis=0)
    mixed = dot(
        jnp.concatenate([value_high, value_low, tail.astype(jnp.bfloat16)], axis=0),
        space_out_ref[...],
    )
    gate = table(2)
    attended = centred(gate * (mixed[:ROWS_T] + mixed[ROWS_T : 2 * ROWS_T]))
    point = centred(gate * (mixed[2 * ROWS_T : 2 * ROWS_T + 8] + mixed[2 * ROWS_T + 8 :]))

    scaled = 1.0 + table(4)
    lat_high, lat_low = halves(embed * scaled)
    ends = jnp.concatenate([table(3), point[:1] * scaled, zeros(6)], axis=0)
    ends_high, ends_low = halves(ends)
    tail = jnp.concatenate([ends_high.astype(jnp.float32), ends_low.astype(jnp.float32)], axis=0)
    rows = jnp.concatenate(
        [(attended * scaled).astype(jnp.bfloat16), lat_high, lat_low, tail.astype(jnp.bfloat16)],
        axis=0,
    )

    def settle(columns):
        lat = columns[LAT:DUP] + columns[DUP : DUP + CHANNELS]
        lat_high = lat.astype(jnp.bfloat16).astype(jnp.float32)
        ends = columns[DUP + CHANNELS : DUP + CHANNELS + 8] + columns[DUP + CHANNELS + 8 :]
        ends_high = ends.astype(jnp.bfloat16).astype(jnp.float32)
        ends_low = ends - ends_high
        width = columns.shape[1]
        return jnp.concatenate(
            [
                columns[:LAT], lat_high, lat - lat_high,
                ends_high[:1], ends_high[:1], ends_low[:1], zeros(ONE - ZERO - 3, width),
                ends_high[1:2], ends_low[1:2], zeros(WIDE - ONE - 2, width),
            ],
            axis=0,
        ).astype(jnp.bfloat16)

    for which in range(3):
        own = slice(which * INNER, (which + 1) * INNER)
        packed_ref[own] = settle(dot_rows(rows, time_in_ref[own, :])).T

    gate = table(5)
    lat_high, lat_low = halves(embed)
    point_high, point_low = halves(point[:1])
    lines_ref[:LAT] = attended.astype(jnp.bfloat16)
    lines_ref[LAT:DUP] = lat_high
    lines_ref[DUP:ZERO] = lat_low
    lines_ref[ZERO:ATT] = jnp.concatenate(
        [
            zeros(ONE - ZERO), point_high.astype(jnp.float32), point_low.astype(jnp.float32),
            zeros(ATT - ONE - 2),
        ],
        axis=0,
    ).astype(jnp.bfloat16)
    lines_ref[ATT:WIDE] = centred(gate * time_out_ref[BASE:].astype(jnp.float32)).astype(jnp.bfloat16)
    for start in range(0, BASE, LANES):
        lines_ref[WIDE + start : WIDE + start + LANES] = centred(
            gate * time_out_ref[start : start + LANES].astype(jnp.float32)
        ).astype(jnp.bfloat16)
    final = final_ref[...].astype(jnp.float32)
    shift_ref[...] = jnp.broadcast_to(
        jnp.sum(final * table(6), -1, keepdims=True), (CHANNELS, LANES)
    )
    base = jnp.concatenate(
        [
            lines_ref[:ZERO],
            (final * (1.0 + table(7))).astype(jnp.bfloat16),
            lines_ref[ZERO + CHANNELS : WIDE],
        ],
        axis=0,
    )
    line = row_of((WIDE, 1))
    plain = (line >= ZERO) & (line < ZERO + CHANNELS)
    tiles = lines_ref.shape[0] // WIDE
    for column in range(tiles):
        other = lines_ref[column * WIDE : (column + 1) * WIDE] if column else base
        for row in range(column, tiles):
            block = dot_rows(other, lines_ref[row * WIDE : (row + 1) * WIDE])
            block = block * ((1.0 if row == column else 2.0) / features) if column else (
                block * jnp.where(plain, 1.0, (1.0 if row == column else 2.0) / features)
            )
            square_ref[column * WIDE : (column + 1) * WIDE, row * WIDE : (row + 1) * WIDE] = (
                block.astype(jnp.bfloat16)
            )


def stack(*parts):
    return jnp.concatenate(parts, axis=0)


def beside(*parts):
    return jnp.concatenate(parts, axis=1)


def on_diagonal(first, second):
    blank = jnp.zeros_like(first)
    return stack(beside(first, blank), beside(blank, second))


def interleave(tasks):
    tasks, running = list(tasks), []
    while tasks or running:
        running += [tasks.pop(0)] if tasks else []
        running = [task for task in running if next(task, tasks) is not tasks]


def pause(turns):
    for turn in range(turns):
        yield


def wait_for(state, key):
    while key not in state:
        yield


def space_kernel(lags, latent_ref, first_ref, offset_ref, token_ref):
    frames, channels, spatial = latent_ref.shape
    bf16 = jnp.bfloat16
    f32 = jnp.float32
    row = row_of((8, spatial))
    blank = jnp.zeros((8, spatial), f32)
    ones = jnp.ones((8, spatial), f32)
    states = [{} for frame in range(frames)]

    def offset(start, rows):
        return offset_ref[start : start + rows]

    def twice(frame):
        latent = latent_ref[frame].astype(bf16)
        return stack(latent, latent)

    def couple_task(frame):
        own = range(frame, min(frame + 2, frames))
        product = dot(first_ref[...], beside(*(twice(index) for index in own)))
        yield from pause(lags[0])
        for place, index in enumerate(own):
            states[index]["result"] = product[:, place * spatial : (place + 1) * spatial]

    def frame_task(frame):
        state = states[frame]
        yield from wait_for(state, "result")
        result = state["result"]
        latent = latent_ref[frame].astype(bf16).astype(f32)
        gram = result[3 * ROWS_T + 8 : 3 * ROWS_T + 8 + channels]
        variance = jnp.maximum(jnp.sum(latent * gram, 0, keepdims=True), 0.0) + EPS
        rate = lax.rsqrt(variance)
        yield
        spread = variance * rate
        scaled = latent * rate

        def norm(index):
            start = ROWS_T + 8 + index * ROWS_T
            place = ROWS_T + 8 + index * (ROWS_T + 8)
            terms = rate * result[start : start + ROWS_T] + offset(place, ROWS_T)
            terms = terms.reshape(channels, HEADS, spatial) * scaled[:, None, :]
            total = jnp.sum(terms, 0) + offset(place + ROWS_T, 8)
            return lax.rsqrt(jnp.maximum(total, 0.0) + EPS)

        key_rate = norm(0)
        yield
        query_rate = norm(1) * rate
        yield
        point = (rate * result[ROWS_T : ROWS_T + 8] + offset(ROWS_T, 8)) * key_rate
        point_high = point.astype(bf16).astype(f32)
        spread_high = spread.astype(bf16).astype(f32)
        ends = jnp.where(row == 1, spread - spread_high, jnp.where(row < 3, spread_high, 0.0))
        source = stack(twice(frame), stack(ends, blank).astype(bf16))
        state.update(
            terms=lambda start: rate * result[start : start + channels] + offset(start, channels),
            key_rate=key_rate,
            query_rate=query_rate,
            point=(point_high, point - point_high),
            right=on_diagonal(source, source),
            rows=stack(scaled, ones, blank).astype(bf16),
            averages=[],
        )

    def pair_task(frame, pair):
        state = states[frame]
        heads = (2 * pair, 2 * pair + 1)
        yield from wait_for(state, "rows")
        left = []
        for head in heads:
            own = state["terms"](head * channels) * state["key_rate"][head : head + 1]
            high, low = (part[head : head + 1] for part in state["point"])
            own_point = jnp.where(row < 2, high, jnp.where(row == 2, low, 0.0))
            left += [*halves(own), stack(own_point, blank).astype(bf16)]
        left = stack(*left).T
        yield
        score = dot(left, state["right"])
        yield from pause(lags[1])
        pace = beside(*(state["query_rate"][head : head + 1] for head in heads))
        weight = jnp.exp2(score * pace).astype(bf16)
        yield
        mixed = dot(state["rows"], weight)
        yield from pause(lags[2])
        share = 1.0 / mixed[channels : channels + 8]
        mixed = (mixed[:channels].reshape(-1, 8, 2 * spatial) * share[None]).reshape(channels, -1)
        state["averages"] += [mixed[:, :spatial], mixed[:, spatial:]]
        if pair == HEADS // 2 - 1:
            latent = latent_ref[frame].astype(bf16).astype(f32)
            token = stack(
                *state["averages"], latent, latent, blank, blank, blank, ones, *[blank] * 8
            )
            token_ref[frame] = token.astype(bf16).T

    def tasks():
        for frame in range(-2, frames):
            ahead = frame + 2
            if ahead < frames:
                if ahead % 2 == 0:
                    yield couple_task(ahead)
                yield frame_task(ahead)
            if frame >= 0:
                yield from (pair_task(frame, pair) for pair in range(HEADS // 2))

    interleave(tasks())


def regrid(chunks):
    count, (_, lanes) = len(chunks), chunks[0].shape
    block = lane_of(chunks[0].shape) // CHUNK
    if count * CHUNK != lanes or count & (count - 1):
        return [
            beside(*(part[:, index * CHUNK : (index + 1) * CHUNK] for part in chunks))
            for index in range(lanes // CHUNK)
        ]
    chunks, step = list(chunks), 1
    while step < count:
        moved = (block & step) != 0
        for low in range(count):
            if low & step == 0:
                first, second = chunks[low], chunks[low + step]
                chunks[low] = jnp.where(moved, pltpu.roll(second, step * CHUNK, 1), first)
                chunks[low + step] = jnp.where(
                    moved, second, pltpu.roll(first, lanes - step * CHUNK, 1)
                )
        step *= 2
    return chunks


def time_tasks(lags, token_ref, packed_ref, square_ref, finish, after=lambda group, parts: ()):
    bf16 = jnp.bfloat16
    f32 = jnp.float32
    frames, positions, width = token_ref.shape
    chunk = CHUNK
    rows = frames * chunk
    size = math.gcd(positions, 2 * chunk)
    parts = size // chunk
    groups = positions // size
    count = parts * rows
    keep = (row_of((rows, 2 * rows)) % chunk) == (lane_of((rows, 2 * rows)) % chunk)
    ones = jnp.ones((8, rows), f32)
    row = row_of((16, count))
    states = [{} for group in range(groups)]

    def group_task(group):
        state = states[group]
        tokens = token_ref[:, group * size : (group + 1) * size, :].astype(f32)
        tokens = tokens.reshape(frames, parts, chunk, width)
        tokens = beside(
            *(tokens[:, part].reshape(rows, width).astype(bf16).T for part in range(parts))
        )
        yield
        squares = dot(square_ref[:ATT, :WIDE], tokens)
        yield from pause(lags[0])
        variance = jnp.sum(tokens[:ATT].astype(f32) * squares, 0, keepdims=True)
        variance = jnp.maximum(variance, 0.0) + EPS
        pace = lax.rsqrt(variance)
        spread = variance * pace
        spread_high = spread.astype(bf16).astype(f32)
        yield
        ends = jnp.where(row == 1, spread - spread_high, jnp.where(row < 3, spread_high, 0.0))
        state.update(
            tokens=tokens, pace=pace, floor=(HD * EPS) * variance, outputs={},
            entry=stack(tokens[:ZERO], ends.astype(bf16), tokens[ZERO + 16 :]),
        )

    def project_task(group, pair):
        state = states[group]
        yield from wait_for(state, "entry")
        starts = [which * INNER + pair * 2 * HD for which in range(3)]
        packed = [dot(packed_ref[start : start + 2 * HD], state["entry"]) for start in starts]
        yield from pause(lags[1])
        state["packed", pair] = packed

    def pair_task(group, pair, part):
        state = states[group]
        own = slice(part * rows, (part + 1) * rows)
        yield from wait_for(state, ("packed", pair))
        packed = [values[:, own] for values in state["packed", pair]]

        def unit(which, head, gain):
            values = packed[which][head * HD : (head + 1) * HD]
            size = lax.rsqrt(jnp.sum(values * values, 0, keepdims=True) + state["floor"][:, own])
            return values * (size * gain if gain else size)

        left = stack(unit(1, 0, None), unit(1, 1, None), jnp.zeros((16, rows), f32)).astype(bf16).T
        yield
        right = on_diagonal(unit(0, 0, UNIT), unit(0, 1, UNIT))
        right = stack(right, jnp.zeros((16, 2 * rows), f32)).astype(bf16)
        score = dot(left, right)
        yield from pause(lags[2])
        weight = jnp.where(keep, jnp.exp2(score), 0.0).astype(bf16)
        yield
        value = packed[2] * state["pace"][:, own]
        value = beside(stack(value[:HD], ones), stack(value[HD:], ones)).astype(bf16)
        mixed = dot(value, on_diagonal(weight[:, :rows], weight[:, rows:]))
        yield from pause(lags[3])
        share = 1.0 / mixed[HD:]
        mixed = (mixed[:HD].reshape(-1, 8, 2 * rows) * share[None]).reshape(HD, 2 * rows)
        state["outputs"][part, pair] = stack(mixed[:, :rows], mixed[:, rows:])

    def last_task(group):
        state = states[group]
        while len(state.get("outputs", ())) < parts * HEADS // 2:
            yield
        attended = beside(
            *(
                stack(*(state["outputs"][part, pair] for pair in range(HEADS // 2)))
                for part in range(parts)
            )
        )
        exact = stack(state["tokens"][:ATT].astype(f32), attended[BASE:], attended[:BASE])
        inputs = exact.astype(bf16)
        yield
        blocks = []
        for start in range(0, exact.shape[0], WIDE):
            blocks.append(dot(square_ref[start : start + WIDE, start:], inputs[start:]))
            yield
        yield from pause(lags[4])
        total = 0.0
        for index, block in enumerate(blocks):
            terms = block * exact[index * WIDE : (index + 1) * WIDE]
            total = total + jnp.sum(terms.reshape(-1, 8, count), 0)
        rate = lax.rsqrt(jnp.maximum(jnp.sum(total, 0, keepdims=True), 0.0) + EPS)
        yield
        predicted = blocks[0][ZERO : ZERO + CHANNELS] * rate
        for part in range(parts):
            finish(group * parts + part, predicted[:, part * rows : (part + 1) * rows])

    def tasks():
        yield group_task(0)
        for group in range(groups):
            for pair in range(HEADS // 2):
                yield project_task(group, pair)
                if pair == 1 and group + 1 < groups:
                    yield group_task(group + 1)
                yield from (pair_task(group, pair, part) for part in range(parts))
            yield last_task(group)
            yield from after(group, parts)

    return tasks()


def time_kernel(lags, token_ref, packed_ref, square_ref, shift_ref, result_ref):
    chunks = {}
    interleave(time_tasks(lags, token_ref, packed_ref, square_ref, chunks.__setitem__))
    for frame, own in enumerate(regrid([chunks[index] for index in sorted(chunks)])):
        result_ref[frame] = own + shift_ref[:, : own.shape[1]]


def step_kernel(
    lags, last, token_ref, packed_ref, square_ref, shift_ref, latent_ref, noise_ref,
    state_ref, denoise_ref, scale_ref, out_ref,
    base_ref, increment_ref, sent_ref, part_ref, total_ref, plane_ref,
    part_send, part_recv, plane_send, plane_recv,
):
    f32 = jnp.float32
    frames = latent_ref.shape[0]
    timestep = lax.axis_index("tok")
    plane, seat = timestep // SIDE, timestep % SIDE
    hops = range(1, SIDE)

    def in_plane(hop):
        return {"tok": plane * SIDE + (seat + hop) % SIDE}

    def in_seat(hop):
        return {"tok": (plane + hop) % SIDE * SIDE + seat}

    barrier = pltpu.get_barrier_semaphore()
    for hop in hops:
        for target in (in_plane(hop), in_seat(hop)):
            pl.semaphore_signal(
                barrier, inc=1, device_id=target, device_id_type=pl.DeviceIdType.MESH
            )

    rate_denoise = denoise_ref[timestep]
    rate_state = state_ref[timestep] + jnp.where(timestep == 0, 1.0, 0.0)
    rate_noise = scale_ref[timestep]
    base = [
        rate_state * latent_ref[frame] + rate_noise * noise_ref[frame] + rate_denoise * shift_ref[...]
        for frame in range(frames)
    ]
    for index, own in enumerate(regrid(base)):
        base_ref[index] = own
    pl.semaphore_wait(barrier, 2 * (SIDE - 1))

    done = set()

    def finish(index, predicted):
        increment = base_ref[index] + rate_denoise * predicted
        increment_ref[index] = increment
        sent_ref[index] = increment.astype(jnp.bfloat16)
        done.add(index)

    def copy(source, target, send, receive, to):
        return pltpu.make_async_remote_copy(
            src_ref=source, dst_ref=target, send_sem=send, recv_sem=receive,
            device_id=to, device_id_type=pl.DeviceIdType.MESH,
        )

    started = []

    def carry_task(block, own):
        while not done.issuperset(range(own.start, own.stop)):
            yield
        parts = [
            copy(
                sent_ref.at[own], part_ref.at[hop - 1, own],
                part_send.at[hop - 1, block], part_recv.at[hop - 1, block], in_plane(hop),
            )
            for hop in hops
        ]
        for part in parts:
            part.start()
        yield from pause(lags[5])
        for part in parts:
            part.wait_recv()
        total = sent_ref[own].astype(f32)
        for hop in hops:
            total = total + part_ref[hop - 1, own].astype(f32)
        total_ref[own] = total.astype(jnp.bfloat16)
        planes = [
            copy(
                total_ref.at[own], plane_ref.at[hop - 1, own],
                plane_send.at[hop - 1, block], plane_recv.at[hop - 1, block], in_seat(hop),
            )
            for hop in hops
        ]
        for part in planes:
            part.start()
        started.append((own, parts, planes))

    def after(group, parts):
        if (group + 1) % CARRIED == 0:
            block = group // CARRIED
            yield carry_task(block, slice(block * CARRIED * parts, (block + 1) * CARRIED * parts))

    interleave(time_tasks(lags, token_ref, packed_ref, square_ref, finish, after))
    chunks = []
    for own, parts, planes in started:
        for part in planes:
            part.wait_recv()
        for index in range(own.start, own.stop):
            before = jnp.zeros(latent_ref.shape[1:], f32)
            for hop in hops:
                value = plane_ref[hop - 1, index].astype(f32)
                before = before + jnp.where(plane >= hop, value, 0.0)
                value = part_ref[hop - 1, index].astype(f32)
                before = before + jnp.where(seat >= hop, value, 0.0)
            chunks.append(before + increment_ref[index] if last else before)
    for frame, own in enumerate(regrid(chunks)):
        out_ref[frame] = own if last else jnp.where(timestep == 0, latent_ref[frame], own)
    for own, parts, planes in started:
        for part in parts + planes:
            part.wait_send()


def whole(array):
    zeros = (0,) * array.ndim
    return pl.BlockSpec(array.shape, lambda *_: zeros, pipeline_mode=pl.Buffered(1))


def fold(own, modulation, embed_weight, space_input, space_output, time_input, time_output, final_weight):
    features = modulation.shape[2]
    shapes = [
        ((ROWS_AA, 2 * CHANNELS), jnp.bfloat16),
        ((3 * (ROWS_T + 8), LANES), jnp.float32),
        ((3 * INNER, WIDE), jnp.bfloat16),
        ((BASE + WIDE, BASE + WIDE), jnp.bfloat16),
        ((CHANNELS, LANES), jnp.float32),
    ]
    weights = (embed_weight, space_input, space_output, time_input, time_output, final_weight)
    return pl.pallas_call(
        fold_kernel,
        out_shape=[jax.ShapeDtypeStruct(*shape) for shape in shapes],
        grid_spec=pltpu.PrefetchScalarGridSpec(
            num_scalar_prefetch=1,
            grid=(1,),
            in_specs=[
                pl.BlockSpec(
                    (None,) + modulation.shape[1:],
                    lambda step, own: (own[0], 0, 0),
                    pipeline_mode=pl.Buffered(1),
                )
            ]
            + [whole(weight) for weight in weights],
            out_specs=[
                pl.BlockSpec(shape, lambda *_: (0, 0), pipeline_mode=pl.Buffered(1))
                for shape, kind in shapes
            ],
            scratch_shapes=[pltpu.VMEM((BASE + WIDE, features), jnp.bfloat16)],
        ),
        compiler_params=pltpu.CompilerParams(vmem_limit_bytes=60 * 1024 * 1024),
        name="fold",
    )(own, modulation, *weights)


def space_block(latent, first, offset):
    frames, channels, spatial = latent.shape
    step_frames = math.gcd(frames, 16)
    return pl.pallas_call(
        functools.partial(space_kernel, SPACE_LAGS),
        out_shape=jax.ShapeDtypeStruct((frames, spatial, WIDE), jnp.bfloat16),
        grid=(frames // step_frames,),
        in_specs=[
            pl.BlockSpec((step_frames, channels, spatial), lambda step: (step, 0, 0)),
            whole(first),
            whole(offset),
        ],
        out_specs=pl.BlockSpec((step_frames, spatial, WIDE), lambda step: (step, 0, 0)),
        compiler_params=pltpu.CompilerParams(vmem_limit_bytes=60 * 1024 * 1024),
        name="space_block",
    )(latent, first, offset)


def time_block(tokens, packed, square, shift):
    frames, positions, width = tokens.shape
    return pl.pallas_call(
        functools.partial(time_kernel, TIME_LAGS),
        out_shape=jax.ShapeDtypeStruct((frames, CHANNELS, positions), jnp.float32),
        grid=(1,),
        in_specs=[whole(array) for array in (tokens, packed, square, shift)],
        out_specs=whole(jax.ShapeDtypeStruct((frames, CHANNELS, positions), jnp.float32)),
        compiler_params=pltpu.CompilerParams(vmem_limit_bytes=60 * 1024 * 1024),
        name="time_block",
    )(tokens, packed, square, shift)


def step_block(last, tokens, packed, square, shift, latent, noise, rates):
    frames, positions, width = tokens.shape
    hops = SIDE - 1
    shape = (positions // CHUNK, CHANNELS, frames * CHUNK)
    blocks = positions // (2 * CHUNK * CARRIED)
    vmem = pl.BlockSpec(memory_space=pltpu.VMEM)
    return pl.pallas_call(
        functools.partial(step_kernel, TIME_LAGS, last),
        out_shape=jax.ShapeDtypeStruct(latent.shape, jnp.float32),
        in_specs=[vmem] * 6 + [pl.BlockSpec(memory_space=pltpu.SMEM)] * 3,
        out_specs=vmem,
        scratch_shapes=[
            pltpu.VMEM(shape, jnp.float32),
            pltpu.VMEM(shape, jnp.float32),
            pltpu.VMEM(shape, jnp.bfloat16),
            pltpu.VMEM((hops,) + shape, jnp.bfloat16),
            pltpu.VMEM(shape, jnp.bfloat16),
            pltpu.VMEM((hops,) + shape, jnp.bfloat16),
        ]
        + [pltpu.SemaphoreType.DMA((hops, blocks))] * 4,
        compiler_params=pltpu.CompilerParams(
            collective_id=int(last), has_side_effects=True, vmem_limit_bytes=60 * 1024 * 1024
        ),
        name="step_last" if last else "step",
    )(tokens, packed, square, shift, latent, noise, *rates)


def carried_in(last, groups, same_block, timestep, sent, increment, latent):
    gathered = lax.all_gather(
        sent, "tok", axis_index_groups=same_block if groups > 1 else None
    )
    earlier = (jnp.arange(P_SIZE) < timestep)[:, None, None, None]
    before = jnp.sum(jnp.where(earlier, gathered.astype(jnp.float32), 0.0), axis=0)
    return before + increment if last else jnp.where(timestep == 0, latent, before)


def body(
    initial_guess,
    noise_draws,
    drift_state,
    drift_denoise,
    noise_scale,
    modulation,
    embed_weight,
    space_input,
    space_output,
    time_input,
    time_output,
    final_weight,
):
    devices = lax.axis_size("tok")
    own_index = lax.axis_index("tok")
    groups = devices // P_SIZE
    timestep = own_index // groups
    own = jnp.reshape(timestep, (1,)).astype(jnp.int32)
    rates = (drift_state, drift_denoise, noise_scale)
    same_step = [[step * groups + block for block in range(groups)] for step in range(P_SIZE)]
    same_block = [[step * groups + block for step in range(P_SIZE)] for block in range(groups)]
    first, offset, packed, square, shift = fold(
        own, modulation, embed_weight, space_input.T, space_output, time_input.T, time_output,
        final_weight.T,
    )
    latent = initial_guess
    for iteration in range(ITERS):
        tokens = space_block(latent, first, offset)
        last = iteration == ITERS - 1
        if groups == 1:
            latent = step_block(last, tokens, packed, square, shift, latent, noise_draws, rates)
        else:
            tokens = lax.all_to_all(
                tokens, "tok", split_axis=1, concat_axis=0, axis_index_groups=same_step, tiled=True
            )
            predicted = time_block(tokens, packed, square, shift)
            predicted = lax.all_to_all(
                predicted, "tok", split_axis=0, concat_axis=2, axis_index_groups=same_step, tiled=True
            )
            rate_state, rate_denoise, rate_noise = (
                lax.dynamic_index_in_dim(rate, timestep, 0, keepdims=False) for rate in rates
            )
            rate_state = rate_state + jnp.where(timestep == 0, 1.0, 0.0)
            increment = rate_state * latent + rate_denoise * predicted + rate_noise * noise_draws
            sent = increment.astype(jnp.bfloat16)
            latent = carried_in(last, groups, same_block, timestep, sent, increment, latent)
    return latent


def solution(mesh):
    placed = (
        P(("group", "tok"), None, None),
        P(("group", "tok"), None, None),
        P(),
        P(),
        P(),
        P(),
        P(),
        P(),
        P(),
        P(),
        P(),
        P(),
    )
    return jax.shard_map(
        body, mesh=mesh, in_specs=placed, out_specs=P(("group", "tok"), None, None), check_vma=False
    )
```

```python
import functools
import math

import jax
import jax.numpy as jnp
from jax import lax
from jax.experimental import pallas as pl
from jax.experimental.pallas import tpu as pltpu
from jax.sharding import PartitionSpec as P

HEADS = 8
HD = 72
P_SIZE = 16
ITERS = 2
LANES = 128
INNER = HEADS * HD
SIDE = math.isqrt(P_SIZE)
CHUNK = 8
CARRIED = 2
SPACE_LAGS = (2, 8, 6)
FOLD_LAG = 4
FOLD_EVERY = 3
TIME_LAGS = (4, 8, 10, 8, 2, 48)
EPS = 1e-06
CHANNELS = 16
WIDE = 2 * LANES
ROWS_T = HEADS * CHANNELS
ROWS_AA = 3 * ROWS_T + 32
BASE = 512
TAIL = INNER - BASE
LAT, DUP, ZERO, ONE, ATT = 128, 144, 160, 184, 192
SCALE = HD**-0.5 * math.log2(math.e)
UNIT = HD**0.5 * math.log2(math.e)


def dot_rows(values, weight_rows, precision=None):
    return lax.dot_general(
        values,
        weight_rows,
        (((1,), (1,)), ((), ())),
        preferred_element_type=jnp.float32,
        precision=precision,
    )


def dot(values, weights):
    return jnp.dot(values, weights, preferred_element_type=jnp.float32)


def halves(values):
    high = values.astype(jnp.bfloat16)
    return high, (values - high.astype(jnp.float32)).astype(jnp.bfloat16)


def lane_of(shape):
    return lax.broadcasted_iota(jnp.int32, shape, len(shape) - 1)


def row_of(shape):
    return lax.broadcasted_iota(jnp.int32, shape, 0)


def centred(rows):
    return rows - jnp.mean(rows, -1, keepdims=True)


def by_head(rows, order):
    count, width = rows.shape
    if order == "hc":
        spread = jnp.concatenate([rows] * HEADS, axis=0)
        head = row_of(spread.shape) // count
    else:
        spread = jnp.broadcast_to(rows[:, None, :], (count, HEADS, width)).reshape(-1, width)
        head = row_of(spread.shape) % HEADS
    return jnp.where(lane_of(spread.shape) // HD == head, spread, 0.0)


def stack(*parts):
    return jnp.concatenate(parts, axis=0)


def beside(*parts):
    return jnp.concatenate(parts, axis=1)


def on_diagonal(first, second):
    blank = jnp.zeros_like(first)
    return stack(beside(first, blank), beside(blank, second))


def interleave(tasks):
    tasks, running = list(tasks), []
    while tasks or running:
        running += [tasks.pop(0)] if tasks else []
        running = [task for task in running if next(task, tasks) is not tasks]


def pause(turns):
    for turn in range(turns):
        yield


def wait_for(state, key):
    while key not in state:
        yield


def fold_first(arrive, table, embed_ref, space_in_ref, first_ref, offset_ref):
    embed = centred(embed_ref[...].astype(jnp.float32))
    features = embed.shape[1]

    def zeros(rows, width=features):
        return jnp.zeros((rows, width), jnp.float32)

    arrive("table")
    lines = stack(*halves(embed * (1.0 + table(1))))
    tail = stack(*(half.astype(jnp.float32) for half in halves(stack(table(0), zeros(7)))))
    arrive("space_in")
    folded = dot_rows(stack(lines, tail.astype(jnp.bfloat16)), space_in_ref[...])
    lat = folded[:CHANNELS] + folded[CHANNELS : 2 * CHANNELS]
    const = folded[2 * CHANNELS : 2 * CHANNELS + 8] + folded[2 * CHANNELS + 8 :]

    def part(values, which):
        return values[:, which * INNER : (which + 1) * INNER]

    def fine(rows, side):
        high, low = halves(rows)
        side_high, side_low = halves(side)
        both = dot_rows(high, stack(side_high, side_low))
        return both[:, :LANES] + both[:, LANES:] + dot_rows(low, side_high)

    def side_of(rows, point):
        width = rows.shape[1]
        return stack(rows, rows, point, zeros(7, width), zeros(LANES - 2 * CHANNELS - 8, width))

    query, key, value = (part(lat, which) for which in range(3))
    query_c, key_c, value_c = (part(const, which)[:1] for which in range(3))
    key_side, query_side = side_of(key, key_c), side_of(query, query_c)
    scores = fine(stack(by_head(query, "hc"), by_head(query_c, "ch")) * SCALE, key_side)
    key_square = fine(stack(by_head(key, "ch"), by_head(key_c, "ch")) * (1.0 / HD), key_side)
    query_square = fine(stack(by_head(query, "ch"), by_head(query_c, "ch")) * (1.0 / HD), query_side)
    gram = fine(embed, side_of(embed, zeros(1))) * (1.0 / features)
    first = stack(scores, key_square[:ROWS_T], query_square[:ROWS_T], gram, zeros(8, LANES))
    high, low = halves(first)
    upper = lane_of(first.shape) < CHANNELS
    chosen = jnp.where(upper, high.astype(jnp.float32), low.astype(jnp.float32))
    first_ref[...] = chosen[:, : 2 * CHANNELS].astype(jnp.bfloat16)
    point = 2 * CHANNELS
    offset_ref[: ROWS_T + 8] = jnp.broadcast_to(scores[:, point : point + 1], (ROWS_T + 8, LANES))
    for index, square in enumerate((key_square, query_square)):
        start = ROWS_T + 8 + index * (ROWS_T + 8)
        offset_ref[start : start + ROWS_T] = jnp.broadcast_to(
            2.0 * square[:ROWS_T, point : point + 1], (ROWS_T, LANES)
        )
        offset_ref[start + ROWS_T : start + ROWS_T + 8] = jnp.broadcast_to(
            square[ROWS_T:, point : point + 1], (8, LANES)
        )
    values = stack(*halves(by_head(value, "hc")))
    tail = stack(*(half.astype(jnp.float32) for half in halves(stack(value_c, zeros(7, INNER)))))
    return embed, stack(values, tail.astype(jnp.bfloat16))


def fold_tasks(
    lag, arrive, table, embed, values, space_out_ref, time_in_ref, time_out_ref, final_ref,
    packed_ref, square_ref, shift_ref, lines_ref,
):
    f32 = jnp.float32
    bf16 = jnp.bfloat16
    features = embed.shape[1]
    state = {"mixed": {}, "lines": set()}

    def zeros(rows, width=features):
        return jnp.zeros((rows, width), f32)

    def mixed_task(start):
        if start == 0:
            arrive("space_out")
        own = dot(values, space_out_ref[:, start : min(start + WIDE, features)])
        yield from pause(lag)
        state["mixed"][start] = own

    def rows_task():
        starts = range(0, features, WIDE)
        while len(state["mixed"]) < len(starts):
            yield
        mixed = beside(*(state["mixed"][start] for start in starts))
        gate = table(2)
        attended = centred(gate * (mixed[:ROWS_T] + mixed[ROWS_T : 2 * ROWS_T]))
        point = centred(gate * (mixed[2 * ROWS_T : 2 * ROWS_T + 8] + mixed[2 * ROWS_T + 8 :]))
        yield
        scaled = 1.0 + table(4)
        ends = halves(stack(table(3), point[:1] * scaled, zeros(6)))
        tail = stack(*(half.astype(f32) for half in ends))
        state["rows"] = stack(
            (attended * scaled).astype(bf16), *halves(embed * scaled), tail.astype(bf16)
        )
        lines_ref[:LAT] = attended.astype(bf16)
        high, low = halves(embed)
        lines_ref[LAT:DUP] = high
        lines_ref[DUP:ZERO] = low
        point = (half.astype(f32) for half in halves(point[:1]))
        lines_ref[ZERO:ATT] = stack(zeros(ONE - ZERO), *point, zeros(ATT - ONE - 2)).astype(bf16)
        state["lines"].add("tokens")

    def settle(columns):
        lat = columns[LAT:DUP] + columns[DUP : DUP + CHANNELS]
        lat_high = lat.astype(bf16).astype(f32)
        ends = columns[DUP + CHANNELS : DUP + CHANNELS + 8] + columns[DUP + CHANNELS + 8 :]
        ends_high = ends.astype(bf16).astype(f32)
        ends_low = ends - ends_high
        width = columns.shape[1]
        return stack(
            columns[:LAT], lat_high, lat - lat_high,
            ends_high[:1], ends_high[:1], ends_low[:1], zeros(ONE - ZERO - 3, width),
            ends_high[1:2], ends_low[1:2], zeros(WIDE - ONE - 2, width),
        ).astype(bf16)

    def packed_task(start):
        yield from wait_for(state, "rows")
        if start == 0:
            arrive("time_in")
        own = slice(start, min(start + WIDE, 3 * INNER))
        columns = dot_rows(state["rows"], time_in_ref[own, :])
        yield from pause(lag)
        packed_ref[own] = settle(columns).T

    def lines_task(start):
        arrive("time_out")
        gate = table(5)
        if start == BASE:
            own, target = slice(BASE, INNER), ATT
        else:
            own, target = slice(start, start + LANES), WIDE + start
        rows = centred(gate * time_out_ref[own].astype(f32))
        lines_ref[target : target + rows.shape[0]] = rows.astype(bf16)
        state["lines"].add(start)
        yield

    tiles = lines_ref.shape[0] // WIDE

    def square_task(column, row):
        while len(state["lines"]) < 2 + BASE // LANES:
            yield
        other = lines_ref[column * WIDE : (column + 1) * WIDE]
        if column == 0:
            final = final_ref[...].astype(f32)
            if row == 0:
                shift_ref[...] = jnp.broadcast_to(
                    jnp.sum(final * table(6), -1, keepdims=True), (CHANNELS, LANES)
                )
            final = (final * (1.0 + table(7))).astype(bf16)
            other = stack(other[:ZERO], final, other[ZERO + CHANNELS :])
        block = dot_rows(other, lines_ref[row * WIDE : (row + 1) * WIDE])
        yield from pause(lag)
        gain = (1.0 if row == column else 2.0) / features
        if column == 0:
            line = row_of((WIDE, 1))
            gain = jnp.where((line >= ZERO) & (line < ZERO + CHANNELS), 1.0, gain)
        square_ref[column * WIDE : (column + 1) * WIDE, row * WIDE : (row + 1) * WIDE] = (
            (block * gain).astype(bf16)
        )

    starts = range(0, features, WIDE)
    yield from (mixed_task(start) for start in starts)
    yield rows_task()
    yield from (lines_task(start) for start in range(0, BASE + 1, LANES))
    yield from (packed_task(start) for start in range(0, 3 * INNER, WIDE))
    yield from (square_task(column, row) for column in range(tiles) for row in range(column, tiles))


def fold_kernel(
    step_ref, table_ref, embed_ref, space_in_ref, space_out_ref, time_in_ref, time_out_ref, final_ref,
    first_ref, offset_ref, packed_ref, square_ref, shift_ref, lines_ref,
):
    def table(row):
        return table_ref[row : row + 1, :]

    def arrive(name):
        pass

    embed, values = fold_first(arrive, table, embed_ref, space_in_ref, first_ref, offset_ref)
    interleave(
        fold_tasks(
            3, arrive, table, embed, values, space_out_ref, time_in_ref, time_out_ref, final_ref,
            packed_ref, square_ref, shift_ref, lines_ref,
        )
    )


def space_tasks(lags, latent_ref, first_ref, offset_ref, token_ref):
    frames, channels, spatial = latent_ref.shape
    bf16 = jnp.bfloat16
    f32 = jnp.float32
    row = row_of((8, spatial))
    blank = jnp.zeros((8, spatial), f32)
    ones = jnp.ones((8, spatial), f32)
    states = [{} for frame in range(frames)]

    def offset(start, rows):
        return offset_ref[start : start + rows]

    def twice(frame):
        latent = latent_ref[frame].astype(bf16)
        return stack(latent, latent)

    def couple_task(frame):
        own = range(frame, min(frame + 2, frames))
        product = dot(first_ref[...], beside(*(twice(index) for index in own)))
        yield from pause(lags[0])
        for place, index in enumerate(own):
            states[index]["result"] = product[:, place * spatial : (place + 1) * spatial]

    def frame_task(frame):
        state = states[frame]
        yield from wait_for(state, "result")
        result = state["result"]
        latent = latent_ref[frame].astype(bf16).astype(f32)
        gram = result[3 * ROWS_T + 8 : 3 * ROWS_T + 8 + channels]
        variance = jnp.maximum(jnp.sum(latent * gram, 0, keepdims=True), 0.0) + EPS
        rate = lax.rsqrt(variance)
        yield
        spread = variance * rate
        scaled = latent * rate

        def norm(index):
            start = ROWS_T + 8 + index * ROWS_T
            place = ROWS_T + 8 + index * (ROWS_T + 8)
            terms = rate * result[start : start + ROWS_T] + offset(place, ROWS_T)
            terms = terms.reshape(channels, HEADS, spatial) * scaled[:, None, :]
            total = jnp.sum(terms, 0) + offset(place + ROWS_T, 8)
            return lax.rsqrt(jnp.maximum(total, 0.0) + EPS)

        key_rate = norm(0)
        yield
        query_rate = norm(1) * rate
        yield
        point = (rate * result[ROWS_T : ROWS_T + 8] + offset(ROWS_T, 8)) * key_rate
        point_high = point.astype(bf16).astype(f32)
        spread_high = spread.astype(bf16).astype(f32)
        ends = jnp.where(row == 1, spread - spread_high, jnp.where(row < 3, spread_high, 0.0))
        source = stack(twice(frame), stack(ends, blank).astype(bf16))
        state.update(
            terms=lambda start: rate * result[start : start + channels] + offset(start, channels),
            key_rate=key_rate,
            query_rate=query_rate,
            point=(point_high, point - point_high),
            right=on_diagonal(source, source),
            rows=stack(scaled, ones, blank).astype(bf16),
            averages=[],
        )

    def pair_task(frame, pair):
        state = states[frame]
        heads = (2 * pair, 2 * pair + 1)
        yield from wait_for(state, "rows")
        left = []
        for head in heads:
            own = state["terms"](head * channels) * state["key_rate"][head : head + 1]
            high, low = (part[head : head + 1] for part in state["point"])
            own_point = jnp.where(row < 2, high, jnp.where(row == 2, low, 0.0))
            left += [*halves(own), stack(own_point, blank).astype(bf16)]
        left = stack(*left).T
        yield
        score = dot(left, state["right"])
        yield from pause(lags[1])
        pace = beside(*(state["query_rate"][head : head + 1] for head in heads))
        weight = jnp.exp2(score * pace).astype(bf16)
        yield
        mixed = dot(state["rows"], weight)
        yield from pause(lags[2])
        share = 1.0 / mixed[channels : channels + 8]
        mixed = (mixed[:channels].reshape(-1, 8, 2 * spatial) * share[None]).reshape(channels, -1)
        state["averages"] += [mixed[:, :spatial], mixed[:, spatial:]]
        if pair == HEADS // 2 - 1:
            latent = latent_ref[frame].astype(bf16).astype(f32)
            token = stack(
                *state["averages"], latent, latent, blank, blank, blank, ones, *[blank] * 8
            )
            token_ref[frame] = token.astype(bf16).T

    def tasks():
        for frame in range(-2, frames):
            ahead = frame + 2
            if ahead < frames:
                if ahead % 2 == 0:
                    yield couple_task(ahead)
                yield frame_task(ahead)
            if frame >= 0:
                yield from (pair_task(frame, pair) for pair in range(HEADS // 2))

    return tasks()


def space_kernel(lags, *refs):
    interleave(space_tasks(lags, *refs))


def regrid(chunks):
    count, (_, lanes) = len(chunks), chunks[0].shape
    block = lane_of(chunks[0].shape) // CHUNK
    if count * CHUNK != lanes or count & (count - 1):
        return [
            beside(*(part[:, index * CHUNK : (index + 1) * CHUNK] for part in chunks))
            for index in range(lanes // CHUNK)
        ]
    chunks, step = list(chunks), 1
    while step < count:
        moved = (block & step) != 0
        for low in range(count):
            if low & step == 0:
                first, second = chunks[low], chunks[low + step]
                chunks[low] = jnp.where(moved, pltpu.roll(second, step * CHUNK, 1), first)
                chunks[low + step] = jnp.where(
                    moved, second, pltpu.roll(first, lanes - step * CHUNK, 1)
                )
        step *= 2
    return chunks


def time_tasks(lags, token_ref, packed_ref, square_ref, finish, after=lambda group, parts: ()):
    bf16 = jnp.bfloat16
    f32 = jnp.float32
    frames, positions, width = token_ref.shape
    chunk = CHUNK
    rows = frames * chunk
    size = math.gcd(positions, 2 * chunk)
    parts = size // chunk
    groups = positions // size
    count = parts * rows
    keep = (row_of((rows, 2 * rows)) % chunk) == (lane_of((rows, 2 * rows)) % chunk)
    ones = jnp.ones((8, rows), f32)
    row = row_of((16, count))
    states = [{} for group in range(groups)]

    def group_task(group):
        state = states[group]
        tokens = token_ref[:, group * size : (group + 1) * size, :].astype(f32)
        tokens = tokens.reshape(frames, parts, chunk, width)
        tokens = beside(
            *(tokens[:, part].reshape(rows, width).astype(bf16).T for part in range(parts))
        )
        yield
        squares = dot(square_ref[:ATT, :WIDE], tokens)
        yield from pause(lags[0])
        variance = jnp.sum(tokens[:ATT].astype(f32) * squares, 0, keepdims=True)
        variance = jnp.maximum(variance, 0.0) + EPS
        pace = lax.rsqrt(variance)
        spread = variance * pace
        spread_high = spread.astype(bf16).astype(f32)
        yield
        ends = jnp.where(row == 1, spread - spread_high, jnp.where(row < 3, spread_high, 0.0))
        state.update(
            tokens=tokens, pace=pace, floor=(HD * EPS) * variance, outputs={},
            entry=stack(tokens[:ZERO], ends.astype(bf16), tokens[ZERO + 16 :]),
        )

    def project_task(group, pair):
        state = states[group]
        yield from wait_for(state, "entry")
        starts = [which * INNER + pair * 2 * HD for which in range(3)]
        packed = [dot(packed_ref[start : start + 2 * HD], state["entry"]) for start in starts]
        yield from pause(lags[1])
        state["packed", pair] = packed

    def pair_task(group, pair, part):
        state = states[group]
        own = slice(part * rows, (part + 1) * rows)
        yield from wait_for(state, ("packed", pair))
        packed = [values[:, own] for values in state["packed", pair]]

        def unit(which, head, gain):
            values = packed[which][head * HD : (head + 1) * HD]
            size = lax.rsqrt(jnp.sum(values * values, 0, keepdims=True) + state["floor"][:, own])
            return values * (size * gain if gain else size)

        left = stack(unit(1, 0, None), unit(1, 1, None), jnp.zeros((16, rows), f32)).astype(bf16).T
        yield
        right = on_diagonal(unit(0, 0, UNIT), unit(0, 1, UNIT))
        right = stack(right, jnp.zeros((16, 2 * rows), f32)).astype(bf16)
        score = dot(left, right)
        yield from pause(lags[2])
        weight = jnp.where(keep, jnp.exp2(score), 0.0).astype(bf16)
        yield
        value = packed[2] * state["pace"][:, own]
        value = beside(stack(value[:HD], ones), stack(value[HD:], ones)).astype(bf16)
        mixed = dot(value, on_diagonal(weight[:, :rows], weight[:, rows:]))
        yield from pause(lags[3])
        share = 1.0 / mixed[HD:]
        mixed = (mixed[:HD].reshape(-1, 8, 2 * rows) * share[None]).reshape(HD, 2 * rows)
        state["outputs"][part, pair] = stack(mixed[:, :rows], mixed[:, rows:])

    def last_task(group):
        state = states[group]
        while len(state.get("outputs", ())) < parts * HEADS // 2:
            yield
        attended = beside(
            *(
                stack(*(state["outputs"][part, pair] for pair in range(HEADS // 2)))
                for part in range(parts)
            )
        )
        exact = stack(state["tokens"][:ATT].astype(f32), attended[BASE:], attended[:BASE])
        inputs = exact.astype(bf16)
        yield
        blocks = []
        for start in range(0, exact.shape[0], WIDE):
            blocks.append(dot(square_ref[start : start + WIDE, start:], inputs[start:]))
            yield
        yield from pause(lags[4])
        total = 0.0
        for index, block in enumerate(blocks):
            terms = block * exact[index * WIDE : (index + 1) * WIDE]
            total = total + jnp.sum(terms.reshape(-1, 8, count), 0)
        rate = lax.rsqrt(jnp.maximum(jnp.sum(total, 0, keepdims=True), 0.0) + EPS)
        yield
        predicted = blocks[0][ZERO : ZERO + CHANNELS] * rate
        for part in range(parts):
            finish(group * parts + part, predicted[:, part * rows : (part + 1) * rows])

    def tasks():
        yield group_task(0)
        for group in range(groups):
            for pair in range(HEADS // 2):
                yield project_task(group, pair)
                if pair == 1 and group + 1 < groups:
                    yield group_task(group + 1)
                yield from (pair_task(group, pair, part) for part in range(parts))
            yield last_task(group)
            yield from after(group, parts)

    return tasks()


def time_kernel(lags, token_ref, packed_ref, square_ref, shift_ref, result_ref):
    chunks = {}
    interleave(time_tasks(lags, token_ref, packed_ref, square_ref, chunks.__setitem__))
    for frame, own in enumerate(regrid([chunks[index] for index in sorted(chunks)])):
        result_ref[frame] = own + shift_ref[:, : own.shape[1]]


def merged(tasks, others, every):
    others = list(others)
    for index, task in enumerate(tasks):
        yield task
        if others and index % every == every - 1:
            yield others.pop(0)
    yield from others


def sampler_kernel(
    table_from, embed_ref, space_in_from, space_out_from, time_in_from, time_out_from, final_ref,
    latent_ref, noise_ref, state_ref, denoise_ref, scale_ref, out_ref,
    table_ref, space_in_ref, space_out_ref, time_in_ref, time_out_ref,
    first_ref, offset_ref, packed_ref, square_ref, shift_ref, lines_ref, token_ref,
    own_ref, fresh_ref, running_ref, increment_ref, sent_ref, part_ref, total_ref, plane_ref,
    load_sem, part_send, part_recv, plane_send, plane_recv,
):
    f32 = jnp.float32
    bf16 = jnp.bfloat16
    frames = latent_ref.shape[0]
    timestep = lax.axis_index("tok")
    plane, seat = timestep // SIDE, timestep % SIDE
    hops = range(1, SIDE)

    loads = {
        name: pltpu.make_async_copy(source, target, load_sem.at[index])
        for index, (name, source, target) in enumerate(
            (
                ("table", table_from.at[timestep], table_ref),
                ("space_in", space_in_from, space_in_ref),
                ("space_out", space_out_from, space_out_ref),
                ("time_out", time_out_from, time_out_ref),
                ("time_in", time_in_from, time_in_ref),
            )
        )
    }
    for load in loads.values():
        load.start()

    def in_plane(hop):
        return {"tok": plane * SIDE + (seat + hop) % SIDE}

    def in_seat(hop):
        return {"tok": (plane + hop) % SIDE * SIDE + seat}

    barrier = pltpu.get_barrier_semaphore()
    for hop in hops:
        for target in (in_plane(hop), in_seat(hop)):
            pl.semaphore_signal(
                barrier, inc=1, device_id=target, device_id_type=pl.DeviceIdType.MESH
            )

    def arrive(name):
        if name in loads:
            loads.pop(name).wait()

    def table(row):
        return table_ref[row : row + 1, :]

    rate_denoise = denoise_ref[timestep]
    rate_state = state_ref[timestep] + jnp.where(timestep == 0, 1.0, 0.0)
    rate_noise = scale_ref[timestep]
    for target, source in ((running_ref, latent_ref), (fresh_ref, noise_ref)):
        for index, own in enumerate(regrid([source[frame] for frame in range(frames)])):
            target[index] = own
    embed, values = fold_first(arrive, table, embed_ref, space_in_ref, first_ref, offset_ref)

    def copy(source, target, send, receive, to):
        return pltpu.make_async_remote_copy(
            src_ref=source, dst_ref=target, send_sem=send, recv_sem=receive,
            device_id=to, device_id_type=pl.DeviceIdType.MESH,
        )

    sent = []
    for iteration in range(ITERS):
        last = iteration == ITERS - 1
        source_ref = own_ref if iteration else latent_ref
        spread = space_tasks(SPACE_LAGS, source_ref, first_ref, offset_ref, token_ref)
        if iteration == 0:
            others = fold_tasks(
                FOLD_LAG, arrive, table, embed, values, space_out_ref, time_in_ref, time_out_ref,
                final_ref, packed_ref, square_ref, shift_ref, lines_ref,
            )
            spread = merged(spread, others, FOLD_EVERY)
        interleave(spread)
        if iteration == 0:
            pl.semaphore_wait(barrier, 2 * (SIDE - 1))
        done, started = set(), []

        def finish(index, predicted):
            increment = rate_denoise * (predicted + shift_ref[...])
            increment = increment + rate_noise * fresh_ref[index] + rate_state * running_ref[index]
            increment_ref[index] = increment
            sent_ref[iteration, index] = increment.astype(bf16)
            done.add(index)

        def carry_task(block, own):
            while not done.issuperset(range(own.start, own.stop)):
                yield
            parts = [
                copy(
                    sent_ref.at[iteration, own], part_ref.at[iteration, hop - 1, own],
                    part_send.at[iteration, hop - 1, block], part_recv.at[iteration, hop - 1, block],
                    in_plane(hop),
                )
                for hop in hops
            ]
            for part in parts:
                part.start()
            yield from pause(TIME_LAGS[5])
            for part in parts:
                part.wait_recv()
            total = sent_ref[iteration, own].astype(f32)
            for hop in hops:
                total = total + part_ref[iteration, hop - 1, own].astype(f32)
            total_ref[iteration, own] = total.astype(bf16)
            planes = [
                copy(
                    total_ref.at[iteration, own], plane_ref.at[iteration, hop - 1, own],
                    plane_send.at[iteration, hop - 1, block], plane_recv.at[iteration, hop - 1, block],
                    in_seat(hop),
                )
                for hop in hops
            ]
            for part in planes:
                part.start()
            started.append((own, planes))
            sent.extend(parts + planes)

        def after(group, parts):
            if (group + 1) % CARRIED == 0:
                block = group // CARRIED
                yield carry_task(block, slice(block * CARRIED * parts, (block + 1) * CARRIED * parts))

        interleave(time_tasks(TIME_LAGS, token_ref, packed_ref, square_ref, finish, after))
        chunks = []
        for own, planes in started:
            for part in planes:
                part.wait_recv()
            for index in range(own.start, own.stop):
                before = jnp.zeros(latent_ref.shape[1:], f32)
                for hop in hops:
                    value = plane_ref[iteration, hop - 1, index].astype(f32)
                    before = before + jnp.where(plane >= hop, value, 0.0)
                    value = part_ref[iteration, hop - 1, index].astype(f32)
                    before = before + jnp.where(seat >= hop, value, 0.0)
                if last:
                    chunks.append(before + increment_ref[index])
                else:
                    chunks.append(jnp.where(timestep == 0, running_ref[index], before))
                    running_ref[index] = chunks[-1]
        target_ref = out_ref if last else own_ref
        for frame, own in enumerate(regrid(chunks)):
            target_ref[frame] = own
    for part in sent:
        part.wait_send()


def whole(array):
    zeros = (0,) * array.ndim
    return pl.BlockSpec(array.shape, lambda *_: zeros, pipeline_mode=pl.Buffered(1))


def fold(own, modulation, embed_weight, space_input, space_output, time_input, time_output, final_weight):
    features = modulation.shape[2]
    shapes = [
        ((ROWS_AA, 2 * CHANNELS), jnp.bfloat16),
        ((3 * (ROWS_T + 8), LANES), jnp.float32),
        ((3 * INNER, WIDE), jnp.bfloat16),
        ((BASE + WIDE, BASE + WIDE), jnp.bfloat16),
        ((CHANNELS, LANES), jnp.float32),
    ]
    weights = (embed_weight, space_input, space_output, time_input, time_output, final_weight)
    return pl.pallas_call(
        fold_kernel,
        out_shape=[jax.ShapeDtypeStruct(*shape) for shape in shapes],
        grid_spec=pltpu.PrefetchScalarGridSpec(
            num_scalar_prefetch=1,
            grid=(1,),
            in_specs=[
                pl.BlockSpec(
                    (None,) + modulation.shape[1:],
                    lambda step, own: (own[0], 0, 0),
                    pipeline_mode=pl.Buffered(1),
                )
            ]
            + [whole(weight) for weight in weights],
            out_specs=[
                pl.BlockSpec(shape, lambda *_: (0, 0), pipeline_mode=pl.Buffered(1))
                for shape, kind in shapes
            ],
            scratch_shapes=[pltpu.VMEM((BASE + WIDE, features), jnp.bfloat16)],
        ),
        compiler_params=pltpu.CompilerParams(vmem_limit_bytes=60 * 1024 * 1024),
        name="fold",
    )(own, modulation, *weights)


def space_block(latent, first, offset):
    frames, channels, spatial = latent.shape
    step_frames = math.gcd(frames, 16)
    return pl.pallas_call(
        functools.partial(space_kernel, SPACE_LAGS),
        out_shape=jax.ShapeDtypeStruct((frames, spatial, WIDE), jnp.bfloat16),
        grid=(frames // step_frames,),
        in_specs=[
            pl.BlockSpec((step_frames, channels, spatial), lambda step: (step, 0, 0)),
            whole(first),
            whole(offset),
        ],
        out_specs=pl.BlockSpec((step_frames, spatial, WIDE), lambda step: (step, 0, 0)),
        compiler_params=pltpu.CompilerParams(vmem_limit_bytes=60 * 1024 * 1024),
        name="space_block",
    )(latent, first, offset)


def time_block(tokens, packed, square, shift):
    frames, positions, width = tokens.shape
    return pl.pallas_call(
        functools.partial(time_kernel, TIME_LAGS),
        out_shape=jax.ShapeDtypeStruct((frames, CHANNELS, positions), jnp.float32),
        grid=(1,),
        in_specs=[whole(array) for array in (tokens, packed, square, shift)],
        out_specs=whole(jax.ShapeDtypeStruct((frames, CHANNELS, positions), jnp.float32)),
        compiler_params=pltpu.CompilerParams(vmem_limit_bytes=60 * 1024 * 1024),
        name="time_block",
    )(tokens, packed, square, shift)


def sampler(modulation, weights, latent, noise, rates):
    embed, space_in, space_out, time_in, time_out, final = weights
    frames, channels, positions = latent.shape
    features = embed.shape[1]
    hops = SIDE - 1
    shape = (positions // CHUNK, channels, frames * CHUNK)
    blocks = positions // (2 * CHUNK * CARRIED)
    vmem, anywhere = (pl.BlockSpec(memory_space=space) for space in (pltpu.VMEM, pl.ANY))
    f32, bf16 = jnp.float32, jnp.bfloat16
    scratch = [(modulation.shape[1:], f32)]
    scratch += [(weight.shape, bf16) for weight in (space_in, space_out, time_in, time_out)]
    scratch += [
        ((ROWS_AA, 2 * CHANNELS), bf16),
        ((3 * (ROWS_T + 8), LANES), f32),
        ((3 * INNER, WIDE), bf16),
        ((BASE + WIDE, BASE + WIDE), bf16),
        ((CHANNELS, LANES), f32),
        ((BASE + WIDE, features), bf16),
        ((frames, positions, WIDE), bf16),
        (latent.shape, f32),
        (shape, f32),
        (shape, f32),
        (shape, f32),
        ((ITERS,) + shape, bf16),
        ((ITERS, hops) + shape, bf16),
        ((ITERS,) + shape, bf16),
        ((ITERS, hops) + shape, bf16),
    ]
    return pl.pallas_call(
        sampler_kernel,
        out_shape=jax.ShapeDtypeStruct(latent.shape, f32),
        in_specs=[anywhere, vmem] + [anywhere] * 4 + [vmem] * 3
        + [pl.BlockSpec(memory_space=pltpu.SMEM)] * 3,
        out_specs=vmem,
        scratch_shapes=[pltpu.VMEM(*each) for each in scratch]
        + [pltpu.SemaphoreType.DMA((5,))]
        + [pltpu.SemaphoreType.DMA((ITERS, hops, blocks))] * 4,
        compiler_params=pltpu.CompilerParams(
            collective_id=0, has_side_effects=True, vmem_limit_bytes=60 * 1024 * 1024
        ),
        name="sampler",
    )(modulation, *weights, latent, noise, *rates)


def carried_in(last, groups, same_block, timestep, sent, increment, latent):
    gathered = lax.all_gather(
        sent, "tok", axis_index_groups=same_block if groups > 1 else None
    )
    earlier = (jnp.arange(P_SIZE) < timestep)[:, None, None, None]
    before = jnp.sum(jnp.where(earlier, gathered.astype(jnp.float32), 0.0), axis=0)
    return before + increment if last else jnp.where(timestep == 0, latent, before)


def body(
    initial_guess,
    noise_draws,
    drift_state,
    drift_denoise,
    noise_scale,
    modulation,
    embed_weight,
    space_input,
    space_output,
    time_input,
    time_output,
    final_weight,
):
    devices = lax.axis_size("tok")
    own_index = lax.axis_index("tok")
    groups = devices // P_SIZE
    timestep = own_index // groups
    own = jnp.reshape(timestep, (1,)).astype(jnp.int32)
    rates = (drift_state, drift_denoise, noise_scale)
    same_step = [[step * groups + block for block in range(groups)] for step in range(P_SIZE)]
    same_block = [[step * groups + block for step in range(P_SIZE)] for block in range(groups)]
    weights = (
        embed_weight, space_input.T, space_output, time_input.T, time_output, final_weight.T
    )
    if groups == 1:
        return sampler(modulation, weights, initial_guess, noise_draws, rates)
    first, offset, packed, square, shift = fold(own, modulation, *weights)
    latent = initial_guess
    for iteration in range(ITERS):
        tokens = space_block(latent, first, offset)
        last = iteration == ITERS - 1
        tokens = lax.all_to_all(
            tokens, "tok", split_axis=1, concat_axis=0, axis_index_groups=same_step, tiled=True
        )
        predicted = time_block(tokens, packed, square, shift)
        predicted = lax.all_to_all(
            predicted, "tok", split_axis=0, concat_axis=2, axis_index_groups=same_step, tiled=True
        )
        rate_state, rate_denoise, rate_noise = (
            lax.dynamic_index_in_dim(rate, timestep, 0, keepdims=False) for rate in rates
        )
        rate_state = rate_state + jnp.where(timestep == 0, 1.0, 0.0)
        increment = rate_state * latent + rate_denoise * predicted + rate_noise * noise_draws
        sent = increment.astype(jnp.bfloat16)
        latent = carried_in(last, groups, same_block, timestep, sent, increment, latent)
    return latent


def solution(mesh):
    placed = (
        P(("group", "tok"), None, None),
        P(("group", "tok"), None, None),
        P(),
        P(),
        P(),
        P(),
        P(),
        P(),
        P(),
        P(),
        P(),
        P(),
    )
    return jax.shard_map(
        body, mesh=mesh, in_specs=placed, out_specs=P(("group", "tok"), None, None), check_vma=False
    )
```

```python
import functools
import math

import jax
import jax.numpy as jnp
from jax import lax
from jax.experimental import pallas as pl
from jax.experimental.pallas import tpu as pltpu
from jax.sharding import PartitionSpec as P

HEADS = 8
HD = 72
P_SIZE = 16
ITERS = 2
LANES = 128
INNER = HEADS * HD
SIDE = math.isqrt(P_SIZE)
CHUNK = 8
CARRIED = 2
SPACE_LAGS = (2, 8, 6)
FOLD_LAG = 4
FOLD_EVERY = 2
TIME_LAGS = (4, 8, 10, 8, 2, 80)
EPS = 1e-06
CHANNELS = 16
WIDE = 2 * LANES
ROWS_T = HEADS * CHANNELS
ROWS_AA = 3 * ROWS_T + 32
BASE = 512
TAIL = INNER - BASE
LAT, DUP, ZERO, ONE, ATT = 128, 144, 160, 184, 192
SCALE = HD**-0.5 * math.log2(math.e)
UNIT = HD**0.5 * math.log2(math.e)


def dot_rows(values, weight_rows, precision=None):
    return lax.dot_general(
        values,
        weight_rows,
        (((1,), (1,)), ((), ())),
        preferred_element_type=jnp.float32,
        precision=precision,
    )


def dot(values, weights):
    return jnp.dot(values, weights, preferred_element_type=jnp.float32)


def halves(values):
    high = values.astype(jnp.bfloat16)
    return high, (values - high.astype(jnp.float32)).astype(jnp.bfloat16)


def lane_of(shape):
    return lax.broadcasted_iota(jnp.int32, shape, len(shape) - 1)


def row_of(shape):
    return lax.broadcasted_iota(jnp.int32, shape, 0)


def centred(rows):
    return rows - jnp.mean(rows, -1, keepdims=True)


def by_head(rows, order):
    count, width = rows.shape
    if order == "hc":
        spread = jnp.concatenate([rows] * HEADS, axis=0)
        head = row_of(spread.shape) // count
    else:
        spread = jnp.broadcast_to(rows[:, None, :], (count, HEADS, width)).reshape(-1, width)
        head = row_of(spread.shape) % HEADS
    return jnp.where(lane_of(spread.shape) // HD == head, spread, 0.0)


def stack(*parts):
    return jnp.concatenate(parts, axis=0)


def beside(*parts):
    return jnp.concatenate(parts, axis=1)


def on_diagonal(first, second):
    blank = jnp.zeros_like(first)
    return stack(beside(first, blank), beside(blank, second))


def interleave(tasks):
    tasks, running = list(tasks), []
    while tasks or running:
        running += [tasks.pop(0)] if tasks else []
        running = [task for task in running if next(task, tasks) is not tasks]


def pause(turns):
    for turn in range(turns):
        yield


def wait_for(state, key):
    while key not in state:
        yield


def fold_tasks(
    lag, arrive, state, table, embed_ref, space_in_ref, space_out_ref, time_in_ref, time_out_ref,
    final_ref, first_ref, offset_ref, packed_ref, square_ref, shift_ref, lines_ref,
):
    f32 = jnp.float32
    bf16 = jnp.bfloat16
    features = embed_ref.shape[1]
    embed = centred(embed_ref[...].astype(f32))
    state.update(mixed={}, lines=set())

    def zeros(rows, width=features):
        return jnp.zeros((rows, width), f32)

    def fine_parts(rows, side):
        high, low = halves(rows)
        side_high, side_low = halves(side)
        return dot_rows(high, stack(side_high, side_low)), dot_rows(low, side_high)

    def fine_sum(both, rest):
        return both[:, :LANES] + both[:, LANES:] + rest

    def side_of(rows, point):
        width = rows.shape[1]
        return stack(rows, rows, point, zeros(7, width), zeros(LANES - 2 * CHANNELS - 8, width))

    def first_task():
        arrive("table")
        lines = stack(*halves(embed * (1.0 + table(1))))
        tail = stack(*(half.astype(f32) for half in halves(stack(table(0), zeros(7)))))
        left = stack(lines, tail.astype(bf16))
        folded = []
        for which in range(3):
            arrive(("space_in", which))
            folded.append(dot_rows(left, space_in_ref[which * INNER : (which + 1) * INNER]))
            yield
        yield from pause(lag)
        query, key, value = (
            own[:CHANNELS] + own[CHANNELS : 2 * CHANNELS] for own in folded
        )
        query_c, key_c, value_c = (
            (own[2 * CHANNELS : 2 * CHANNELS + 8] + own[2 * CHANNELS + 8 :])[:1] for own in folded
        )
        key_side, query_side = side_of(key, key_c), side_of(query, query_c)
        scores = fine_parts(stack(by_head(query, "hc"), by_head(query_c, "ch")) * SCALE, key_side)
        yield
        key_square = fine_parts(
            stack(by_head(key, "ch"), by_head(key_c, "ch")) * (1.0 / HD), key_side
        )
        yield
        query_square = fine_parts(
            stack(by_head(query, "ch"), by_head(query_c, "ch")) * (1.0 / HD), query_side
        )
        gram = fine_parts(embed, side_of(embed, zeros(1)))
        yield
        values = stack(*halves(by_head(value, "hc")))
        tail = stack(*(half.astype(f32) for half in halves(stack(value_c, zeros(7, INNER)))))
        state["values"] = stack(values, tail.astype(bf16))
        yield from pause(lag)
        scores, key_square, query_square = (
            fine_sum(*each) for each in (scores, key_square, query_square)
        )
        gram = fine_sum(*gram) * (1.0 / features)
        first = stack(scores, key_square[:ROWS_T], query_square[:ROWS_T], gram, zeros(8, LANES))
        high, low = halves(first)
        upper = lane_of(first.shape) < CHANNELS
        chosen = jnp.where(upper, high.astype(f32), low.astype(f32))
        first_ref[...] = chosen[:, : 2 * CHANNELS].astype(bf16)
        point = 2 * CHANNELS
        offset_ref[: ROWS_T + 8] = jnp.broadcast_to(
            scores[:, point : point + 1], (ROWS_T + 8, LANES)
        )
        for index, square in enumerate((key_square, query_square)):
            start = ROWS_T + 8 + index * (ROWS_T + 8)
            offset_ref[start : start + ROWS_T] = jnp.broadcast_to(
                2.0 * square[:ROWS_T, point : point + 1], (ROWS_T, LANES)
            )
            offset_ref[start + ROWS_T : start + ROWS_T + 8] = jnp.broadcast_to(
                square[ROWS_T:, point : point + 1], (8, LANES)
            )
        state["first"] = True

    def mixed_task(start):
        yield from wait_for(state, "values")
        if start == 0:
            arrive("space_out")
        own = dot(state["values"], space_out_ref[:, start : min(start + WIDE, features)])
        yield from pause(lag)
        state["mixed"][start] = own

    def rows_task():
        starts = range(0, features, WIDE)
        while len(state["mixed"]) < len(starts):
            yield
        mixed = beside(*(state["mixed"][start] for start in starts))
        gate = table(2)
        attended = centred(gate * (mixed[:ROWS_T] + mixed[ROWS_T : 2 * ROWS_T]))
        point = centred(gate * (mixed[2 * ROWS_T : 2 * ROWS_T + 8] + mixed[2 * ROWS_T + 8 :]))
        yield
        scaled = 1.0 + table(4)
        ends = halves(stack(table(3), point[:1] * scaled, zeros(6)))
        tail = stack(*(half.astype(f32) for half in ends))
        state["rows"] = stack(
            (attended * scaled).astype(bf16), *halves(embed * scaled), tail.astype(bf16)
        )
        lines_ref[:LAT] = attended.astype(bf16)
        high, low = halves(embed)
        lines_ref[LAT:DUP] = high
        lines_ref[DUP:ZERO] = low
        point = (half.astype(f32) for half in halves(point[:1]))
        lines_ref[ZERO:ATT] = stack(zeros(ONE - ZERO), *point, zeros(ATT - ONE - 2)).astype(bf16)
        state["lines"].add("tokens")

    def settle(columns):
        lat = columns[LAT:DUP] + columns[DUP : DUP + CHANNELS]
        lat_high = lat.astype(bf16).astype(f32)
        ends = columns[DUP + CHANNELS : DUP + CHANNELS + 8] + columns[DUP + CHANNELS + 8 :]
        ends_high = ends.astype(bf16).astype(f32)
        ends_low = ends - ends_high
        width = columns.shape[1]
        return stack(
            columns[:LAT], lat_high, lat - lat_high,
            ends_high[:1], ends_high[:1], ends_low[:1], zeros(ONE - ZERO - 3, width),
            ends_high[1:2], ends_low[1:2], zeros(WIDE - ONE - 2, width),
        ).astype(bf16)

    def packed_task(start):
        yield from wait_for(state, "rows")
        if start == 0:
            arrive("time_in")
        own = slice(start, min(start + WIDE, 3 * INNER))
        columns = dot_rows(state["rows"], time_in_ref[own, :])
        yield from pause(lag)
        packed_ref[own] = settle(columns).T

    def lines_task(start):
        arrive("time_out")
        gate = table(5)
        if start == BASE:
            own, target = slice(BASE, INNER), ATT
        else:
            own, target = slice(start, start + LANES), WIDE + start
        rows = centred(gate * time_out_ref[own].astype(f32))
        lines_ref[target : target + rows.shape[0]] = rows.astype(bf16)
        state["lines"].add(start)
        yield

    tiles = lines_ref.shape[0] // WIDE

    def square_task(column, row):
        while len(state["lines"]) < 2 + BASE // LANES - (column > 0) or column == 0 and "tokens" not in state["lines"]:
            yield
        other = lines_ref[column * WIDE : (column + 1) * WIDE]
        if column == 0:
            final = final_ref[...].astype(f32)
            if row == 0:
                shift_ref[...] = jnp.broadcast_to(
                    jnp.sum(final * table(6), -1, keepdims=True), (CHANNELS, LANES)
                )
            final = (final * (1.0 + table(7))).astype(bf16)
            other = stack(other[:ZERO], final, other[ZERO + CHANNELS :])
        block = dot_rows(other, lines_ref[row * WIDE : (row + 1) * WIDE])
        yield from pause(lag)
        gain = (1.0 if row == column else 2.0) / features
        if column == 0:
            line = row_of((WIDE, 1))
            gain = jnp.where((line >= ZERO) & (line < ZERO + CHANNELS), 1.0, gain)
        square_ref[column * WIDE : (column + 1) * WIDE, row * WIDE : (row + 1) * WIDE] = (
            (block * gain).astype(bf16)
        )

    def ordered():
        packed = [packed_task(start) for start in range(0, 3 * INNER, WIDE)]
        early = [square_task(column, row) for column in range(1, tiles) for row in range(column, tiles)]
        mixed = [mixed_task(start) for start in range(0, features, WIDE)]
        yield from mixed[:2]
        yield from early
        yield from mixed[2:]
        yield rows_task()
        yield from packed
        yield from (square_task(0, row) for row in range(tiles))

    lines = [lines_task(start) for start in range(0, BASE + 1, LANES)]
    return [first_task(), *lines], ordered()


def fold_kernel(
    step_ref, table_ref, embed_ref, space_in_ref, space_out_ref, time_in_ref, time_out_ref, final_ref,
    first_ref, offset_ref, packed_ref, square_ref, shift_ref, lines_ref,
):
    def table(row):
        return table_ref[row : row + 1, :]

    def arrive(name):
        pass

    ahead, others = fold_tasks(
        3, arrive, {}, table, embed_ref, space_in_ref, space_out_ref, time_in_ref, time_out_ref,
        final_ref, first_ref, offset_ref, packed_ref, square_ref, shift_ref, lines_ref,
    )
    interleave([*ahead, *others])


def space_tasks(lags, ready, latent_ref, first_ref, offset_ref, token_ref):
    frames, channels, spatial = latent_ref.shape
    bf16 = jnp.bfloat16
    f32 = jnp.float32
    row = row_of((8, spatial))
    blank = jnp.zeros((8, spatial), f32)
    ones = jnp.ones((8, spatial), f32)
    states = [{} for frame in range(frames)]

    def offset(start, rows):
        return offset_ref[start : start + rows]

    def twice(frame):
        latent = latent_ref[frame].astype(bf16)
        return stack(latent, latent)

    def couple_task(frame):
        yield from wait_for(ready, "first")
        own = range(frame, min(frame + 2, frames))
        product = dot(first_ref[...], beside(*(twice(index) for index in own)))
        yield from pause(lags[0])
        for place, index in enumerate(own):
            states[index]["result"] = product[:, place * spatial : (place + 1) * spatial]

    def frame_task(frame):
        state = states[frame]
        yield from wait_for(state, "result")
        result = state["result"]
        latent = latent_ref[frame].astype(bf16).astype(f32)
        gram = result[3 * ROWS_T + 8 : 3 * ROWS_T + 8 + channels]
        variance = jnp.maximum(jnp.sum(latent * gram, 0, keepdims=True), 0.0) + EPS
        rate = lax.rsqrt(variance)
        yield
        spread = variance * rate
        scaled = latent * rate

        def norm(index):
            start = ROWS_T + 8 + index * ROWS_T
            place = ROWS_T + 8 + index * (ROWS_T + 8)
            terms = rate * result[start : start + ROWS_T] + offset(place, ROWS_T)
            terms = terms.reshape(channels, HEADS, spatial) * scaled[:, None, :]
            total = jnp.sum(terms, 0) + offset(place + ROWS_T, 8)
            return lax.rsqrt(jnp.maximum(total, 0.0) + EPS)

        key_rate = norm(0)
        yield
        query_rate = norm(1) * rate
        yield
        point = (rate * result[ROWS_T : ROWS_T + 8] + offset(ROWS_T, 8)) * key_rate
        point_high = point.astype(bf16).astype(f32)
        spread_high = spread.astype(bf16).astype(f32)
        ends = jnp.where(row == 1, spread - spread_high, jnp.where(row < 3, spread_high, 0.0))
        source = stack(twice(frame), stack(ends, blank).astype(bf16))
        state.update(
            terms=lambda start: rate * result[start : start + channels] + offset(start, channels),
            key_rate=key_rate,
            query_rate=query_rate,
            point=(point_high, point - point_high),
            right=on_diagonal(source, source),
            rows=stack(scaled, ones, blank).astype(bf16),
            averages=[],
        )

    def pair_task(frame, pair):
        state = states[frame]
        heads = (2 * pair, 2 * pair + 1)
        yield from wait_for(state, "rows")
        left = []
        for head in heads:
            own = state["terms"](head * channels) * state["key_rate"][head : head + 1]
            high, low = (part[head : head + 1] for part in state["point"])
            own_point = jnp.where(row < 2, high, jnp.where(row == 2, low, 0.0))
            left += [*halves(own), stack(own_point, blank).astype(bf16)]
        left = stack(*left).T
        yield
        score = dot(left, state["right"])
        yield from pause(lags[1])
        pace = beside(*(state["query_rate"][head : head + 1] for head in heads))
        weight = jnp.exp2(score * pace).astype(bf16)
        yield
        mixed = dot(state["rows"], weight)
        yield from pause(lags[2])
        share = 1.0 / mixed[channels : channels + 8]
        mixed = (mixed[:channels].reshape(-1, 8, 2 * spatial) * share[None]).reshape(channels, -1)
        state["averages"] += [mixed[:, :spatial], mixed[:, spatial:]]
        if pair == HEADS // 2 - 1:
            latent = latent_ref[frame].astype(bf16).astype(f32)
            token = stack(
                *state["averages"], latent, latent, blank, blank, blank, ones, *[blank] * 8
            )
            token_ref[frame] = token.astype(bf16).T

    def tasks():
        for frame in range(-2, frames):
            ahead = frame + 2
            if ahead < frames:
                if ahead % 2 == 0:
                    yield couple_task(ahead)
                yield frame_task(ahead)
            if frame >= 0:
                yield from (pair_task(frame, pair) for pair in range(HEADS // 2))

    return tasks()


def space_kernel(lags, *refs):
    interleave(space_tasks(lags, {"first": True}, *refs))


def regrid(chunks):
    count, (_, lanes) = len(chunks), chunks[0].shape
    block = lane_of(chunks[0].shape) // CHUNK
    if count * CHUNK != lanes or count & (count - 1):
        return [
            beside(*(part[:, index * CHUNK : (index + 1) * CHUNK] for part in chunks))
            for index in range(lanes // CHUNK)
        ]
    chunks, step = list(chunks), 1
    while step < count:
        moved = (block & step) != 0
        for low in range(count):
            if low & step == 0:
                first, second = chunks[low], chunks[low + step]
                chunks[low] = jnp.where(moved, pltpu.roll(second, step * CHUNK, 1), first)
                chunks[low + step] = jnp.where(
                    moved, second, pltpu.roll(first, lanes - step * CHUNK, 1)
                )
        step *= 2
    return chunks


def time_tasks(lags, token_ref, packed_ref, square_ref, finish, after=lambda group, parts: ()):
    bf16 = jnp.bfloat16
    f32 = jnp.float32
    frames, positions, width = token_ref.shape
    chunk = CHUNK
    rows = frames * chunk
    size = math.gcd(positions, 2 * chunk)
    parts = size // chunk
    groups = positions // size
    count = parts * rows
    keep = (row_of((rows, 2 * rows)) % chunk) == (lane_of((rows, 2 * rows)) % chunk)
    ones = jnp.ones((8, rows), f32)
    row = row_of((16, count))
    states = [{} for group in range(groups)]

    def group_task(group):
        state = states[group]
        tokens = token_ref[:, group * size : (group + 1) * size, :].astype(f32)
        tokens = tokens.reshape(frames, parts, chunk, width)
        tokens = beside(
            *(tokens[:, part].reshape(rows, width).astype(bf16).T for part in range(parts))
        )
        yield
        squares = dot(square_ref[:ATT, :WIDE], tokens)
        yield from pause(lags[0])
        variance = jnp.sum(tokens[:ATT].astype(f32) * squares, 0, keepdims=True)
        variance = jnp.maximum(variance, 0.0) + EPS
        pace = lax.rsqrt(variance)
        spread = variance * pace
        spread_high = spread.astype(bf16).astype(f32)
        yield
        ends = jnp.where(row == 1, spread - spread_high, jnp.where(row < 3, spread_high, 0.0))
        state.update(
            tokens=tokens, pace=pace, floor=(HD * EPS) * variance, outputs={},
            entry=stack(tokens[:ZERO], ends.astype(bf16), tokens[ZERO + 16 :]),
        )

    def project_task(group, pair):
        state = states[group]
        yield from wait_for(state, "entry")
        starts = [which * INNER + pair * 2 * HD for which in range(3)]
        packed = [dot(packed_ref[start : start + 2 * HD], state["entry"]) for start in starts]
        yield from pause(lags[1])
        state["packed", pair] = packed

    def pair_task(group, pair, part):
        state = states[group]
        own = slice(part * rows, (part + 1) * rows)
        yield from wait_for(state, ("packed", pair))
        packed = [values[:, own] for values in state["packed", pair]]

        def unit(which, head, gain):
            values = packed[which][head * HD : (head + 1) * HD]
            size = lax.rsqrt(jnp.sum(values * values, 0, keepdims=True) + state["floor"][:, own])
            return values * (size * gain if gain else size)

        left = stack(unit(1, 0, None), unit(1, 1, None), jnp.zeros((16, rows), f32)).astype(bf16).T
        yield
        right = on_diagonal(unit(0, 0, UNIT), unit(0, 1, UNIT))
        right = stack(right, jnp.zeros((16, 2 * rows), f32)).astype(bf16)
        score = dot(left, right)
        yield from pause(lags[2])
        weight = jnp.where(keep, jnp.exp2(score), 0.0).astype(bf16)
        yield
        value = packed[2] * state["pace"][:, own]
        value = beside(stack(value[:HD], ones), stack(value[HD:], ones)).astype(bf16)
        mixed = dot(value, on_diagonal(weight[:, :rows], weight[:, rows:]))
        yield from pause(lags[3])
        share = 1.0 / mixed[HD:]
        mixed = (mixed[:HD].reshape(-1, 8, 2 * rows) * share[None]).reshape(HD, 2 * rows)
        state["outputs"][part, pair] = stack(mixed[:, :rows], mixed[:, rows:])

    def last_task(group):
        state = states[group]
        while len(state.get("outputs", ())) < parts * HEADS // 2:
            yield
        attended = beside(
            *(
                stack(*(state["outputs"][part, pair] for pair in range(HEADS // 2)))
                for part in range(parts)
            )
        )
        exact = stack(state["tokens"][:ATT].astype(f32), attended[BASE:], attended[:BASE])
        inputs = exact.astype(bf16)
        yield
        blocks = []
        for start in range(0, exact.shape[0], WIDE):
            blocks.append(dot(square_ref[start : start + WIDE, start:], inputs[start:]))
            yield
        yield from pause(lags[4])
        total = 0.0
        for index, block in enumerate(blocks):
            terms = block * exact[index * WIDE : (index + 1) * WIDE]
            total = total + jnp.sum(terms.reshape(-1, 8, count), 0)
        rate = lax.rsqrt(jnp.maximum(jnp.sum(total, 0, keepdims=True), 0.0) + EPS)
        yield
        predicted = blocks[0][ZERO : ZERO + CHANNELS] * rate
        for part in range(parts):
            finish(group * parts + part, predicted[:, part * rows : (part + 1) * rows])

    def tasks():
        yield group_task(0)
        for group in range(groups):
            for pair in range(HEADS // 2):
                yield project_task(group, pair)
                if pair == 1 and group + 1 < groups:
                    yield group_task(group + 1)
                yield from (pair_task(group, pair, part) for part in range(parts))
            yield last_task(group)
            yield from after(group, parts)

    return tasks()


def time_kernel(lags, token_ref, packed_ref, square_ref, shift_ref, result_ref):
    chunks = {}
    interleave(time_tasks(lags, token_ref, packed_ref, square_ref, chunks.__setitem__))
    for frame, own in enumerate(regrid([chunks[index] for index in sorted(chunks)])):
        result_ref[frame] = own + shift_ref[:, : own.shape[1]]


def merged(tasks, others, every):
    others = list(others)
    for index, task in enumerate(tasks):
        yield task
        if others and index % every == every - 1:
            yield others.pop(0)
    yield from others


def sampler_kernel(
    table_from, embed_ref, space_in_from, space_out_from, time_in_from, time_out_from, final_ref,
    latent_ref, noise_ref, state_ref, denoise_ref, scale_ref, out_ref,
    table_ref, space_in_ref, space_out_ref, time_in_ref, time_out_ref,
    first_ref, offset_ref, packed_ref, square_ref, shift_ref, lines_ref, token_ref,
    own_ref, fresh_ref, running_ref, increment_ref, sent_ref, part_ref, total_ref, plane_ref,
    load_sem, part_send, part_recv, plane_send, plane_recv,
):
    f32 = jnp.float32
    bf16 = jnp.bfloat16
    frames = latent_ref.shape[0]
    timestep = lax.axis_index("tok")
    plane, seat = timestep // SIDE, timestep % SIDE
    hops = range(1, SIDE)

    def rows_of(which):
        return slice(which * INNER, (which + 1) * INNER)

    loads = {
        name: pltpu.make_async_copy(source, target, load_sem.at[index])
        for index, (name, source, target) in enumerate(
            (
                ("table", table_from.at[timestep], table_ref),
                *(
                    (("space_in", which), space_in_from.at[rows_of(which)], space_in_ref.at[rows_of(which)])
                    for which in range(3)
                ),
                ("time_out", time_out_from, time_out_ref),
                ("space_out", space_out_from, space_out_ref),
                ("time_in", time_in_from, time_in_ref),
            )
        )
    }
    for load in loads.values():
        load.start()

    def in_plane(hop):
        return {"tok": plane * SIDE + (seat + hop) % SIDE}

    def in_seat(hop):
        return {"tok": (plane + hop) % SIDE * SIDE + seat}

    barrier = pltpu.get_barrier_semaphore()
    for hop in hops:
        for target in (in_plane(hop), in_seat(hop)):
            pl.semaphore_signal(
                barrier, inc=1, device_id=target, device_id_type=pl.DeviceIdType.MESH
            )

    def arrive(name):
        if name in loads:
            loads.pop(name).wait()

    def table(row):
        return table_ref[row : row + 1, :]

    rate_denoise = denoise_ref[timestep]
    rate_state = state_ref[timestep] + jnp.where(timestep == 0, 1.0, 0.0)
    rate_noise = scale_ref[timestep]
    for target, source in ((running_ref, latent_ref), (fresh_ref, noise_ref)):
        for index, own in enumerate(regrid([source[frame] for frame in range(frames)])):
            target[index] = own
    state = {}

    def copy(source, target, send, receive, to):
        return pltpu.make_async_remote_copy(
            src_ref=source, dst_ref=target, send_sem=send, recv_sem=receive,
            device_id=to, device_id_type=pl.DeviceIdType.MESH,
        )

    sent = []
    for iteration in range(ITERS):
        last = iteration == ITERS - 1
        source_ref = own_ref if iteration else latent_ref
        spread = space_tasks(SPACE_LAGS, state, source_ref, first_ref, offset_ref, token_ref)
        if iteration == 0:
            ahead, others = fold_tasks(
                FOLD_LAG, arrive, state, table, embed_ref, space_in_ref, space_out_ref, time_in_ref,
                time_out_ref, final_ref, first_ref, offset_ref, packed_ref, square_ref, shift_ref,
                lines_ref,
            )
            spread = [*ahead, *merged(spread, others, FOLD_EVERY)]
        interleave(spread)
        if iteration == 0:
            pl.semaphore_wait(barrier, 2 * (SIDE - 1))
        done, started = set(), []

        def finish(index, predicted):
            increment = rate_denoise * (predicted + shift_ref[...])
            increment = increment + rate_noise * fresh_ref[index] + rate_state * running_ref[index]
            increment_ref[index] = increment
            sent_ref[iteration, index] = increment.astype(bf16)
            done.add(index)

        def carry_task(block, own):
            while not done.issuperset(range(own.start, own.stop)):
                yield
            parts = [
                copy(
                    sent_ref.at[iteration, own], part_ref.at[iteration, hop - 1, own],
                    part_send.at[iteration, hop - 1, block], part_recv.at[iteration, hop - 1, block],
                    in_plane(hop),
                )
                for hop in hops
            ]
            for part in parts:
                part.start()
            yield from pause(TIME_LAGS[5])
            for part in parts:
                part.wait_recv()
            total = sent_ref[iteration, own].astype(f32)
            for hop in hops:
                total = total + part_ref[iteration, hop - 1, own].astype(f32)
            total_ref[iteration, own] = total.astype(bf16)
            planes = [
                copy(
                    total_ref.at[iteration, own], plane_ref.at[iteration, hop - 1, own],
                    plane_send.at[iteration, hop - 1, block], plane_recv.at[iteration, hop - 1, block],
                    in_seat(hop),
                )
                for hop in hops
            ]
            for part in planes:
                part.start()
            started.append((own, planes))
            sent.extend(parts + planes)

        def after(group, parts):
            if (group + 1) % CARRIED == 0:
                block = group // CARRIED
                yield carry_task(block, slice(block * CARRIED * parts, (block + 1) * CARRIED * parts))

        interleave(time_tasks(TIME_LAGS, token_ref, packed_ref, square_ref, finish, after))
        chunks = []
        for own, planes in started:
            for part in planes:
                part.wait_recv()
            for index in range(own.start, own.stop):
                before = jnp.zeros(latent_ref.shape[1:], f32)
                for hop in hops:
                    value = plane_ref[iteration, hop - 1, index].astype(f32)
                    before = before + jnp.where(plane >= hop, value, 0.0)
                    value = part_ref[iteration, hop - 1, index].astype(f32)
                    before = before + jnp.where(seat >= hop, value, 0.0)
                if last:
                    chunks.append(before + increment_ref[index])
                else:
                    chunks.append(jnp.where(timestep == 0, running_ref[index], before))
                    running_ref[index] = chunks[-1]
        target_ref = out_ref if last else own_ref
        for frame, own in enumerate(regrid(chunks)):
            target_ref[frame] = own
    for part in sent:
        part.wait_send()


def whole(array):
    zeros = (0,) * array.ndim
    return pl.BlockSpec(array.shape, lambda *_: zeros, pipeline_mode=pl.Buffered(1))


def fold(own, modulation, embed_weight, space_input, space_output, time_input, time_output, final_weight):
    features = modulation.shape[2]
    shapes = [
        ((ROWS_AA, 2 * CHANNELS), jnp.bfloat16),
        ((3 * (ROWS_T + 8), LANES), jnp.float32),
        ((3 * INNER, WIDE), jnp.bfloat16),
        ((BASE + WIDE, BASE + WIDE), jnp.bfloat16),
        ((CHANNELS, LANES), jnp.float32),
    ]
    weights = (embed_weight, space_input, space_output, time_input, time_output, final_weight)
    return pl.pallas_call(
        fold_kernel,
        out_shape=[jax.ShapeDtypeStruct(*shape) for shape in shapes],
        grid_spec=pltpu.PrefetchScalarGridSpec(
            num_scalar_prefetch=1,
            grid=(1,),
            in_specs=[
                pl.BlockSpec(
                    (None,) + modulation.shape[1:],
                    lambda step, own: (own[0], 0, 0),
                    pipeline_mode=pl.Buffered(1),
                )
            ]
            + [whole(weight) for weight in weights],
            out_specs=[
                pl.BlockSpec(shape, lambda *_: (0, 0), pipeline_mode=pl.Buffered(1))
                for shape, kind in shapes
            ],
            scratch_shapes=[pltpu.VMEM((BASE + WIDE, features), jnp.bfloat16)],
        ),
        compiler_params=pltpu.CompilerParams(vmem_limit_bytes=60 * 1024 * 1024),
        name="fold",
    )(own, modulation, *weights)


def space_block(latent, first, offset):
    frames, channels, spatial = latent.shape
    step_frames = math.gcd(frames, 16)
    return pl.pallas_call(
        functools.partial(space_kernel, SPACE_LAGS),
        out_shape=jax.ShapeDtypeStruct((frames, spatial, WIDE), jnp.bfloat16),
        grid=(frames // step_frames,),
        in_specs=[
            pl.BlockSpec((step_frames, channels, spatial), lambda step: (step, 0, 0)),
            whole(first),
            whole(offset),
        ],
        out_specs=pl.BlockSpec((step_frames, spatial, WIDE), lambda step: (step, 0, 0)),
        compiler_params=pltpu.CompilerParams(vmem_limit_bytes=60 * 1024 * 1024),
        name="space_block",
    )(latent, first, offset)


def time_block(tokens, packed, square, shift):
    frames, positions, width = tokens.shape
    return pl.pallas_call(
        functools.partial(time_kernel, TIME_LAGS),
        out_shape=jax.ShapeDtypeStruct((frames, CHANNELS, positions), jnp.float32),
        grid=(1,),
        in_specs=[whole(array) for array in (tokens, packed, square, shift)],
        out_specs=whole(jax.ShapeDtypeStruct((frames, CHANNELS, positions), jnp.float32)),
        compiler_params=pltpu.CompilerParams(vmem_limit_bytes=60 * 1024 * 1024),
        name="time_block",
    )(tokens, packed, square, shift)


def sampler(modulation, weights, latent, noise, rates):
    embed, space_in, space_out, time_in, time_out, final = weights
    frames, channels, positions = latent.shape
    features = embed.shape[1]
    hops = SIDE - 1
    shape = (positions // CHUNK, channels, frames * CHUNK)
    blocks = positions // (2 * CHUNK * CARRIED)
    vmem, anywhere = (pl.BlockSpec(memory_space=space) for space in (pltpu.VMEM, pl.ANY))
    f32, bf16 = jnp.float32, jnp.bfloat16
    scratch = [(modulation.shape[1:], f32)]
    scratch += [(weight.shape, bf16) for weight in (space_in, space_out, time_in, time_out)]
    scratch += [
        ((ROWS_AA, 2 * CHANNELS), bf16),
        ((3 * (ROWS_T + 8), LANES), f32),
        ((3 * INNER, WIDE), bf16),
        ((BASE + WIDE, BASE + WIDE), bf16),
        ((CHANNELS, LANES), f32),
        ((BASE + WIDE, features), bf16),
        ((frames, positions, WIDE), bf16),
        (latent.shape, f32),
        (shape, f32),
        (shape, f32),
        (shape, f32),
        ((ITERS,) + shape, bf16),
        ((ITERS, hops) + shape, bf16),
        ((ITERS,) + shape, bf16),
        ((ITERS, hops) + shape, bf16),
    ]
    return pl.pallas_call(
        sampler_kernel,
        out_shape=jax.ShapeDtypeStruct(latent.shape, f32),
        in_specs=[anywhere, vmem] + [anywhere] * 4 + [vmem] * 3
        + [pl.BlockSpec(memory_space=pltpu.SMEM)] * 3,
        out_specs=vmem,
        scratch_shapes=[pltpu.VMEM(*each) for each in scratch]
        + [pltpu.SemaphoreType.DMA((7,))]
        + [pltpu.SemaphoreType.DMA((ITERS, hops, blocks))] * 4,
        compiler_params=pltpu.CompilerParams(
            collective_id=0, has_side_effects=True, vmem_limit_bytes=60 * 1024 * 1024
        ),
        name="sampler",
    )(modulation, *weights, latent, noise, *rates)


def carried_in(last, groups, same_block, timestep, sent, increment, latent):
    gathered = lax.all_gather(
        sent, "tok", axis_index_groups=same_block if groups > 1 else None
    )
    earlier = (jnp.arange(P_SIZE) < timestep)[:, None, None, None]
    before = jnp.sum(jnp.where(earlier, gathered.astype(jnp.float32), 0.0), axis=0)
    return before + increment if last else jnp.where(timestep == 0, latent, before)


def body(
    initial_guess,
    noise_draws,
    drift_state,
    drift_denoise,
    noise_scale,
    modulation,
    embed_weight,
    space_input,
    space_output,
    time_input,
    time_output,
    final_weight,
):
    devices = lax.axis_size("tok")
    own_index = lax.axis_index("tok")
    groups = devices // P_SIZE
    timestep = own_index // groups
    own = jnp.reshape(timestep, (1,)).astype(jnp.int32)
    rates = (drift_state, drift_denoise, noise_scale)
    same_step = [[step * groups + block for block in range(groups)] for step in range(P_SIZE)]
    same_block = [[step * groups + block for step in range(P_SIZE)] for block in range(groups)]
    weights = (
        embed_weight, space_input.T, space_output, time_input.T, time_output, final_weight.T
    )
    if groups == 1:
        return sampler(modulation, weights, initial_guess, noise_draws, rates)
    first, offset, packed, square, shift = fold(own, modulation, *weights)
    latent = initial_guess
    for iteration in range(ITERS):
        tokens = space_block(latent, first, offset)
        last = iteration == ITERS - 1
        tokens = lax.all_to_all(
            tokens, "tok", split_axis=1, concat_axis=0, axis_index_groups=same_step, tiled=True
        )
        predicted = time_block(tokens, packed, square, shift)
        predicted = lax.all_to_all(
            predicted, "tok", split_axis=0, concat_axis=2, axis_index_groups=same_step, tiled=True
        )
        rate_state, rate_denoise, rate_noise = (
            lax.dynamic_index_in_dim(rate, timestep, 0, keepdims=False) for rate in rates
        )
        rate_state = rate_state + jnp.where(timestep == 0, 1.0, 0.0)
        increment = rate_state * latent + rate_denoise * predicted + rate_noise * noise_draws
        sent = increment.astype(jnp.bfloat16)
        latent = carried_in(last, groups, same_block, timestep, sent, increment, latent)
    return latent


def solution(mesh):
    placed = (
        P(("group", "tok"), None, None),
        P(("group", "tok"), None, None),
        P(),
        P(),
        P(),
        P(),
        P(),
        P(),
        P(),
        P(),
        P(),
        P(),
    )
    return jax.shard_map(
        body, mesh=mesh, in_specs=placed, out_specs=P(("group", "tok"), None, None), check_vma=False
    )
```

```python
import functools
import math

import jax
import jax.numpy as jnp
from jax import lax
from jax.experimental import pallas as pl
from jax.experimental.pallas import tpu as pltpu
from jax.sharding import PartitionSpec as P

HEADS = 8
HD = 72
P_SIZE = 16
ITERS = 2
LANES = 128
INNER = HEADS * HD
SIDE = math.isqrt(P_SIZE)
CHUNK = 8
CARRIED = 2
SPACE_LAGS = (2, 8, 6)
FOLD_LAG = 4
FOLD_EVERY = 2
TIME_LAGS = (4, 8, 10, 8, 2, 80)
EPS = 1e-06
CHANNELS = 16
WIDE = 2 * LANES
ROWS_T = HEADS * CHANNELS
ROWS_AA = 3 * ROWS_T + 32
BASE = 512
TAIL = INNER - BASE
LAT, DUP, ZERO, ONE, ATT = 128, 144, 160, 184, 192
SCALE = HD**-0.5 * math.log2(math.e)
UNIT = HD**0.5 * math.log2(math.e)


def dot_rows(values, weight_rows, precision=None):
    return lax.dot_general(
        values,
        weight_rows,
        (((1,), (1,)), ((), ())),
        preferred_element_type=jnp.float32,
        precision=precision,
    )


def dot(values, weights):
    return jnp.dot(values, weights, preferred_element_type=jnp.float32)


def halves(values):
    high = values.astype(jnp.bfloat16)
    return high, (values - high.astype(jnp.float32)).astype(jnp.bfloat16)


def lane_of(shape):
    return lax.broadcasted_iota(jnp.int32, shape, len(shape) - 1)


def row_of(shape):
    return lax.broadcasted_iota(jnp.int32, shape, 0)


def centred(rows):
    return rows - jnp.mean(rows, -1, keepdims=True)


def by_head(rows, order):
    count, width = rows.shape
    if order == "hc":
        spread = jnp.concatenate([rows] * HEADS, axis=0)
        head = row_of(spread.shape) // count
    else:
        spread = jnp.broadcast_to(rows[:, None, :], (count, HEADS, width)).reshape(-1, width)
        head = row_of(spread.shape) % HEADS
    return jnp.where(lane_of(spread.shape) // HD == head, spread, 0.0)


def stack(*parts):
    return jnp.concatenate(parts, axis=0)


def beside(*parts):
    return jnp.concatenate(parts, axis=1)


def on_diagonal(first, second):
    blank = jnp.zeros_like(first)
    return stack(beside(first, blank), beside(blank, second))


def interleave(tasks):
    tasks, running = list(tasks), []
    while tasks or running:
        running += [tasks.pop(0)] if tasks else []
        running = [task for task in running if next(task, tasks) is not tasks]


def pause(turns):
    for turn in range(turns):
        yield


def wait_for(state, key):
    while key not in state:
        yield


def fold_tasks(
    lag, arrive, state, table, embed_ref, space_in_ref, space_out_ref, time_in_ref, time_out_ref,
    final_ref, first_ref, offset_ref, packed_ref, square_ref, shift_ref, lines_ref,
):
    f32 = jnp.float32
    bf16 = jnp.bfloat16
    features = embed_ref.shape[1]
    embed = centred(embed_ref[...].astype(f32))
    state.update(mixed={}, lines=set())

    def zeros(rows, width=features):
        return jnp.zeros((rows, width), f32)

    def fine_parts(rows, side):
        high, low = halves(rows)
        side_high, side_low = halves(side)
        return dot_rows(high, stack(side_high, side_low)), dot_rows(low, side_high)

    def fine_sum(both, rest):
        return both[:, :LANES] + both[:, LANES:] + rest

    def side_of(rows, point):
        width = rows.shape[1]
        return stack(rows, rows, point, zeros(7, width), zeros(LANES - 2 * CHANNELS - 8, width))

    def first_task():
        arrive("table")
        lines = stack(*halves(embed * (1.0 + table(1))))
        tail = stack(*(half.astype(f32) for half in halves(stack(table(0), zeros(7)))))
        left = stack(lines, tail.astype(bf16))
        folded = []
        for which in range(3):
            arrive(("space_in", which))
            folded.append(dot_rows(left, space_in_ref[which * INNER : (which + 1) * INNER]))
            yield
        yield from pause(lag)
        query, key, value = (
            own[:CHANNELS] + own[CHANNELS : 2 * CHANNELS] for own in folded
        )
        query_c, key_c, value_c = (
            (own[2 * CHANNELS : 2 * CHANNELS + 8] + own[2 * CHANNELS + 8 :])[:1] for own in folded
        )
        key_side, query_side = side_of(key, key_c), side_of(query, query_c)
        scores = fine_parts(stack(by_head(query, "hc"), by_head(query_c, "ch")) * SCALE, key_side)
        yield
        key_square = fine_parts(
            stack(by_head(key, "ch"), by_head(key_c, "ch")) * (1.0 / HD), key_side
        )
        yield
        query_square = fine_parts(
            stack(by_head(query, "ch"), by_head(query_c, "ch")) * (1.0 / HD), query_side
        )
        gram = fine_parts(embed, side_of(embed, zeros(1)))
        yield
        values = stack(*halves(by_head(value, "hc")))
        tail = stack(*(half.astype(f32) for half in halves(stack(value_c, zeros(7, INNER)))))
        state["values"] = stack(values, tail.astype(bf16))
        yield from pause(lag)
        scores, key_square, query_square = (
            fine_sum(*each) for each in (scores, key_square, query_square)
        )
        gram = fine_sum(*gram) * (1.0 / features)
        first = stack(scores, key_square[:ROWS_T], query_square[:ROWS_T], gram, zeros(8, LANES))
        high, low = halves(first)
        upper = lane_of(first.shape) < CHANNELS
        chosen = jnp.where(upper, high.astype(f32), low.astype(f32))
        first_ref[...] = chosen[:, : 2 * CHANNELS].astype(bf16)
        point = 2 * CHANNELS
        offset_ref[: ROWS_T + 8] = jnp.broadcast_to(
            scores[:, point : point + 1], (ROWS_T + 8, LANES)
        )
        for index, square in enumerate((key_square, query_square)):
            start = ROWS_T + 8 + index * (ROWS_T + 8)
            offset_ref[start : start + ROWS_T] = jnp.broadcast_to(
                2.0 * square[:ROWS_T, point : point + 1], (ROWS_T, LANES)
            )
            offset_ref[start + ROWS_T : start + ROWS_T + 8] = jnp.broadcast_to(
                square[ROWS_T:, point : point + 1], (8, LANES)
            )
        state["first"] = True

    def mixed_task(start):
        yield from wait_for(state, "values")
        if start == 0:
            arrive("space_out")
        own = dot(state["values"], space_out_ref[:, start : min(start + WIDE, features)])
        yield from pause(lag)
        state["mixed"][start] = own

    def rows_task():
        starts = range(0, features, WIDE)
        while len(state["mixed"]) < len(starts):
            yield
        mixed = beside(*(state["mixed"][start] for start in starts))
        gate = table(2)
        attended = centred(gate * (mixed[:ROWS_T] + mixed[ROWS_T : 2 * ROWS_T]))
        point = centred(gate * (mixed[2 * ROWS_T : 2 * ROWS_T + 8] + mixed[2 * ROWS_T + 8 :]))
        yield
        scaled = 1.0 + table(4)
        ends = halves(stack(table(3), point[:1] * scaled, zeros(6)))
        tail = stack(*(half.astype(f32) for half in ends))
        state["rows"] = stack(
            (attended * scaled).astype(bf16), *halves(embed * scaled), tail.astype(bf16)
        )
        lines_ref[:LAT] = attended.astype(bf16)
        high, low = halves(embed)
        lines_ref[LAT:DUP] = high
        lines_ref[DUP:ZERO] = low
        point = (half.astype(f32) for half in halves(point[:1]))
        lines_ref[ZERO:ATT] = stack(zeros(ONE - ZERO), *point, zeros(ATT - ONE - 2)).astype(bf16)
        state["lines"].add("tokens")

    def settle(columns):
        lat = columns[LAT:DUP] + columns[DUP : DUP + CHANNELS]
        lat_high = lat.astype(bf16).astype(f32)
        ends = columns[DUP + CHANNELS : DUP + CHANNELS + 8] + columns[DUP + CHANNELS + 8 :]
        ends_high = ends.astype(bf16).astype(f32)
        ends_low = ends - ends_high
        width = columns.shape[1]
        return stack(
            columns[:LAT], lat_high, lat - lat_high,
            ends_high[:1], ends_high[:1], ends_low[:1], zeros(ONE - ZERO - 3, width),
            ends_high[1:2], ends_low[1:2], zeros(WIDE - ONE - 2, width),
        ).astype(bf16)

    def packed_task(start):
        yield from wait_for(state, "rows")
        if start == 0:
            arrive("time_in")
        own = slice(start, min(start + WIDE, 3 * INNER))
        columns = dot_rows(state["rows"], time_in_ref[own, :])
        yield from pause(lag)
        packed_ref[own] = settle(columns).T

    def lines_task(start):
        arrive("time_out")
        gate = table(5)
        if start == BASE:
            own, target = slice(BASE, INNER), ATT
        else:
            own, target = slice(start, start + LANES), WIDE + start
        rows = centred(gate * time_out_ref[own].astype(f32))
        lines_ref[target : target + rows.shape[0]] = rows.astype(bf16)
        state["lines"].add(start)
        yield

    tiles = lines_ref.shape[0] // WIDE

    def square_task(column, row):
        while len(state["lines"]) < 2 + BASE // LANES - (column > 0) or column == 0 and "tokens" not in state["lines"]:
            yield
        other = lines_ref[column * WIDE : (column + 1) * WIDE]
        if column == 0:
            final = final_ref[...].astype(f32)
            if row == 0:
                shift_ref[...] = jnp.broadcast_to(
                    jnp.sum(final * table(6), -1, keepdims=True), (CHANNELS, LANES)
                )
            final = (final * (1.0 + table(7))).astype(bf16)
            other = stack(other[:ZERO], final, other[ZERO + CHANNELS :])
        block = dot_rows(other, lines_ref[row * WIDE : (row + 1) * WIDE])
        yield from pause(lag)
        gain = (1.0 if row == column else 2.0) / features
        if column == 0:
            line = row_of((WIDE, 1))
            gain = jnp.where((line >= ZERO) & (line < ZERO + CHANNELS), 1.0, gain)
        square_ref[column * WIDE : (column + 1) * WIDE, row * WIDE : (row + 1) * WIDE] = (
            (block * gain).astype(bf16)
        )

    def ordered():
        packed = [packed_task(start) for start in range(0, 3 * INNER, WIDE)]
        early = [square_task(column, row) for column in range(1, tiles) for row in range(column, tiles)]
        mixed = [mixed_task(start) for start in range(0, features, WIDE)]
        yield from mixed[:2]
        yield from early
        yield from mixed[2:]
        yield rows_task()
        yield from packed
        yield from (square_task(0, row) for row in range(tiles))

    lines = [lines_task(start) for start in range(0, BASE + 1, LANES)]
    return [first_task(), *lines], ordered()


def fold_kernel(
    step_ref, table_ref, embed_ref, space_in_ref, space_out_ref, time_in_ref, time_out_ref, final_ref,
    first_ref, offset_ref, packed_ref, square_ref, shift_ref, lines_ref,
):
    def table(row):
        return table_ref[row : row + 1, :]

    def arrive(name):
        pass

    ahead, others = fold_tasks(
        3, arrive, {}, table, embed_ref, space_in_ref, space_out_ref, time_in_ref, time_out_ref,
        final_ref, first_ref, offset_ref, packed_ref, square_ref, shift_ref, lines_ref,
    )
    interleave([*ahead, *others])


def space_tasks(lags, ready, latent_ref, first_ref, offset_ref, token_ref):
    frames, channels, spatial = latent_ref.shape
    bf16 = jnp.bfloat16
    f32 = jnp.float32
    row = row_of((8, spatial))
    blank = jnp.zeros((8, spatial), f32)
    ones = jnp.ones((8, spatial), f32)
    states = [{} for frame in range(frames)]

    def offset(start, rows):
        return offset_ref[start : start + rows]

    def twice(frame):
        latent = latent_ref[frame].astype(bf16)
        return stack(latent, latent)

    def couple_task(frame):
        yield from wait_for(ready, "first")
        own = range(frame, min(frame + 2, frames))
        product = dot(first_ref[...], beside(*(twice(index) for index in own)))
        yield from pause(lags[0])
        for place, index in enumerate(own):
            states[index]["result"] = product[:, place * spatial : (place + 1) * spatial]

    def frame_task(frame):
        state = states[frame]
        yield from wait_for(state, "result")
        result = state["result"]
        latent = latent_ref[frame].astype(bf16).astype(f32)
        gram = result[3 * ROWS_T + 8 : 3 * ROWS_T + 8 + channels]
        variance = jnp.maximum(jnp.sum(latent * gram, 0, keepdims=True), 0.0) + EPS
        rate = lax.rsqrt(variance)
        yield
        spread = variance * rate
        scaled = latent * rate

        def norm(index):
            start = ROWS_T + 8 + index * ROWS_T
            place = ROWS_T + 8 + index * (ROWS_T + 8)
            terms = rate * result[start : start + ROWS_T] + offset(place, ROWS_T)
            terms = terms.reshape(channels, HEADS, spatial) * scaled[:, None, :]
            total = jnp.sum(terms, 0) + offset(place + ROWS_T, 8)
            return lax.rsqrt(jnp.maximum(total, 0.0) + EPS)

        key_rate = norm(0)
        yield
        query_rate = norm(1) * rate
        yield
        point = (rate * result[ROWS_T : ROWS_T + 8] + offset(ROWS_T, 8)) * key_rate
        point_high = point.astype(bf16).astype(f32)
        spread_high = spread.astype(bf16).astype(f32)
        ends = jnp.where(row == 1, spread - spread_high, jnp.where(row < 3, spread_high, 0.0))
        source = stack(twice(frame), stack(ends, blank).astype(bf16))
        state.update(
            terms=lambda start: rate * result[start : start + channels] + offset(start, channels),
            key_rate=key_rate,
            query_rate=query_rate,
            point=(point_high, point - point_high),
            right=on_diagonal(source, source),
            rows=stack(scaled, ones, blank).astype(bf16),
            averages=[],
        )

    def pair_task(frame, pair):
        state = states[frame]
        heads = (2 * pair, 2 * pair + 1)
        yield from wait_for(state, "rows")
        left = []
        for head in heads:
            own = state["terms"](head * channels) * state["key_rate"][head : head + 1]
            high, low = (part[head : head + 1] for part in state["point"])
            own_point = jnp.where(row < 2, high, jnp.where(row == 2, low, 0.0))
            left += [*halves(own), stack(own_point, blank).astype(bf16)]
        left = stack(*left).T
        yield
        score = dot(left, state["right"])
        yield from pause(lags[1])
        pace = beside(*(state["query_rate"][head : head + 1] for head in heads))
        weight = jnp.exp2(score * pace).astype(bf16)
        yield
        mixed = dot(state["rows"], weight)
        yield from pause(lags[2])
        share = 1.0 / mixed[channels : channels + 8]
        mixed = (mixed[:channels].reshape(-1, 8, 2 * spatial) * share[None]).reshape(channels, -1)
        state["averages"] += [mixed[:, :spatial], mixed[:, spatial:]]
        if pair == HEADS // 2 - 1:
            latent = latent_ref[frame].astype(bf16).astype(f32)
            token = stack(
                *state["averages"], latent, latent, blank, blank, blank, ones, *[blank] * 8
            )
            token_ref[frame] = token.astype(bf16).T

    def tasks():
        for frame in range(-2, frames):
            ahead = frame + 2
            if ahead < frames:
                if ahead % 2 == 0:
                    yield couple_task(ahead)
                yield frame_task(ahead)
            if frame >= 0:
                yield from (pair_task(frame, pair) for pair in range(HEADS // 2))

    return tasks()


def space_kernel(lags, *refs):
    interleave(space_tasks(lags, {"first": True}, *refs))


def regrid(chunks):
    count, (_, lanes) = len(chunks), chunks[0].shape
    block = lane_of(chunks[0].shape) // CHUNK
    if count * CHUNK != lanes or count & (count - 1):
        return [
            beside(*(part[:, index * CHUNK : (index + 1) * CHUNK] for part in chunks))
            for index in range(lanes // CHUNK)
        ]
    chunks, step = list(chunks), 1
    while step < count:
        moved = (block & step) != 0
        for low in range(count):
            if low & step == 0:
                first, second = chunks[low], chunks[low + step]
                chunks[low] = jnp.where(moved, pltpu.roll(second, step * CHUNK, 1), first)
                chunks[low + step] = jnp.where(
                    moved, second, pltpu.roll(first, lanes - step * CHUNK, 1)
                )
        step *= 2
    return chunks


def time_tasks(lags, token_ref, packed_ref, square_ref, finish, after=lambda group, parts: ()):
    bf16 = jnp.bfloat16
    f32 = jnp.float32
    frames, positions, width = token_ref.shape
    chunk = CHUNK
    rows = frames * chunk
    size = math.gcd(positions, 2 * chunk)
    parts = size // chunk
    groups = positions // size
    count = parts * rows
    keep = (row_of((rows, 2 * rows)) % chunk) == (lane_of((rows, 2 * rows)) % chunk)
    ones = jnp.ones((8, rows), f32)
    row = row_of((16, count))
    states = [{} for group in range(groups)]

    def group_task(group):
        state = states[group]
        tokens = token_ref[:, group * size : (group + 1) * size, :].astype(f32)
        tokens = tokens.reshape(frames, parts, chunk, width)
        tokens = beside(
            *(tokens[:, part].reshape(rows, width).astype(bf16).T for part in range(parts))
        )
        yield
        squares = dot(square_ref[:ATT, :WIDE], tokens)
        yield from pause(lags[0])
        variance = jnp.sum(tokens[:ATT].astype(f32) * squares, 0, keepdims=True)
        variance = jnp.maximum(variance, 0.0) + EPS
        pace = lax.rsqrt(variance)
        spread = variance * pace
        spread_high = spread.astype(bf16).astype(f32)
        yield
        ends = jnp.where(row == 1, spread - spread_high, jnp.where(row < 3, spread_high, 0.0))
        state.update(
            tokens=tokens, pace=pace, floor=(HD * EPS) * variance, outputs={},
            entry=stack(tokens[:ZERO], ends.astype(bf16), tokens[ZERO + 16 :]),
        )

    def project_task(group, pair):
        state = states[group]
        yield from wait_for(state, "entry")
        starts = [which * INNER + pair * 2 * HD for which in range(3)]
        packed = [dot(packed_ref[start : start + 2 * HD], state["entry"]) for start in starts]
        yield from pause(lags[1])
        state["packed", pair] = packed

    def pair_task(group, pair, part):
        state = states[group]
        own = slice(part * rows, (part + 1) * rows)
        yield from wait_for(state, ("packed", pair))
        packed = [values[:, own] for values in state["packed", pair]]

        def unit(which, head, gain):
            values = packed[which][head * HD : (head + 1) * HD]
            size = lax.rsqrt(jnp.sum(values * values, 0, keepdims=True) + state["floor"][:, own])
            return values * (size * gain if gain else size)

        left = stack(unit(1, 0, None), unit(1, 1, None), jnp.zeros((16, rows), f32)).astype(bf16).T
        yield
        right = on_diagonal(unit(0, 0, UNIT), unit(0, 1, UNIT))
        right = stack(right, jnp.zeros((16, 2 * rows), f32)).astype(bf16)
        score = dot(left, right)
        yield from pause(lags[2])
        weight = jnp.where(keep, jnp.exp2(score), 0.0).astype(bf16)
        yield
        value = packed[2] * state["pace"][:, own]
        value = beside(stack(value[:HD], ones), stack(value[HD:], ones)).astype(bf16)
        mixed = dot(value, on_diagonal(weight[:, :rows], weight[:, rows:]))
        yield from pause(lags[3])
        share = 1.0 / mixed[HD:]
        mixed = (mixed[:HD].reshape(-1, 8, 2 * rows) * share[None]).reshape(HD, 2 * rows)
        state["outputs"][part, pair] = stack(mixed[:, :rows], mixed[:, rows:])

    def last_task(group):
        state = states[group]
        while len(state.get("outputs", ())) < parts * HEADS // 2:
            yield
        attended = beside(
            *(
                stack(*(state["outputs"][part, pair] for pair in range(HEADS // 2)))
                for part in range(parts)
            )
        )
        exact = stack(state["tokens"][:ATT].astype(f32), attended[BASE:], attended[:BASE])
        inputs = exact.astype(bf16)
        yield
        blocks = []
        for start in range(0, exact.shape[0], WIDE):
            blocks.append(dot(square_ref[start : start + WIDE, start:], inputs[start:]))
            yield
        yield from pause(lags[4])
        total = 0.0
        for index, block in enumerate(blocks):
            terms = block * exact[index * WIDE : (index + 1) * WIDE]
            total = total + jnp.sum(terms.reshape(-1, 8, count), 0)
        rate = lax.rsqrt(jnp.maximum(jnp.sum(total, 0, keepdims=True), 0.0) + EPS)
        yield
        predicted = blocks[0][ZERO : ZERO + CHANNELS] * rate
        for part in range(parts):
            finish(group * parts + part, predicted[:, part * rows : (part + 1) * rows])

    def tasks():
        yield group_task(0)
        for group in range(groups):
            for pair in range(HEADS // 2):
                yield project_task(group, pair)
                if pair == 1 and group + 1 < groups:
                    yield group_task(group + 1)
                yield from (pair_task(group, pair, part) for part in range(parts))
            yield last_task(group)
            yield from after(group, parts)

    return tasks()


def time_kernel(lags, token_ref, packed_ref, square_ref, shift_ref, result_ref):
    chunks = {}
    interleave(time_tasks(lags, token_ref, packed_ref, square_ref, chunks.__setitem__))
    for frame, own in enumerate(regrid([chunks[index] for index in sorted(chunks)])):
        result_ref[frame] = own + shift_ref[:, : own.shape[1]]


def merged(tasks, others, every):
    others = list(others)
    for index, task in enumerate(tasks):
        yield task
        if others and index % every == every - 1:
            yield others.pop(0)
    yield from others


def sampler_kernel(
    table_from, embed_ref, space_in_from, space_out_from, time_in_from, time_out_from, final_ref,
    latent_ref, noise_ref, state_ref, denoise_ref, scale_ref, out_ref,
    table_ref, space_in_ref, space_out_ref, time_in_ref, time_out_ref,
    first_ref, offset_ref, packed_ref, square_ref, shift_ref, lines_ref, token_ref,
    own_ref, fresh_ref, running_ref, increment_ref, sent_ref, part_ref, total_ref, plane_ref,
    load_sem, part_send, part_recv, plane_send, plane_recv,
):
    f32 = jnp.float32
    bf16 = jnp.bfloat16
    frames, _, positions = latent_ref.shape
    timestep = lax.axis_index("tok")
    plane, seat = timestep // SIDE, timestep % SIDE
    hops = range(1, SIDE)

    def rows_of(which):
        return slice(which * INNER, (which + 1) * INNER)

    loads = {
        name: pltpu.make_async_copy(source, target, load_sem.at[index])
        for index, (name, source, target) in enumerate(
            (
                ("table", table_from.at[timestep], table_ref),
                *(
                    (("space_in", which), space_in_from.at[rows_of(which)], space_in_ref.at[rows_of(which)])
                    for which in range(3)
                ),
                ("time_out", time_out_from, time_out_ref),
                ("space_out", space_out_from, space_out_ref),
                ("time_in", time_in_from, time_in_ref),
            )
        )
    }
    for load in loads.values():
        load.start()

    def in_plane(hop):
        return {"tok": plane * SIDE + (seat + hop) % SIDE}

    def in_seat(hop):
        return {"tok": (plane + hop) % SIDE * SIDE + seat}

    plane_ref[...] = jnp.zeros_like(plane_ref)
    barrier = pltpu.get_barrier_semaphore()
    for hop in hops:
        for target in (in_plane(hop), in_seat(hop)):
            pl.semaphore_signal(
                barrier, inc=1, device_id=target, device_id_type=pl.DeviceIdType.MESH
            )

    def arrive(name):
        if name in loads:
            loads.pop(name).wait()

    def table(row):
        return table_ref[row : row + 1, :]

    rate_denoise = denoise_ref[timestep]
    rate_state = state_ref[timestep] + jnp.where(timestep == 0, 1.0, 0.0)
    rate_noise = scale_ref[timestep]
    for target, source in ((running_ref, latent_ref), (fresh_ref, noise_ref)):
        for index, own in enumerate(regrid([source[frame] for frame in range(frames)])):
            target[index] = own
    state = {}

    def copy(source, target, send, receive, to):
        return pltpu.make_async_remote_copy(
            src_ref=source, dst_ref=target, send_sem=send, recv_sem=receive,
            device_id=to, device_id_type=pl.DeviceIdType.MESH,
        )

    sent = []
    for iteration in range(ITERS):
        last = iteration == ITERS - 1
        source_ref = own_ref if iteration else latent_ref
        spread = space_tasks(SPACE_LAGS, state, source_ref, first_ref, offset_ref, token_ref)
        if iteration == 0:
            ahead, others = fold_tasks(
                FOLD_LAG, arrive, state, table, embed_ref, space_in_ref, space_out_ref, time_in_ref,
                time_out_ref, final_ref, first_ref, offset_ref, packed_ref, square_ref, shift_ref,
                lines_ref,
            )
            spread = [*ahead, *merged(spread, others, FOLD_EVERY)]
        interleave(spread)
        if iteration == 0:
            pl.semaphore_wait(barrier, 2 * (SIDE - 1))
        done, started = set(), []

        def finish(index, predicted):
            increment = rate_denoise * (predicted + shift_ref[...])
            increment = increment + rate_noise * fresh_ref[index] + rate_state * running_ref[index]
            increment_ref[index] = increment
            sent_ref[iteration, index] = increment.astype(bf16)
            done.add(index)

        def carry_task(block, own):
            while not done.issuperset(range(own.start, own.stop)):
                yield
            parts = [
                copy(
                    sent_ref.at[iteration, own], part_ref.at[iteration, hop - 1, own],
                    part_send.at[iteration, hop - 1, block], part_recv.at[iteration, hop - 1, block],
                    in_plane(hop),
                )
                for hop in hops
            ]
            for part in parts:
                part.start()
            yield from pause(TIME_LAGS[5])
            for part in parts:
                part.wait_recv()
            total = sent_ref[iteration, own].astype(f32)
            for hop in hops:
                total = total + part_ref[iteration, hop - 1, own].astype(f32)
            total_ref[iteration, own] = total.astype(bf16)
            planes = [
                copy(
                    total_ref.at[iteration, own], plane_ref.at[iteration, hop - 1, own],
                    plane_send.at[iteration, hop - 1, block], plane_recv.at[iteration, hop - 1, block],
                    in_seat(hop),
                )
                for hop in hops
            ]
            only = True
            for hop, part in zip(hops, planes):
                if only:
                    pl.when(plane + hop < SIDE)(part.start)
                else:
                    part.start()
            started.append((own, planes, only))
            sent.extend((0, part) for part in parts)
            sent.extend((hop if only else 0, part) for hop, part in zip(hops, planes))

        def after(group, parts):
            if (group + 1) % CARRIED == 0:
                block = group // CARRIED
                yield carry_task(block, slice(block * CARRIED * parts, (block + 1) * CARRIED * parts))

        interleave(time_tasks(TIME_LAGS, token_ref, packed_ref, square_ref, finish, after))
        chunks = []
        for own, planes, only in started:
            for hop, part in zip(hops, planes):
                if only:
                    pl.when(plane >= hop)(part.wait_recv)
                else:
                    part.wait_recv()
            for index in range(own.start, own.stop):
                before = jnp.zeros(latent_ref.shape[1:], f32)
                for hop in hops:
                    value = plane_ref[iteration, hop - 1, index].astype(f32)
                    before = before + jnp.where(plane >= hop, value, 0.0)
                    value = part_ref[iteration, hop - 1, index].astype(f32)
                    before = before + jnp.where(seat >= hop, value, 0.0)
                if last:
                    chunks.append(before + increment_ref[index])
                else:
                    chunks.append(jnp.where(timestep == 0, running_ref[index], before))
                    running_ref[index] = chunks[-1]
        target_ref = out_ref if last else own_ref
        for frame, own in enumerate(regrid(chunks)):
            target_ref[frame] = own
    for hop, part in sent:
        if hop:
            pl.when(plane + hop < SIDE)(part.wait_send)
        else:
            part.wait_send()


def whole(array):
    zeros = (0,) * array.ndim
    return pl.BlockSpec(array.shape, lambda *_: zeros, pipeline_mode=pl.Buffered(1))


def fold(own, modulation, embed_weight, space_input, space_output, time_input, time_output, final_weight):
    features = modulation.shape[2]
    shapes = [
        ((ROWS_AA, 2 * CHANNELS), jnp.bfloat16),
        ((3 * (ROWS_T + 8), LANES), jnp.float32),
        ((3 * INNER, WIDE), jnp.bfloat16),
        ((BASE + WIDE, BASE + WIDE), jnp.bfloat16),
        ((CHANNELS, LANES), jnp.float32),
    ]
    weights = (embed_weight, space_input, space_output, time_input, time_output, final_weight)
    return pl.pallas_call(
        fold_kernel,
        out_shape=[jax.ShapeDtypeStruct(*shape) for shape in shapes],
        grid_spec=pltpu.PrefetchScalarGridSpec(
            num_scalar_prefetch=1,
            grid=(1,),
            in_specs=[
                pl.BlockSpec(
                    (None,) + modulation.shape[1:],
                    lambda step, own: (own[0], 0, 0),
                    pipeline_mode=pl.Buffered(1),
                )
            ]
            + [whole(weight) for weight in weights],
            out_specs=[
                pl.BlockSpec(shape, lambda *_: (0, 0), pipeline_mode=pl.Buffered(1))
                for shape, kind in shapes
            ],
            scratch_shapes=[pltpu.VMEM((BASE + WIDE, features), jnp.bfloat16)],
        ),
        compiler_params=pltpu.CompilerParams(vmem_limit_bytes=60 * 1024 * 1024),
        name="fold",
    )(own, modulation, *weights)


def space_block(latent, first, offset):
    frames, channels, spatial = latent.shape
    step_frames = math.gcd(frames, 16)
    return pl.pallas_call(
        functools.partial(space_kernel, SPACE_LAGS),
        out_shape=jax.ShapeDtypeStruct((frames, spatial, WIDE), jnp.bfloat16),
        grid=(frames // step_frames,),
        in_specs=[
            pl.BlockSpec((step_frames, channels, spatial), lambda step: (step, 0, 0)),
            whole(first),
            whole(offset),
        ],
        out_specs=pl.BlockSpec((step_frames, spatial, WIDE), lambda step: (step, 0, 0)),
        compiler_params=pltpu.CompilerParams(vmem_limit_bytes=60 * 1024 * 1024),
        name="space_block",
    )(latent, first, offset)


def time_block(tokens, packed, square, shift):
    frames, positions, width = tokens.shape
    return pl.pallas_call(
        functools.partial(time_kernel, TIME_LAGS),
        out_shape=jax.ShapeDtypeStruct((frames, CHANNELS, positions), jnp.float32),
        grid=(1,),
        in_specs=[whole(array) for array in (tokens, packed, square, shift)],
        out_specs=whole(jax.ShapeDtypeStruct((frames, CHANNELS, positions), jnp.float32)),
        compiler_params=pltpu.CompilerParams(vmem_limit_bytes=60 * 1024 * 1024),
        name="time_block",
    )(tokens, packed, square, shift)


def sampler(modulation, weights, latent, noise, rates):
    embed, space_in, space_out, time_in, time_out, final = weights
    frames, channels, positions = latent.shape
    features = embed.shape[1]
    hops = SIDE - 1
    shape = (positions // CHUNK, channels, frames * CHUNK)
    blocks = positions // (2 * CHUNK * CARRIED)
    vmem, anywhere = (pl.BlockSpec(memory_space=space) for space in (pltpu.VMEM, pl.ANY))
    f32, bf16 = jnp.float32, jnp.bfloat16
    scratch = [(modulation.shape[1:], f32)]
    scratch += [(weight.shape, bf16) for weight in (space_in, space_out, time_in, time_out)]
    scratch += [
        ((ROWS_AA, 2 * CHANNELS), bf16),
        ((3 * (ROWS_T + 8), LANES), f32),
        ((3 * INNER, WIDE), bf16),
        ((BASE + WIDE, BASE + WIDE), bf16),
        ((CHANNELS, LANES), f32),
        ((BASE + WIDE, features), bf16),
        ((frames, positions, WIDE), bf16),
        (latent.shape, f32),
        (shape, f32),
        (shape, f32),
        (shape, f32),
        ((ITERS,) + shape, bf16),
        ((ITERS, hops) + shape, bf16),
        ((ITERS,) + shape, bf16),
        ((ITERS, hops) + shape, bf16),
    ]
    return pl.pallas_call(
        sampler_kernel,
        out_shape=jax.ShapeDtypeStruct(latent.shape, f32),
        in_specs=[anywhere, vmem] + [anywhere] * 4 + [vmem] * 3
        + [pl.BlockSpec(memory_space=pltpu.SMEM)] * 3,
        out_specs=vmem,
        scratch_shapes=[pltpu.VMEM(*each) for each in scratch]
        + [pltpu.SemaphoreType.DMA((7,))]
        + [pltpu.SemaphoreType.DMA((ITERS, hops, blocks))] * 4,
        compiler_params=pltpu.CompilerParams(
            collective_id=0, has_side_effects=True, vmem_limit_bytes=60 * 1024 * 1024
        ),
        name="sampler",
    )(modulation, *weights, latent, noise, *rates)


def carried_in(last, groups, same_block, timestep, sent, increment, latent):
    gathered = lax.all_gather(
        sent, "tok", axis_index_groups=same_block if groups > 1 else None
    )
    earlier = (jnp.arange(P_SIZE) < timestep)[:, None, None, None]
    before = jnp.sum(jnp.where(earlier, gathered.astype(jnp.float32), 0.0), axis=0)
    return before + increment if last else jnp.where(timestep == 0, latent, before)


def body(
    initial_guess,
    noise_draws,
    drift_state,
    drift_denoise,
    noise_scale,
    modulation,
    embed_weight,
    space_input,
    space_output,
    time_input,
    time_output,
    final_weight,
):
    devices = lax.axis_size("tok")
    own_index = lax.axis_index("tok")
    groups = devices // P_SIZE
    timestep = own_index // groups
    own = jnp.reshape(timestep, (1,)).astype(jnp.int32)
    rates = (drift_state, drift_denoise, noise_scale)
    same_step = [[step * groups + block for block in range(groups)] for step in range(P_SIZE)]
    same_block = [[step * groups + block for step in range(P_SIZE)] for block in range(groups)]
    weights = (
        embed_weight, space_input.T, space_output, time_input.T, time_output, final_weight.T
    )
    if groups == 1:
        return sampler(modulation, weights, initial_guess, noise_draws, rates)
    first, offset, packed, square, shift = fold(own, modulation, *weights)
    latent = initial_guess
    for iteration in range(ITERS):
        tokens = space_block(latent, first, offset)
        last = iteration == ITERS - 1
        tokens = lax.all_to_all(
            tokens, "tok", split_axis=1, concat_axis=0, axis_index_groups=same_step, tiled=True
        )
        predicted = time_block(tokens, packed, square, shift)
        predicted = lax.all_to_all(
            predicted, "tok", split_axis=0, concat_axis=2, axis_index_groups=same_step, tiled=True
        )
        rate_state, rate_denoise, rate_noise = (
            lax.dynamic_index_in_dim(rate, timestep, 0, keepdims=False) for rate in rates
        )
        rate_state = rate_state + jnp.where(timestep == 0, 1.0, 0.0)
        increment = rate_state * latent + rate_denoise * predicted + rate_noise * noise_draws
        sent = increment.astype(jnp.bfloat16)
        latent = carried_in(last, groups, same_block, timestep, sent, increment, latent)
    return latent


def solution(mesh):
    placed = (
        P(("group", "tok"), None, None),
        P(("group", "tok"), None, None),
        P(),
        P(),
        P(),
        P(),
        P(),
        P(),
        P(),
        P(),
        P(),
        P(),
    )
    return jax.shard_map(
        body, mesh=mesh, in_specs=placed, out_specs=P(("group", "tok"), None, None), check_vma=False
    )
```
